32 devices in a mesh: ctx: 8 (over z, y), mp: 4 (over x, core).
Axes of the slice: x: 2, y: 2, z: 4, core: 2. Of those that a mesh axis runs over, the one named last changes fastest.
Arguments:
- features: bfloat16 [1024, 24576], P('ctx', 'mp'), may hold values from -3 to 3
- destination: int32 [1024], P('ctx'), may hold values from 0 to 1023, as said below
- targets: int32 [1024], P('ctx'), may hold values from 0 to 4095
- domains: int32 [1024], P('ctx'), may hold values from 0 to 21
- domain_tokens: int32 [22], replicated, may hold values from 23 to 92
- short_filter: float32 [3, 4, 3, 2048], P(None, 'mp', None, 'ctx'), may hold values from -0.4 to 0.4
- long_filter: float32 [4, 2048, 1024], P('mp', 'ctx'), may hold values from -0.1875 to 0.1875
- skip: float32 [4, 2048], P('mp', 'ctx'), may hold values from 0.5 to 1.5
Outputs:
- mixed: bfloat16 [1024, 8192], P('ctx', 'mp')
- excess: float32 [22], replicated
The draws below stay inside these ranges and needn't reach their ends.
Inputs may be any that keep to these rules, and one draw needn't show every extreme that they name: destination is a permutation of the 1024 positions; each loader (block of 128 rows) sends its rows to the owners of position blocks of 128 in counts that are the same numbers for every loader in another order, at most 40 rows to one owner, and exactly 40 to one owner.
All inputs are finite; a program needn't handle non-finite values.
Results may differ from the reference program's by a relative error of at most 0.001.
Values may be sent and summed in bfloat16 or wider, within the bound.
A program may use at most 128 MiB of HBM per device.

```python
import math
import jax
import jax.numpy as jnp
import numpy as np
from jax import lax

D = 4096
TAPS = 3
MODELS = 2
DOMAINS = 22
ROWS = 128
SEQ = 1024
CAP = 40


def draw_destination(key, part):
    devices = SEQ // ROWS
    key_counts, key_delta, key_sigma, key_owner, key_slot, key_rows = jax.random.split(key, 6)
    remaining = ROWS - CAP
    others = devices - 1
    base_count = remaining // others
    surplus = remaining % others
    reach = max(min(base_count - 1, CAP - base_count - 1), 0)
    amounts_rest = base_count + (jnp.arange(others) < surplus).astype(jnp.int32)
    pair_count = others // 2
    if pair_count > 0:
        change = jax.random.randint(key_delta, (pair_count,), 0, reach + 1).astype(jnp.int32)
        amounts_rest = amounts_rest.at[0:2 * pair_count:2].add(change)
        amounts_rest = amounts_rest.at[1:2 * pair_count:2].add(-change)
    amounts = jnp.concatenate([jnp.array([CAP], jnp.int32), amounts_rest.astype(jnp.int32)])
    amounts = jax.random.permutation(key_counts, amounts)
    ends = jnp.cumsum(amounts)
    row_index = jnp.arange(ROWS, dtype=jnp.int32)
    step_of_row = jnp.sum((row_index[:, None] >= ends[None, :]).astype(jnp.int32), axis=1)
    sigma = jax.random.permutation(key_sigma, devices).astype(jnp.int32)
    mapping = jax.random.permutation(key_owner, devices).astype(jnp.int32)
    owner_dev = mapping[(sigma[:, None] + step_of_row[None, :]) % devices]
    slot_tables = jax.vmap(lambda inner_key: jax.random.permutation(inner_key, ROWS))(jax.random.split(key_slot, devices)).astype(jnp.int32)
    position = owner_dev * ROWS + slot_tables[owner_dev, row_index[None, :]]
    shuffle = jax.vmap(lambda inner_key: jax.random.permutation(inner_key, ROWS))(jax.random.split(key_rows, devices)).astype(jnp.int32)
    loader_index = jnp.arange(devices, dtype=jnp.int32)[:, None]
    placed = jnp.zeros((devices, ROWS), jnp.int32).at[loader_index, shuffle].set(position)
    return placed.reshape(SEQ)


def plant(entries, rng, smallest, high):
    index_at = [jax.random.randint(jax.random.fold_in(rng, axis), (), 0, length) for axis, length in enumerate(entries.shape)]
    longest = entries.shape.index(max(entries.shape))
    beside = index_at[:longest] + [(index_at[longest] + 1) % entries.shape[longest]] + index_at[longest + 1:]
    return entries.at[tuple(index_at)].set(smallest).at[tuple(beside)].set(high)


def levels(key, extent, pieces, smallest, high):
    gain = 1.0
    for axis_at, blocks in pieces:
        steps = jax.random.uniform(jax.random.fold_in(jax.random.fold_in(key, 6), axis_at), (blocks,), jnp.float32, smallest / len(pieces), high / len(pieces))
        gain = gain * jnp.repeat(jnp.exp(steps), extent[axis_at] // blocks).reshape((-1,) + (1,) * (len(extent) - 1 - axis_at))
    return gain


def rank_bounds(number_of, slope):
    portions = [(1 << 20) // math.isqrt(standing ** slope) + 1 for standing in range(1, number_of + 1)]
    width = 1 + sum(portions) // (1 << 30)
    return np.cumsum(np.array([max(1, weight // width) for weight in portions]))


def ranked(stream_key, extent, amount, lean):
    listing = rank_bounds(amount, lean)
    lot = jax.random.randint(jax.random.fold_in(stream_key, 1), extent, 0, int(listing[amount - 1]))
    grade = jnp.searchsorted(jnp.asarray(listing, jnp.int32), lot, side="right")
    return jax.random.permutation(jax.random.fold_in(stream_key, 2), amount)[grade].astype(jnp.int32)


def centred(rng, shape, spread, limit, cuts=(), held_as=jnp.bfloat16):
    entries = spread * jax.random.normal(rng, shape, jnp.float32)
    if cuts:
        entries = entries * levels(rng, shape, cuts, -0.22, 0.18)
    return jnp.clip(entries, -limit, limit).astype(held_as)


def setup_inputs(seed: int = 0) -> dict:
    splits = jax.random.split(jax.random.key(seed), 9)
    features = centred(splits[0], (SEQ, 3 * MODELS * D), 1.0, 3.0, ((0, 8), (1, 4)))
    destination = draw_destination(jax.random.fold_in(splits[8], 71), 0)
    targets = plant(jax.random.randint(splits[2], (SEQ,), 0, D), jax.random.fold_in(splits[2], 1), 0, D - 1).astype(jnp.int32)
    domains = plant(ranked(splits[3], (SEQ,), DOMAINS, 2), jax.random.fold_in(splits[3], 3), 0, DOMAINS - 1).astype(jnp.int32)
    domain_tokens = plant(jax.random.randint(splits[4], (DOMAINS,), SEQ // (2 * DOMAINS), 2 * SEQ // DOMAINS), jax.random.fold_in(splits[4], 1), SEQ // (2 * DOMAINS), (2 * SEQ // DOMAINS) - 1).astype(jnp.int32)
    short_filter = jnp.clip(jax.random.uniform(splits[5], (TAPS, 2 * MODELS, 3, D // 2), jnp.float32, -0.4, 0.4) * levels(splits[5], (TAPS, 2 * MODELS, 3, D // 2), ((1, 4), (3, 8)), -0.4, 0.0), -0.4, 0.4)
    long_filter = centred(splits[6], (2 * MODELS, D // 2, SEQ), SEQ ** -0.5, 0.1875, ((0, 4), (1, 8)), jnp.float32)
    skip = jnp.clip(0.5 + 1.0 * jax.random.uniform(splits[7], (2 * MODELS, D // 2), jnp.float32) ** levels(splits[7], (2 * MODELS, D // 2), ((0, 4), (1, 8)), -0.2, 0.2), 0.5, 1.5)
    return {"features": features, "destination": destination, "targets": targets, "domains": domains, "domain_tokens": domain_tokens, "short_filter": short_filter, "long_filter": long_filter, "skip": skip}


def reference(features, destination, targets, domains, domain_tokens, short_filter, long_filter, skip):
    half_width = D // 2
    inverse_order = jnp.zeros((SEQ,), jnp.int32).at[destination].set(jnp.arange(SEQ, dtype=jnp.int32))

    def one_copy(copy_index):
        block_cols = lax.dynamic_slice_in_dim(features, copy_index * 3 * half_width, 3 * half_width, 1)
        seq_rows = jnp.take(block_cols, inverse_order, axis=0).astype(jnp.float32).reshape(SEQ, 3, half_width)
        tap_weights = lax.dynamic_index_in_dim(short_filter, copy_index, 1, keepdims=False)
        shorted = jnp.zeros((SEQ, 3, half_width), jnp.float32)
        for tap_index in range(TAPS):
            shifted = jnp.pad(seq_rows, ((tap_index, 0), (0, 0), (0, 0)))[:SEQ]
            shorted = shorted + tap_weights[tap_index][None] * shifted
        signal = shorted[:, 0] * shorted[:, 2]
        kernel = lax.dynamic_index_in_dim(long_filter, copy_index, 0, keepdims=False).T
        spectrum = jnp.fft.rfft(signal, n=2 * SEQ, axis=0) * jnp.fft.rfft(kernel, n=2 * SEQ, axis=0)
        long_part = jnp.fft.irfft(spectrum, n=2 * SEQ, axis=0)[:SEQ]
        skip_gain = lax.dynamic_index_in_dim(skip, copy_index, 0, keepdims=False)
        return (shorted[:, 1] * (long_part + skip_gain[None] * signal)).astype(jnp.bfloat16)

    all_copies = lax.map(one_copy, jnp.arange(2 * MODELS, dtype=jnp.int32))
    mixed = jnp.transpose(all_copies, (1, 0, 2)).reshape(SEQ, MODELS * D)
    values = mixed.astype(jnp.float32).reshape(SEQ, MODELS, D)
    log_totals = jnp.log(jnp.sum(jnp.exp(values), axis=2))
    target_index = jnp.broadcast_to(targets[:, None, None], (SEQ, MODELS, 1)).astype(jnp.int32)
    picked = jnp.take_along_axis(values, target_index, axis=2)[:, :, 0]
    losses = log_totals - picked
    token_excess = jnp.maximum(losses[:, 0] - losses[:, 1], 0.0)
    domain_sums = jax.ops.segment_sum(token_excess, domains, num_segments=DOMAINS)
    return mixed, domain_sums / domain_tokens.astype(token_excess.dtype)
```

```python
import functools
import math

import jax
import jax.numpy as jnp
import numpy as np
from jax import lax
from jax.experimental import pallas as pl
from jax.experimental.pallas import tpu as pltpu
from jax.sharding import PartitionSpec as P

MODELS = 2


HIGHEST = lax.Precision.HIGHEST


def dft_tables(count, limit, modulus):
    row_index = jnp.arange(count, dtype=jnp.int32)[:, None]
    col_index = jnp.arange(limit, dtype=jnp.int32)[None, :]
    angle = 2.0 * math.pi / modulus * (row_index * col_index % modulus).astype(jnp.float32)
    return (jnp.cos(angle), jnp.sin(angle))


def forward_transform(signal, outer_cos, outer_sin, twist_cos, twist_sin, inner_cos, inner_sin):
    real_a = jnp.einsum("kp,cpq->ckq", outer_cos, signal, precision=HIGHEST)
    imag_a = -jnp.einsum("kp,cpq->ckq", outer_sin, signal, precision=HIGHEST)
    real_b = real_a * twist_cos + imag_a * twist_sin
    imag_b = imag_a * twist_cos - real_a * twist_sin
    real_c = jnp.einsum("ckq,qj->ckj", real_b, inner_cos, precision=HIGHEST) + jnp.einsum(
        "ckq,qj->ckj", imag_b, inner_sin, precision=HIGHEST
    )
    imag_c = jnp.einsum("ckq,qj->ckj", imag_b, inner_cos, precision=HIGHEST) - jnp.einsum(
        "ckq,qj->ckj", real_b, inner_sin, precision=HIGHEST
    )
    return (real_c, imag_c)


def causal_convolution(signal, kernel):
    channels, length = signal.shape
    inner_size = 128
    outer_size = 2 * length // inner_size
    half_outer = outer_size // 2
    outer_cos, outer_sin = dft_tables(outer_size, half_outer, outer_size)
    twist_cos, twist_sin = dft_tables(outer_size, inner_size, 2 * length)
    inner_cos, inner_sin = dft_tables(inner_size, inner_size, inner_size)
    sig_re, sig_im = forward_transform(
        signal.reshape(channels, half_outer, inner_size),
        outer_cos,
        outer_sin,
        twist_cos,
        twist_sin,
        inner_cos,
        inner_sin,
    )
    ker_re, ker_im = forward_transform(
        kernel.reshape(channels, half_outer, inner_size),
        outer_cos,
        outer_sin,
        twist_cos,
        twist_sin,
        inner_cos,
        inner_sin,
    )
    prod_re = sig_re * ker_re - sig_im * ker_im
    prod_im = sig_re * ker_im + sig_im * ker_re
    back_re = jnp.einsum("ckj,qj->ckq", prod_re, inner_cos, precision=HIGHEST) - jnp.einsum(
        "ckj,qj->ckq", prod_im, inner_sin, precision=HIGHEST
    )
    back_im = jnp.einsum("ckj,qj->ckq", prod_im, inner_cos, precision=HIGHEST) + jnp.einsum(
        "ckj,qj->ckq", prod_re, inner_sin, precision=HIGHEST
    )
    turned_re = back_re * twist_cos - back_im * twist_sin
    turned_im = back_im * twist_cos + back_re * twist_sin
    result = jnp.einsum("kp,ckq->cpq", outer_cos, turned_re, precision=HIGHEST) - jnp.einsum(
        "kp,ckq->cpq", outer_sin, turned_im, precision=HIGHEST
    )
    return (result / (2.0 * length)).reshape(channels, length)


def general_body(features, destination, targets, domains, domain_tokens, short_filter, long_filter, skip):
    devices = lax.axis_size("ctx")
    rows_here = features.shape[0]
    length = devices * rows_here
    half_width = features.shape[1] // 3
    channels = half_width // devices
    capacity = 5 * rows_here // (2 * devices)
    owner_dev = destination // rows_here
    offset = destination % rows_here
    order = jnp.arange(rows_here, dtype=jnp.int32)
    ahead = (owner_dev[:, None] == owner_dev[None, :]) & (order[None, :] < order[:, None])
    slot_rank = jnp.sum(ahead.astype(jnp.int32), axis=1)
    buffer = (
        jnp.zeros((devices, capacity, 3 * half_width), features.dtype)
        .at[owner_dev, slot_rank]
        .set(features)
    )
    places = (
        jnp.full((devices, capacity), rows_here, jnp.int32).at[owner_dev, slot_rank].set(offset)
    )
    arrived, arrived_places = (
        lax.all_to_all(buffer, "ctx", split_axis=0, concat_axis=0, tiled=True),
        lax.all_to_all(places, "ctx", split_axis=0, concat_axis=0, tiled=True),
    )
    ordered = jnp.zeros((rows_here + 1, 3 * half_width), features.dtype)
    ordered = ordered.at[arrived_places.reshape(-1)].set(arrived.reshape(-1, 3 * half_width))[
        :rows_here
    ]
    blocks = ordered.reshape(rows_here, 3, devices, channels).transpose(2, 1, 3, 0)
    columns = lax.all_to_all(blocks, "ctx", split_axis=0, concat_axis=3, tiled=True)[0]
    inputs = columns.astype(jnp.float32)
    tap_weights = short_filter[:, 0]
    shorted = jnp.zeros_like(inputs)
    for tap_index in range(tap_weights.shape[0]):
        shifted = jnp.pad(inputs, ((0, 0), (0, 0), (tap_index, 0)))[:, :, :length]
        shorted = shorted + tap_weights[tap_index][:, :, None] * shifted
    signal = shorted[0] * shorted[2]
    long_part = causal_convolution(signal, long_filter[0])
    output_cols = (shorted[1] * (long_part + skip[0][:, None] * signal)).astype(jnp.bfloat16)
    returned = lax.all_to_all(
        output_cols.reshape(channels, devices, rows_here),
        "ctx",
        split_axis=1,
        concat_axis=0,
        tiled=True,
    )
    mixed = returned.reshape(half_width, rows_here).T
    copy_index = lax.axis_index("mp")
    model_index = copy_index // 2
    half_index = copy_index % 2
    values = mixed.astype(jnp.float32)
    part_exp = jnp.sum(jnp.exp(values), axis=1)
    local_target = targets - half_index * half_width
    inside = (local_target >= 0) & (local_target < half_width)
    picked = jnp.take_along_axis(
        values, jnp.clip(local_target, 0, half_width - 1)[:, None], axis=1
    )[:, 0]
    part_target = jnp.where(inside, picked, 0.0)
    is_model = jnp.arange(MODELS, dtype=jnp.int32)[:, None] == model_index
    exp_terms = jnp.where(is_model, part_exp[None, :], 0.0)
    target_terms = jnp.where(is_model, part_target[None, :], 0.0)
    total_exp, total_target = lax.psum((exp_terms, target_terms), "mp")
    losses = jnp.log(total_exp) - total_target
    token_excess = jnp.maximum(losses[0] - losses[1], 0.0)
    domain_count = domain_tokens.shape[0]
    in_domain = domains[None, :] == jnp.arange(domain_count, dtype=jnp.int32)[:, None]
    partial_sums = jnp.sum(jnp.where(in_domain, token_excess[None, :], 0.0), axis=1)
    domain_sums = lax.psum(partial_sums, "ctx")
    return (mixed, domain_sums / domain_tokens.astype(jnp.float32))


INNER = 128
OUTER = 16
FREQS = OUTER // 2 + 1
BF16 = jnp.bfloat16
F32 = jnp.float32


def weighted(terms):
    total = None
    for coef, value in terms:
        if value is None or abs(coef) < 1e-9:
            continue
        if abs(abs(coef) - 1.0) < 1e-9:
            term = value
            if coef < 0:
                total = -term if total is None else total - term
                continue
        else:
            term = coef * value
        total = term if total is None else total + term
    return total


def outer_forward(blocks):
    real, imag = [None] * FREQS, [None] * FREQS
    for k in range(FREQS // 2 + 1):
        angle = [2.0 * math.pi * p * k / OUTER for p in range(8)]
        parts = []
        for first in (0, 1):
            picks = range(first, 8, 2)
            parts.append(weighted([(math.cos(angle[p]), blocks[p]) for p in picks]))
            parts.append(weighted([(-math.sin(angle[p]), blocks[p]) for p in picks]))
        real_even, imag_even, real_odd, imag_odd = parts
        real[k] = weighted([(1.0, real_even), (1.0, real_odd)])
        imag[k] = weighted([(1.0, imag_even), (1.0, imag_odd)])
        if k < 4:
            real[8 - k] = weighted([(1.0, real_even), (-1.0, real_odd)])
            imag[8 - k] = weighted([(-1.0, imag_even), (1.0, imag_odd)])
    return real, imag


def outer_backward(real, imag):
    sums = {}
    for sign in (1.0, -1.0):
        sums[sign] = [
            (
                weighted([(1.0, real[k]), (sign, real[8 - k])]),
                weighted([(1.0, imag[k]), (-sign, imag[8 - k])]) if k else None,
            )
            for k in range(4)
        ]
    blocks = []
    for a in range(8):
        sign = 1.0 if a % 2 == 0 else -1.0
        terms = [(1.0, sums[sign][0][0])]
        for k in range(1, 4):
            angle = 2.0 * math.pi * k * a / OUTER
            terms.append((math.cos(angle), sums[sign][k][0]))
            terms.append((-math.sin(angle), sums[sign][k][1]))
        terms.append((math.cos(math.pi * a / 2), real[4]))
        terms.append((-math.sin(math.pi * a / 2), imag[4]))
        blocks.append(weighted(terms))
    return blocks


def halves(value):
    high = value.astype(BF16)
    return high, (value - high.astype(F32)).astype(BF16)


def stacked_dot(left, right, dims=(((1,), (0,)), ((), ()))):
    return lax.dot_general(left, right, dims, preferred_element_type=F32)


def table_inputs():
    index = np.arange(INNER)
    inner = 2.0 * np.pi * (np.outer(index, index) % INNER) / INNER
    twist = 2.0 * np.pi * np.outer(np.arange(FREQS), index) / (OUTER * INNER)
    inner_tab = np.stack([np.cos(inner), np.sin(inner)]).astype(np.float32)
    row_tab = np.stack([np.cos(twist), np.sin(twist)])[:, :, None, :].astype(np.float32)
    return jnp.asarray(inner_tab), jnp.asarray(row_tab)


def make_tables(inner_ref, row_ref, forward, backward):
    lower, upper = pl.ds(0, INNER), pl.ds(INNER, INNER)

    def store(ref, k, cos, sin, flip):
        cos_parts, sin_parts = halves(cos), halves(sin)
        for place, kind in ((0, 0), (1, 0), (2, 1)):
            c, s = cos_parts[kind], sin_parts[kind]
            first = pl.ds(place * 2 * INNER, INNER)
            second = pl.ds(place * 2 * INNER + INNER, INNER)
            ref[k, lower, first] = c
            ref[k, lower, second] = -s if flip else s
            ref[k, upper, first] = s if flip else -s
            ref[k, upper, second] = c

    def step(k, carry):
        base_cos, base_sin = inner_ref[0], inner_ref[1]
        row_cos, row_sin = row_ref[0, k], row_ref[1, k]
        cos, sin = base_cos * row_cos - base_sin * row_sin, base_sin * row_cos + base_cos * row_sin
        store(forward, k, cos, sin, False)
        col_cos = jnp.broadcast_to(row_cos, (INNER, INNER)).T
        col_sin = jnp.broadcast_to(row_sin, (INNER, INNER)).T
        cos, sin = base_cos * col_cos - base_sin * col_sin, base_sin * col_cos + base_cos * col_sin
        store(backward, k, cos, sin, True)
        return carry

    lax.fori_loop(0, FREQS, step, 0)


def filter_spectrum(filter_ref, forward, work, spectrum_ref):
    channels = filter_ref.shape[1]

    def stage(block, carry):
        rows = pl.ds(pl.multiple_of(block * 16, 16), 16)
        real, imag = outer_forward([filter_ref[0, rows, pl.ds(p * INNER, INNER)] for p in range(8)])
        for k in range(FREQS):
            for place, part in ((0, real[k]), (INNER, imag[k])):
                part = jnp.zeros((16, INNER), F32) if part is None else part
                high, low = halves(part)
                work[k, rows, pl.ds(place, INNER)] = high
                work[k, rows, pl.ds(place + 2 * INNER, INNER)] = low
                work[k, rows, pl.ds(place + 4 * INNER, INNER)] = high
        return carry

    lax.fori_loop(0, channels // 16, stage, 0)

    def transform(k, carry):
        scale = jnp.where((k == 0) | (k == FREQS - 1), 0.5, 1.0) * (2.0 / (OUTER * INNER))
        spectrum_ref[k] = scale * stacked_dot(forward[k], work[k], (((1,), (1,)), ((), ())))
        return carry

    lax.fori_loop(0, FREQS, transform, 0)


WIDTH = 128


def build_picks(places, pick_ref):
    length = pick_ref.shape[0]

    def step(block, carry):
        here = lax.broadcasted_iota(jnp.int32, (128, length), 0) + block * 128
        rows = pl.ds(pl.multiple_of(block * 128, 128), 128)
        pick_ref[rows, :] = jnp.where(here == places, 1.0, 0.0).astype(BF16)
        return carry

    lax.fori_loop(0, length // 128, step, 0)


def order_rows(cols_ref, pick_ref, seq_ref, first, width):
    length = cols_ref.shape[0]

    def step(block, carry):
        rows = pl.multiple_of(block * 256, 256)
        seq_ref[pl.ds(rows + 8, 256), pl.ds(first, width)] = jnp.dot(
            pick_ref[pl.ds(rows, 256), :], cols_ref[:, pl.ds(first, width)],
            preferred_element_type=F32,
        )
        return carry

    lax.fori_loop(0, length // 256, step, 0)


def shorted_rows(seq_ref, taps_ref, start, count, place, part, here):
    window = seq_ref[pl.ds(start, count + 8), pl.ds(place * WIDTH, WIDTH)]
    total = None
    for tap in range(taps_ref.shape[0] // 3):
        weight = taps_ref[tap * 3 + part, :, here]
        term = weight * window[8 - tap : 8 + count - tap]
        total = term if total is None else total + term
    return total


def short_and_outer(seq_ref, taps_ref, work, signal_ref, here):
    def stage(block, carry):
        offset = pl.multiple_of(block * 16, 16)
        signals = []
        for p in range(8):
            rows = pl.ds(p * INNER + offset, 16)
            start = pl.multiple_of(p * INNER + block * 16, 16)
            signal = shorted_rows(seq_ref, taps_ref, start, 16, 0, 0, here) * shorted_rows(
                seq_ref, taps_ref, start, 16, 1, 2, here
            )
            signal_ref[rows, :] = signal
            signals.append(signal)
        real, imag = outer_forward(signals)
        for k in range(FREQS):
            for place, part in ((0, real[k]), (INNER, imag[k])):
                part = jnp.zeros((16, WIDTH), F32) if part is None else part
                high, low = halves(part)
                work[k, pl.ds(place + offset, 16), :] = high
                work[k, pl.ds(place + 2 * INNER + offset, 16), :] = low
                work[k, pl.ds(place + 4 * INNER + offset, 16), :] = high
        return carry

    lax.fori_loop(0, INNER // 16, stage, 0)


def transform_product(spectrum_ref, forward, backward, work, back_ref, here):
    def step(k, carry):
        value = stacked_dot(forward[k], work[k])
        real, imag = value[:INNER], value[INNER:]
        other = spectrum_ref[k, :, here]
        other_real, other_imag = other[:INNER], other[INNER:]
        product = jnp.concatenate(
            [real * other_real - imag * other_imag, real * other_imag + imag * other_real], axis=0
        )
        high, low = halves(product)
        back_ref[k] = stacked_dot(backward[k], jnp.concatenate([high, low, high], axis=0))
        return carry

    lax.fori_loop(0, FREQS, step, 0, unroll=3)


def long_and_direct(back_ref, signal_ref, skip_ref, total_ref, piece, here):
    def step(block, carry):
        offset = pl.multiple_of(block * 16, 16)
        real = [back_ref[k, pl.ds(offset, 16), :] for k in range(FREQS)]
        imag = [
            back_ref[k, pl.ds(INNER + offset, 16), :] if 0 < k < FREQS - 1 else None
            for k in range(FREQS)
        ]
        direct = skip_ref[pl.ds(0, 1), here]
        for p, long_part in enumerate(outer_backward(real, imag)):
            rows = pl.ds(p * INNER + offset, 16)
            total_ref[piece, rows, :] = long_part + direct * signal_ref[rows, :]
        return carry

    lax.fori_loop(0, INNER // 16, step, 0)


LIMIT = 56 * 2**20
MESH = pl.DeviceIdType.MESH
PARTS = ((0, 0), (1, 2), (2, 1))


def whole_kernel(
    devices, copies, pieces,
    features, place_ref, target_ref, domain_ref, taps_ref, filter_hbm, skip_ref,
    inner_ref, row_ref,
    mixed_ref, sums_ref,
    filter_ref, cols, places, pick_ref, wanted_ref, spectrum, forward, backward, filter_work,
    seq_ref, work, back_ref, signal_ref, total_ref, out_ref, exp_ref, hit_ref,
    given, stats, both_stats, domain_sums,
    in_send, in_recv, own_sem, place_send, place_recv, out_send, out_recv, out_own,
    given_send, given_recv, both_send, both_recv, sum_send, sum_recv, filter_sem,
):
    me = lax.axis_index("ctx")
    copy_index = lax.axis_index("mp")
    rows_here, half_width = mixed_ref.shape
    channels = half_width // devices

    def after(step):
        return lax.rem(me + step, devices)

    def before(step):
        return lax.rem(me + devices - step, devices)

    def rows_of(device):
        return pl.ds(pl.multiple_of(device * rows_here, rows_here), rows_here)

    def feature_cols(device, part, piece):
        start = part * half_width + device * channels + piece * WIDTH
        return pl.ds(pl.multiple_of(start, WIDTH), WIDTH)

    def mixed_cols(device, piece):
        return pl.ds(pl.multiple_of(device * channels + piece * WIDTH, WIDTH), WIDTH)

    def place_cols(place):
        return pl.ds(place * WIDTH, WIDTH)

    def ctx_copy(source, target, send, recv, step):
        return pltpu.make_async_remote_copy(
            src_ref=source, dst_ref=target, send_sem=send, recv_sem=recv,
            device_id={"ctx": after(step)}, device_id_type=MESH,
        )

    def place_copy(step, source):
        return ctx_copy(
            places.at[me], places.at[source], place_send.at[step], place_recv.at[step], step
        )

    def in_copy(piece, step, kind, source):
        place, part = PARTS[kind]
        return ctx_copy(
            features.at[:, feature_cols(after(step), part, piece)],
            cols.at[piece, rows_of(source), place_cols(place)],
            in_send.at[piece, step, kind], in_recv.at[piece, step, kind], step,
        )

    def own_copy(piece, kind):
        place, part = PARTS[kind]
        return pltpu.make_async_copy(
            features.at[:, feature_cols(me, part, piece)],
            cols.at[piece, rows_of(me), place_cols(place)],
            own_sem.at[piece, kind],
        )

    def out_copy(piece, step, source):
        return ctx_copy(
            out_ref.at[piece, rows_of(after(step)), :],
            mixed_ref.at[:, mixed_cols(source, piece)],
            out_send.at[piece, step], out_recv.at[piece, step], step,
        )

    def out_own_copy(piece):
        return pltpu.make_async_copy(
            out_ref.at[piece, rows_of(me), :], mixed_ref.at[:, mixed_cols(me, piece)],
            out_own.at[piece],
        )

    def given_copy(step, source):
        return ctx_copy(
            given.at[after(step)], stats.at[source], given_send.at[step], given_recv.at[step], step
        )

    def sum_copy(step, source):
        return ctx_copy(
            domain_sums.at[me], domain_sums.at[source], sum_send.at[step], sum_recv.at[step], step
        )

    def both_copy(near, source):
        return pltpu.make_async_remote_copy(
            src_ref=both_stats.at[copy_index], dst_ref=both_stats.at[source],
            send_sem=both_send.at[near], recv_sem=both_recv.at[near],
            device_id={"mp": lax.rem(copy_index + near, copies)}, device_id_type=MESH,
        )

    def each(count, action):
        def step(index, carry):
            action(index)
            return carry

        lax.fori_loop(1, count, step, 0)

    def send(piece, kinds):
        def start(s):
            for kind in kinds:
                in_copy(piece, s, kind, me).start()

        each(devices, start)

    def arrive(piece, kinds):
        def wait(s):
            for kind in kinds:
                in_copy(piece, s, kind, before(s)).wait_recv()

        each(devices, wait)
        for kind in kinds:
            own_copy(piece, kind).wait()

    barrier = pltpu.get_barrier_semaphore()
    each(devices, lambda s: pl.semaphore_signal(
        barrier, inc=1, device_id={"ctx": after(s)}, device_id_type=MESH))
    each(copies, lambda s: pl.semaphore_signal(
        barrier, inc=1, device_id={"mp": lax.rem(copy_index + s, copies)}, device_id_type=MESH))
    places[me] = jnp.concatenate([place_ref[...], target_ref[...]], axis=0)
    pl.semaphore_wait(barrier, devices + copies - 2)

    send(0, (0, 1))
    each(devices, lambda s: place_copy(s, me).start())
    for piece in range(1, pieces):
        send(piece, (0, 1))
    for piece in range(pieces):
        send(piece, (2,))
    filter_copy = pltpu.make_async_copy(filter_hbm, filter_ref, filter_sem)
    filter_copy.start()
    for piece in range(pieces):
        for kind in range(3):
            own_copy(piece, kind).start()

    make_tables(inner_ref, row_ref, forward, backward)
    filter_copy.wait()
    filter_spectrum(filter_ref, forward, filter_work, spectrum)
    seq_ref[pl.ds(0, 8), :] = jnp.zeros((8, seq_ref.shape[1]), F32)

    each(devices, lambda s: place_copy(s, before(s)).wait_recv())
    build_picks(jnp.concatenate([places[d][0:1] for d in range(devices)], axis=1), pick_ref)
    base = lax.rem(copy_index, 2) * half_width + me * channels

    @pl.loop(0, devices)
    def _(device):
        loader = places[device][1:2]
        wanted_ref[rows_of(device), :] = jnp.broadcast_to(loader - base, (rows_here, rows_here)).T

    for piece in range(pieces):
        here = pl.ds(piece * WIDTH, WIDTH)
        arrive(piece, (0, 1))
        order_rows(cols.at[piece], pick_ref, seq_ref, 0, 2 * WIDTH)
        short_and_outer(seq_ref, taps_ref, work, signal_ref, here)
        transform_product(spectrum, forward, backward, work, back_ref, here)
        long_and_direct(back_ref, signal_ref, skip_ref, total_ref, piece, here)

    lane = lax.broadcasted_iota(jnp.int32, (rows_here, WIDTH), 1)
    picker = lax.broadcasted_iota(jnp.int32, (8, 4 * WIDTH), 1) < 3 * WIDTH
    picker_row = lax.broadcasted_iota(jnp.int32, (8, 4 * WIDTH), 0)
    picker = jnp.where((picker & (picker_row == 0)) | (~picker & (picker_row == 1)), 1.0, 0.0)
    picker = picker.astype(BF16)

    for piece in range(pieces):
        here = pl.ds(piece * WIDTH, WIDTH)
        arrive(piece, (2,))
        order_rows(cols.at[piece], pick_ref, seq_ref, 2 * WIDTH, WIDTH)

        def gate(owner, piece=piece, here=here):
            start = pl.multiple_of(owner * rows_here, rows_here)
            value = shorted_rows(seq_ref, taps_ref, start, rows_here, 2, 1, here)
            value = value * total_ref[piece, rows_of(owner), :]
            out_ref[piece, rows_of(owner), :] = value.astype(out_ref.dtype)

        def give(s, piece=piece, gate=gate):
            gate(after(s))
            out_copy(piece, s, me).start()

        each(devices, give)
        gate(me)
        out_own_copy(piece).start()

        def tally(owner, piece=piece):
            rows = rows_of(owner)
            value = out_ref[piece, rows, :].astype(F32)
            power = jnp.exp(value)
            hit = jnp.where(lane + piece * WIDTH == wanted_ref[rows, :], value, 0.0)
            if piece:
                power = power + exp_ref[rows, :]
                hit = hit + hit_ref[rows, :]
            if piece < pieces - 1:
                exp_ref[rows, :] = power
                hit_ref[rows, :] = hit
                return
            high, low = halves(power)
            rest = (power - high.astype(F32) - low.astype(F32)).astype(BF16)
            terms = jnp.concatenate([high, low, rest, hit.astype(BF16)], axis=1)
            sums = stacked_dot(picker, terms, (((1,), (1,)), ((), ())))
            given[owner] = sums[0:2]

        def tell(s, piece=piece, tally=tally):
            tally(after(s))
            if piece == pieces - 1:
                given_copy(s, me).start()

        each(devices, tell)
        tally(me)

    stats[me] = given[me]
    each(devices, lambda s: given_copy(s, before(s)).wait_recv())
    here_stats = stats[0]
    for device in range(1, devices):
        here_stats = here_stats + stats[device]
    both_stats[copy_index] = here_stats
    each(copies, lambda s: both_copy(s, copy_index).start())
    each(copies, lambda s: both_copy(s, lax.rem(copy_index + copies - s, copies)).wait_recv())
    losses = []
    for model in range(MODELS):
        both = both_stats[2 * model] + both_stats[2 * model + 1]
        losses.append(jnp.log(both[0:1]) - both[1:2])
    excess = jnp.maximum(losses[0] - losses[1], 0.0)
    kind = lax.broadcasted_iota(jnp.int32, (WIDTH, rows_here), 0)
    by_kind = jnp.where(kind == domain_ref[...], excess, 0.0)
    domain_sums[me] = jnp.sum(by_kind.T, axis=0, keepdims=True)
    each(devices, lambda s: sum_copy(s, me).start())
    each(devices, lambda s: place_copy(s, me).wait_send())
    for piece in range(pieces):
        def sent(s, piece=piece):
            for kind in range(3):
                in_copy(piece, s, kind, me).wait_send()

        each(devices, sent)
    each(devices, lambda s: given_copy(s, me).wait_send())
    each(copies, lambda s: both_copy(s, copy_index).wait_send())
    each(devices, lambda s: sum_copy(s, before(s)).wait_recv())
    sums = domain_sums[0]
    for device in range(1, devices):
        sums = sums + domain_sums[device]
    sums_ref[...] = sums[:, : sums_ref.shape[1]]
    each(devices, lambda s: sum_copy(s, me).wait_send())
    for piece in range(pieces):
        def done(s, piece=piece):
            out_copy(piece, s, before(s)).wait_recv()
            out_copy(piece, s, me).wait_send()

        each(devices, done)
        out_own_copy(piece).wait()


def body(features, destination, targets, domains, domain_tokens, short_filter, long_filter, skip):
    devices = lax.axis_size("ctx")
    copies = lax.axis_size("mp")
    rows_here = features.shape[0]
    length = devices * rows_here
    half_width = features.shape[1] // 3
    channels = half_width // devices
    if length != 8 * INNER or rows_here != 128 or channels != 256 or copies != 4 or domain_tokens.shape[0] > WIDTH:
        return general_body(
            features, destination, targets, domains, domain_tokens, short_filter, long_filter, skip
        )
    pieces = channels // WIDTH
    count = domain_tokens.shape[0]
    vmem = pl.BlockSpec(memory_space=pltpu.VMEM)
    hbm = pl.BlockSpec(memory_space=pl.ANY)
    big = (FREQS, 2 * INNER, 6 * INNER)
    dma = pltpu.SemaphoreType.DMA
    mixed, sums = pl.pallas_call(
        functools.partial(whole_kernel, devices, copies, pieces),
        out_shape=[
            pltpu.VMEM((rows_here, half_width), BF16),
            pltpu.VMEM((1, count), F32),
        ],
        in_specs=[hbm, vmem, vmem, vmem, vmem, hbm, vmem, vmem, vmem],
        out_specs=[vmem, vmem],
        scratch_shapes=[
            pltpu.VMEM((1, channels, length), F32),
            pltpu.VMEM((pieces, length, 3 * WIDTH), BF16),
            pltpu.VMEM((devices, 2, rows_here), jnp.int32),
            pltpu.VMEM((length, length), BF16),
            pltpu.VMEM((length, WIDTH), jnp.int32),
            pltpu.VMEM((FREQS, 2 * INNER, channels), F32),
            pltpu.VMEM(big, BF16),
            pltpu.VMEM(big, BF16),
            pltpu.VMEM((FREQS, channels, 6 * INNER), BF16),
            pltpu.VMEM((length + 8, 3 * WIDTH), F32),
            pltpu.VMEM((FREQS, 6 * INNER, WIDTH), BF16),
            pltpu.VMEM((FREQS, 2 * INNER, WIDTH), F32),
            pltpu.VMEM((length, WIDTH), F32),
            pltpu.VMEM((pieces, length, WIDTH), F32),
            pltpu.VMEM((pieces, length, WIDTH), BF16),
            pltpu.VMEM((length, WIDTH), F32),
            pltpu.VMEM((length, WIDTH), F32),
            pltpu.VMEM((devices, 2, rows_here), F32),
            pltpu.VMEM((devices, 2, rows_here), F32),
            pltpu.VMEM((copies, 2, rows_here), F32),
            pltpu.VMEM((devices, 1, WIDTH), F32),
            dma((pieces, devices, 3)),
            dma((pieces, devices, 3)),
            dma((pieces, 3)),
            dma((devices,)),
            dma((devices,)),
            dma((pieces, devices)),
            dma((pieces, devices)),
            dma((pieces,)),
            dma((devices,)),
            dma((devices,)),
            dma((copies,)),
            dma((copies,)),
            dma((devices,)),
            dma((devices,)),
            dma,
        ],
        compiler_params=pltpu.CompilerParams(
            vmem_limit_bytes=LIMIT, collective_id=0, has_side_effects=True
        ),
    )(
        features, destination.reshape(1, rows_here), targets.reshape(1, rows_here),
        domains.reshape(1, rows_here),
        short_filter.transpose(0, 2, 1, 3).reshape(-1, 1, channels), long_filter, skip,
        *table_inputs(),
    )
    return (mixed, sums.reshape(count) / domain_tokens.astype(F32))


def solution(mesh):
    return jax.shard_map(
        body,
        mesh=mesh,
        in_specs=(
            P("ctx", "mp"),
            P("ctx"),
            P("ctx"),
            P("ctx"),
            P(),
            P(None, "mp", None, "ctx"),
            P("mp", "ctx", None),
            P("mp", "ctx"),
        ),
        out_specs=(P("ctx", "mp"), P()),
        check_vma=False,
    )
```

```python
import functools
import math

import jax
import jax.numpy as jnp
import numpy as np
from jax import lax
from jax.experimental import pallas as pl
from jax.experimental.pallas import tpu as pltpu
from jax.sharding import PartitionSpec as P

MODELS = 2


HIGHEST = lax.Precision.HIGHEST


def dft_tables(count, limit, modulus):
    row_index = jnp.arange(count, dtype=jnp.int32)[:, None]
    col_index = jnp.arange(limit, dtype=jnp.int32)[None, :]
    angle = 2.0 * math.pi / modulus * (row_index * col_index % modulus).astype(jnp.float32)
    return (jnp.cos(angle), jnp.sin(angle))


def forward_transform(signal, outer_cos, outer_sin, twist_cos, twist_sin, inner_cos, inner_sin):
    real_a = jnp.einsum("kp,cpq->ckq", outer_cos, signal, precision=HIGHEST)
    imag_a = -jnp.einsum("kp,cpq->ckq", outer_sin, signal, precision=HIGHEST)
    real_b = real_a * twist_cos + imag_a * twist_sin
    imag_b = imag_a * twist_cos - real_a * twist_sin
    real_c = jnp.einsum("ckq,qj->ckj", real_b, inner_cos, precision=HIGHEST) + jnp.einsum(
        "ckq,qj->ckj", imag_b, inner_sin, precision=HIGHEST
    )
    imag_c = jnp.einsum("ckq,qj->ckj", imag_b, inner_cos, precision=HIGHEST) - jnp.einsum(
        "ckq,qj->ckj", real_b, inner_sin, precision=HIGHEST
    )
    return (real_c, imag_c)


def causal_convolution(signal, kernel):
    channels, length = signal.shape
    inner_size = 128
    outer_size = 2 * length // inner_size
    half_outer = outer_size // 2
    outer_cos, outer_sin = dft_tables(outer_size, half_outer, outer_size)
    twist_cos, twist_sin = dft_tables(outer_size, inner_size, 2 * length)
    inner_cos, inner_sin = dft_tables(inner_size, inner_size, inner_size)
    sig_re, sig_im = forward_transform(
        signal.reshape(channels, half_outer, inner_size),
        outer_cos,
        outer_sin,
        twist_cos,
        twist_sin,
        inner_cos,
        inner_sin,
    )
    ker_re, ker_im = forward_transform(
        kernel.reshape(channels, half_outer, inner_size),
        outer_cos,
        outer_sin,
        twist_cos,
        twist_sin,
        inner_cos,
        inner_sin,
    )
    prod_re = sig_re * ker_re - sig_im * ker_im
    prod_im = sig_re * ker_im + sig_im * ker_re
    back_re = jnp.einsum("ckj,qj->ckq", prod_re, inner_cos, precision=HIGHEST) - jnp.einsum(
        "ckj,qj->ckq", prod_im, inner_sin, precision=HIGHEST
    )
    back_im = jnp.einsum("ckj,qj->ckq", prod_im, inner_cos, precision=HIGHEST) + jnp.einsum(
        "ckj,qj->ckq", prod_re, inner_sin, precision=HIGHEST
    )
    turned_re = back_re * twist_cos - back_im * twist_sin
    turned_im = back_im * twist_cos + back_re * twist_sin
    result = jnp.einsum("kp,ckq->cpq", outer_cos, turned_re, precision=HIGHEST) - jnp.einsum(
        "kp,ckq->cpq", outer_sin, turned_im, precision=HIGHEST
    )
    return (result / (2.0 * length)).reshape(channels, length)


def general_body(features, destination, targets, domains, domain_tokens, short_filter, long_filter, skip):
    devices = lax.axis_size("ctx")
    rows_here = features.shape[0]
    length = devices * rows_here
    half_width = features.shape[1] // 3
    channels = half_width // devices
    capacity = 5 * rows_here // (2 * devices)
    owner_dev = destination // rows_here
    offset = destination % rows_here
    order = jnp.arange(rows_here, dtype=jnp.int32)
    ahead = (owner_dev[:, None] == owner_dev[None, :]) & (order[None, :] < order[:, None])
    slot_rank = jnp.sum(ahead.astype(jnp.int32), axis=1)
    buffer = (
        jnp.zeros((devices, capacity, 3 * half_width), features.dtype)
        .at[owner_dev, slot_rank]
        .set(features)
    )
    places = (
        jnp.full((devices, capacity), rows_here, jnp.int32).at[owner_dev, slot_rank].set(offset)
    )
    arrived, arrived_places = (
        lax.all_to_all(buffer, "ctx", split_axis=0, concat_axis=0, tiled=True),
        lax.all_to_all(places, "ctx", split_axis=0, concat_axis=0, tiled=True),
    )
    ordered = jnp.zeros((rows_here + 1, 3 * half_width), features.dtype)
    ordered = ordered.at[arrived_places.reshape(-1)].set(arrived.reshape(-1, 3 * half_width))[
        :rows_here
    ]
    blocks = ordered.reshape(rows_here, 3, devices, channels).transpose(2, 1, 3, 0)
    columns = lax.all_to_all(blocks, "ctx", split_axis=0, concat_axis=3, tiled=True)[0]
    inputs = columns.astype(jnp.float32)
    tap_weights = short_filter[:, 0]
    shorted = jnp.zeros_like(inputs)
    for tap_index in range(tap_weights.shape[0]):
        shifted = jnp.pad(inputs, ((0, 0), (0, 0), (tap_index, 0)))[:, :, :length]
        shorted = shorted + tap_weights[tap_index][:, :, None] * shifted
    signal = shorted[0] * shorted[2]
    long_part = causal_convolution(signal, long_filter[0])
    output_cols = (shorted[1] * (long_part + skip[0][:, None] * signal)).astype(jnp.bfloat16)
    returned = lax.all_to_all(
        output_cols.reshape(channels, devices, rows_here),
        "ctx",
        split_axis=1,
        concat_axis=0,
        tiled=True,
    )
    mixed = returned.reshape(half_width, rows_here).T
    copy_index = lax.axis_index("mp")
    model_index = copy_index // 2
    half_index = copy_index % 2
    values = mixed.astype(jnp.float32)
    part_exp = jnp.sum(jnp.exp(values), axis=1)
    local_target = targets - half_index * half_width
    inside = (local_target >= 0) & (local_target < half_width)
    picked = jnp.take_along_axis(
        values, jnp.clip(local_target, 0, half_width - 1)[:, None], axis=1
    )[:, 0]
    part_target = jnp.where(inside, picked, 0.0)
    is_model = jnp.arange(MODELS, dtype=jnp.int32)[:, None] == model_index
    exp_terms = jnp.where(is_model, part_exp[None, :], 0.0)
    target_terms = jnp.where(is_model, part_target[None, :], 0.0)
    total_exp, total_target = lax.psum((exp_terms, target_terms), "mp")
    losses = jnp.log(total_exp) - total_target
    token_excess = jnp.maximum(losses[0] - losses[1], 0.0)
    domain_count = domain_tokens.shape[0]
    in_domain = domains[None, :] == jnp.arange(domain_count, dtype=jnp.int32)[:, None]
    partial_sums = jnp.sum(jnp.where(in_domain, token_excess[None, :], 0.0), axis=1)
    domain_sums = lax.psum(partial_sums, "ctx")
    return (mixed, domain_sums / domain_tokens.astype(jnp.float32))


INNER = 128
OUTER = 16
FREQS = OUTER // 2 + 1
BF16 = jnp.bfloat16
F32 = jnp.float32


def weighted(terms):
    total = None
    for coef, value in terms:
        if value is None or abs(coef) < 1e-9:
            continue
        if abs(abs(coef) - 1.0) < 1e-9:
            term = value
            if coef < 0:
                total = -term if total is None else total - term
                continue
        else:
            term = coef * value
        total = term if total is None else total + term
    return total


def outer_forward(blocks):
    real, imag = [None] * FREQS, [None] * FREQS
    for k in range(FREQS // 2 + 1):
        angle = [2.0 * math.pi * p * k / OUTER for p in range(8)]
        parts = []
        for first in (0, 1):
            picks = range(first, 8, 2)
            parts.append(weighted([(math.cos(angle[p]), blocks[p]) for p in picks]))
            parts.append(weighted([(-math.sin(angle[p]), blocks[p]) for p in picks]))
        real_even, imag_even, real_odd, imag_odd = parts
        real[k] = weighted([(1.0, real_even), (1.0, real_odd)])
        imag[k] = weighted([(1.0, imag_even), (1.0, imag_odd)])
        if k < 4:
            real[8 - k] = weighted([(1.0, real_even), (-1.0, real_odd)])
            imag[8 - k] = weighted([(-1.0, imag_even), (1.0, imag_odd)])
    return real, imag


def outer_backward(real, imag):
    sums = {}
    for sign in (1.0, -1.0):
        sums[sign] = [
            (
                weighted([(1.0, real[k]), (sign, real[8 - k])]),
                weighted([(1.0, imag[k]), (-sign, imag[8 - k])]) if k else None,
            )
            for k in range(4)
        ]
    blocks = []
    for a in range(8):
        sign = 1.0 if a % 2 == 0 else -1.0
        terms = [(1.0, sums[sign][0][0])]
        for k in range(1, 4):
            angle = 2.0 * math.pi * k * a / OUTER
            terms.append((math.cos(angle), sums[sign][k][0]))
            terms.append((-math.sin(angle), sums[sign][k][1]))
        terms.append((math.cos(math.pi * a / 2), real[4]))
        terms.append((-math.sin(math.pi * a / 2), imag[4]))
        blocks.append(weighted(terms))
    return blocks


def halves(value):
    high = value.astype(BF16)
    return high, (value - high.astype(F32)).astype(BF16)


def stacked_dot(left, right, dims=(((1,), (0,)), ((), ()))):
    return lax.dot_general(left, right, dims, preferred_element_type=F32)


def table_inputs():
    index = np.arange(INNER)
    inner = 2.0 * np.pi * (np.outer(index, index) % INNER) / INNER
    twist = 2.0 * np.pi * np.outer(np.arange(FREQS), index) / (OUTER * INNER)
    inner_tab = np.stack([np.cos(inner), np.sin(inner)]).astype(np.float32)
    row_tab = np.stack([np.cos(twist), np.sin(twist)])[:, :, None, :].astype(np.float32)
    return jnp.asarray(inner_tab), jnp.asarray(row_tab)


def make_tables(inner_ref, row_ref, forward, backward):
    lower, upper = pl.ds(0, INNER), pl.ds(INNER, INNER)

    def store(ref, k, cos, sin, flip):
        cos_parts, sin_parts = halves(cos), halves(sin)
        for place, kind in ((0, 0), (1, 0), (2, 1)):
            c, s = cos_parts[kind], sin_parts[kind]
            first = pl.ds(place * 2 * INNER, INNER)
            second = pl.ds(place * 2 * INNER + INNER, INNER)
            ref[k, lower, first] = c
            ref[k, lower, second] = -s if flip else s
            ref[k, upper, first] = s if flip else -s
            ref[k, upper, second] = c

    def step(k, carry):
        base_cos, base_sin = inner_ref[0], inner_ref[1]
        row_cos, row_sin = row_ref[0, k], row_ref[1, k]
        cos, sin = base_cos * row_cos - base_sin * row_sin, base_sin * row_cos + base_cos * row_sin
        store(forward, k, cos, sin, False)
        col_cos = jnp.broadcast_to(row_cos, (INNER, INNER)).T
        col_sin = jnp.broadcast_to(row_sin, (INNER, INNER)).T
        cos, sin = base_cos * col_cos - base_sin * col_sin, base_sin * col_cos + base_cos * col_sin
        store(backward, k, cos, sin, True)
        return carry

    lax.fori_loop(0, FREQS, step, 0)


def filter_spectrum(filter_ref, forward, work, spectrum_ref):
    channels = filter_ref.shape[1]

    def stage(block, carry):
        rows = pl.ds(pl.multiple_of(block * 16, 16), 16)
        real, imag = outer_forward([filter_ref[0, rows, pl.ds(p * INNER, INNER)] for p in range(8)])
        for k in range(FREQS):
            for place, part in ((0, real[k]), (INNER, imag[k])):
                part = jnp.zeros((16, INNER), F32) if part is None else part
                high, low = halves(part)
                work[k, rows, pl.ds(place, INNER)] = high
                work[k, rows, pl.ds(place + 2 * INNER, INNER)] = low
                work[k, rows, pl.ds(place + 4 * INNER, INNER)] = high
        return carry

    lax.fori_loop(0, channels // 16, stage, 0)

    def transform(k, carry):
        scale = jnp.where((k == 0) | (k == FREQS - 1), 0.5, 1.0) * (2.0 / (OUTER * INNER))
        spectrum_ref[k] = scale * stacked_dot(forward[k], work[k], (((1,), (1,)), ((), ())))
        return carry

    lax.fori_loop(0, FREQS, transform, 0)


WIDTH = 128


def build_picks(places, pick_ref):
    length = pick_ref.shape[0]

    def step(block, carry):
        here = lax.broadcasted_iota(jnp.int32, (128, length), 0) + block * 128
        rows = pl.ds(pl.multiple_of(block * 128, 128), 128)
        pick_ref[rows, :] = jnp.where(here == places, 1.0, 0.0).astype(BF16)
        return carry

    lax.fori_loop(0, length // 128, step, 0)


def order_rows(cols_ref, pick_ref, seq_ref, first, width):
    length = cols_ref.shape[0]

    def step(block, carry):
        rows = pl.multiple_of(block * 256, 256)
        seq_ref[pl.ds(rows + 8, 256), pl.ds(first, width)] = jnp.dot(
            pick_ref[pl.ds(rows, 256), :], cols_ref[:, pl.ds(first, width)],
            preferred_element_type=F32,
        )
        return carry

    lax.fori_loop(0, length // 256, step, 0)


def shorted_rows(seq_ref, taps_ref, start, count, place, part, here):
    window = seq_ref[pl.ds(start, count + 8), pl.ds(place * WIDTH, WIDTH)]
    total = None
    for tap in range(taps_ref.shape[0] // 3):
        weight = taps_ref[tap * 3 + part, :, here]
        term = weight * window[8 - tap : 8 + count - tap]
        total = term if total is None else total + term
    return total


def short_and_outer(seq_ref, taps_ref, work, signal_ref, here):
    def stage(block, carry):
        offset = pl.multiple_of(block * 16, 16)
        signals = []
        for p in range(8):
            rows = pl.ds(p * INNER + offset, 16)
            start = pl.multiple_of(p * INNER + block * 16, 16)
            signal = shorted_rows(seq_ref, taps_ref, start, 16, 0, 0, here) * shorted_rows(
                seq_ref, taps_ref, start, 16, 1, 2, here
            )
            signal_ref[rows, :] = signal
            signals.append(signal)
        real, imag = outer_forward(signals)
        for k in range(FREQS):
            for place, part in ((0, real[k]), (INNER, imag[k])):
                part = jnp.zeros((16, WIDTH), F32) if part is None else part
                high, low = halves(part)
                work[k, pl.ds(place + offset, 16), :] = high
                work[k, pl.ds(place + 2 * INNER + offset, 16), :] = low
                work[k, pl.ds(place + 4 * INNER + offset, 16), :] = high
        return carry

    lax.fori_loop(0, INNER // 16, stage, 0)


def transform_product(spectrum_ref, forward, backward, work, back_ref, here):
    def step(k, carry):
        value = stacked_dot(forward[k], work[k])
        real, imag = value[:INNER], value[INNER:]
        other = spectrum_ref[k, :, here]
        other_real, other_imag = other[:INNER], other[INNER:]
        product = jnp.concatenate(
            [real * other_real - imag * other_imag, real * other_imag + imag * other_real], axis=0
        )
        high, low = halves(product)
        back_ref[k] = stacked_dot(backward[k], jnp.concatenate([high, low, high], axis=0))
        return carry

    lax.fori_loop(0, FREQS, step, 0, unroll=3)


def long_and_direct(back_ref, signal_ref, skip_ref, total_ref, piece, here):
    def step(block, carry):
        offset = pl.multiple_of(block * 16, 16)
        real = [back_ref[k, pl.ds(offset, 16), :] for k in range(FREQS)]
        imag = [
            back_ref[k, pl.ds(INNER + offset, 16), :] if 0 < k < FREQS - 1 else None
            for k in range(FREQS)
        ]
        direct = skip_ref[pl.ds(0, 1), here]
        for p, long_part in enumerate(outer_backward(real, imag)):
            rows = pl.ds(p * INNER + offset, 16)
            total_ref[piece, rows, :] = long_part + direct * signal_ref[rows, :]
        return carry

    lax.fori_loop(0, INNER // 16, step, 0)


LIMIT = 56 * 2**20
MESH = pl.DeviceIdType.MESH
PARTS = (0, 2, 1)


def whole_kernel(
    devices, copies, pieces,
    features, place_ref, target_ref, domain_ref, taps_ref, filter_hbm, skip_ref,
    inner_ref, row_ref,
    mixed_ref, sums_ref,
    filter_ref, cols, places, pick_ref, wanted_ref, spectrum, forward, backward, filter_work,
    seq_ref, work, back_ref, signal_ref, total_ref, out_ref, exp_ref, hit_ref,
    given, stats, domain_sums,
    in_send, in_recv, place_send, place_recv, out_send, out_recv,
    given_send, given_recv, sum_send, sum_recv, filter_sem,
):
    me = lax.axis_index("ctx")
    copy_index = lax.axis_index("mp")
    rows_here, half_width = mixed_ref.shape
    channels = half_width // devices
    others = devices - 1
    mine = me * copies + copy_index
    far = [lax.rem(me + step, devices) for step in range(devices)]
    near = [lax.rem(copy_index + step, copies) for step in range(copies)]

    def rows_of(device):
        return pl.ds(pl.multiple_of(device * rows_here, rows_here), rows_here)

    def feature_cols(device, part, piece):
        start = part * half_width + device * channels + piece * WIDTH
        return pl.ds(pl.multiple_of(start, WIDTH), WIDTH)

    def place_cols(place):
        return pl.ds(place * WIDTH, WIDTH)

    def ctx_start(source, target, send, recv, device):
        pltpu.make_async_remote_copy(
            src_ref=source, dst_ref=target, send_sem=send, recv_sem=recv,
            device_id={"ctx": device}, device_id_type=MESH,
        ).start()

    def wait_for(ref, sem):
        pltpu.make_async_copy(ref, ref, sem).wait()

    def send(piece, kinds):
        for device in far[1:]:
            for place in kinds:
                ctx_start(
                    features.at[:, feature_cols(device, PARTS[place], piece)],
                    cols.at[piece, rows_of(me), place_cols(place)],
                    in_send, in_recv.at[piece, place], device,
                )

    def own(piece, place):
        pltpu.make_async_copy(
            features.at[:, feature_cols(me, PARTS[place], piece)],
            cols.at[piece, rows_of(me), place_cols(place)],
            in_recv.at[piece, place],
        ).start()

    def arrive(piece, kinds):
        for place in kinds:
            wait_for(cols.at[piece, :, place_cols(place)], in_recv.at[piece, place])

    barrier = pltpu.get_barrier_semaphore()
    for device in far[1:]:
        pl.semaphore_signal(barrier, inc=1, device_id={"ctx": device}, device_id_type=MESH)
    for copy in near[1:]:
        pl.semaphore_signal(barrier, inc=1, device_id={"mp": copy}, device_id_type=MESH)
    places[me] = jnp.concatenate([place_ref[...], target_ref[...]], axis=0)
    pl.semaphore_wait(barrier, devices + copies - 2)

    send(0, (0, 1))
    for device in far[1:]:
        ctx_start(places.at[me], places.at[me], place_send, place_recv, device)
    for piece in range(1, pieces):
        send(piece, (0, 1))
    for piece in range(pieces):
        send(piece, (2,))
    filter_copy = pltpu.make_async_copy(filter_hbm, filter_ref, filter_sem)
    filter_copy.start()
    for piece in range(pieces):
        for place in range(3):
            own(piece, place)

    make_tables(inner_ref, row_ref, forward, backward)
    filter_copy.wait()
    filter_spectrum(filter_ref, forward, filter_work, spectrum)
    seq_ref[pl.ds(0, 8), :] = jnp.zeros((8, seq_ref.shape[1]), F32)

    wait_for(places.at[pl.ds(0, others)], place_recv)
    build_picks(jnp.concatenate([places[d][0:1] for d in range(devices)], axis=1), pick_ref)
    base = lax.rem(copy_index, 2) * half_width + me * channels

    @pl.loop(0, devices)
    def _(device):
        loader = places[device][1:2]
        wanted_ref[rows_of(device), :] = jnp.broadcast_to(loader - base, (rows_here, rows_here)).T

    for piece in range(pieces):
        here = pl.ds(piece * WIDTH, WIDTH)
        arrive(piece, (0, 1))
        order_rows(cols.at[piece], pick_ref, seq_ref, 0, 2 * WIDTH)
        short_and_outer(seq_ref, taps_ref, work, signal_ref, here)
        transform_product(spectrum, forward, backward, work, back_ref, here)
        long_and_direct(back_ref, signal_ref, skip_ref, total_ref, piece, here)

    lane = lax.broadcasted_iota(jnp.int32, (rows_here, WIDTH), 1)
    picker = lax.broadcasted_iota(jnp.int32, (8, 4 * WIDTH), 1) < 3 * WIDTH
    picker_row = lax.broadcasted_iota(jnp.int32, (8, 4 * WIDTH), 0)
    picker = jnp.where((picker & (picker_row == 0)) | (~picker & (picker_row == 1)), 1.0, 0.0)
    picker = picker.astype(BF16)

    for piece in range(pieces):
        here = pl.ds(piece * WIDTH, WIDTH)
        arrive(piece, (2,))
        order_rows(cols.at[piece], pick_ref, seq_ref, 2 * WIDTH, WIDTH)

        def gate(owner, piece=piece, here=here):
            start = pl.multiple_of(owner * rows_here, rows_here)
            value = shorted_rows(seq_ref, taps_ref, start, rows_here, 2, 1, here)
            value = value * total_ref[piece, rows_of(owner), :]
            out_ref[piece, rows_of(owner), :] = value.astype(out_ref.dtype)

        def tally(owner, piece=piece):
            rows = rows_of(owner)
            value = out_ref[piece, rows, :].astype(F32)
            power = jnp.exp(value)
            hit = jnp.where(lane + piece * WIDTH == wanted_ref[rows, :], value, 0.0)
            if piece:
                power = power + exp_ref[rows, :]
                hit = hit + hit_ref[rows, :]
            if piece < pieces - 1:
                exp_ref[rows, :] = power
                hit_ref[rows, :] = hit
                return
            high, low = halves(power)
            rest = (power - high.astype(F32) - low.astype(F32)).astype(BF16)
            terms = jnp.concatenate([high, low, rest, hit.astype(BF16)], axis=1)
            sums = stacked_dot(picker, terms, (((1,), (1,)), ((), ())))
            given[owner] = sums[0:2]

        def give(device, piece=piece):
            start = pl.multiple_of(me * channels + piece * WIDTH, WIDTH)
            target = mixed_ref.at[:, pl.ds(start, WIDTH)]
            ctx_start(out_ref.at[piece, rows_of(device), :], target, out_send, out_recv, device)

        def keep(piece=piece):
            start = pl.multiple_of(me * channels + piece * WIDTH, WIDTH)
            target = mixed_ref.at[:, pl.ds(start, WIDTH)]
            pltpu.make_async_copy(out_ref.at[piece, rows_of(me), :], target, out_recv).start()

        def tell(device, first=0):
            for copy in near[first:]:
                pltpu.make_async_remote_copy(
                    src_ref=given.at[device], dst_ref=stats.at[mine],
                    send_sem=given_send, recv_sem=given_recv,
                    device_id={"ctx": device, "mp": copy}, device_id_type=MESH,
                ).start()

        last = piece == pieces - 1

        @pl.loop(1, devices)
        def _(step, gate=gate, give=give, tally=tally, tell=tell, last=last):
            device = lax.rem(me + step, devices)
            gate(device)
            if last:
                tally(device)
                tell(device)
            else:
                give(device)

        gate(me)
        if last:
            tally(me)
            tell(me, 1)
            for device in far[1:]:
                give(device)
            keep()
        else:
            keep()

            @pl.loop(0, devices)
            def _(device, tally=tally):
                tally(device)

    wait_for(features.at[:, pl.ds(0, 3 * channels * others)], in_send)
    wait_for(places.at[pl.ds(0, others)], place_send)
    stats[mine] = given[me]
    wait_for(stats.at[pl.ds(0, devices * copies - 1)], given_recv)
    losses = []
    for model in range(MODELS):
        both = None
        for copy in (2 * model, 2 * model + 1):
            for device in range(devices):
                term = stats[device * copies + copy]
                both = term if both is None else both + term
        losses.append(jnp.log(both[0:1]) - both[1:2])
    excess = jnp.maximum(losses[0] - losses[1], 0.0)
    kind = lax.broadcasted_iota(jnp.int32, (WIDTH, rows_here), 0)
    by_kind = jnp.where(kind == domain_ref[...], excess, 0.0)
    domain_sums[me] = jnp.sum(by_kind.T, axis=0, keepdims=True)
    for device in far[1:]:
        ctx_start(domain_sums.at[me], domain_sums.at[me], sum_send, sum_recv, device)
    wait_for(stats.at[pl.ds(0, devices * copies - 1)], given_send)
    wait_for(domain_sums.at[pl.ds(0, others)], sum_recv)
    sums = domain_sums[0]
    for device in range(1, devices):
        sums = sums + domain_sums[device]
    sums_ref[...] = sums[:, : sums_ref.shape[1]]
    wait_for(mixed_ref, out_recv)
    wait_for(domain_sums.at[pl.ds(0, others)], sum_send)
    wait_for(out_ref.at[:, pl.ds(0, rows_here * others), :], out_send)


def body(features, destination, targets, domains, domain_tokens, short_filter, long_filter, skip):
    devices = lax.axis_size("ctx")
    copies = lax.axis_size("mp")
    rows_here = features.shape[0]
    length = devices * rows_here
    half_width = features.shape[1] // 3
    channels = half_width // devices
    if length != 8 * INNER or rows_here != 128 or channels != 256 or copies != 4 or domain_tokens.shape[0] > WIDTH:
        return general_body(
            features, destination, targets, domains, domain_tokens, short_filter, long_filter, skip
        )
    pieces = channels // WIDTH
    count = domain_tokens.shape[0]
    vmem = pl.BlockSpec(memory_space=pltpu.VMEM)
    hbm = pl.BlockSpec(memory_space=pl.ANY)
    big = (FREQS, 2 * INNER, 6 * INNER)
    dma = pltpu.SemaphoreType.DMA
    mixed, sums = pl.pallas_call(
        functools.partial(whole_kernel, devices, copies, pieces),
        out_shape=[
            pltpu.VMEM((rows_here, half_width), BF16),
            pltpu.VMEM((1, count), F32),
        ],
        in_specs=[hbm, vmem, vmem, vmem, vmem, hbm, vmem, vmem, vmem],
        out_specs=[vmem, vmem],
        scratch_shapes=[
            pltpu.VMEM((1, channels, length), F32),
            pltpu.VMEM((pieces, length, 3 * WIDTH), BF16),
            pltpu.VMEM((devices, 2, rows_here), jnp.int32),
            pltpu.VMEM((length, length), BF16),
            pltpu.VMEM((length, WIDTH), jnp.int32),
            pltpu.VMEM((FREQS, 2 * INNER, channels), F32),
            pltpu.VMEM(big, BF16),
            pltpu.VMEM(big, BF16),
            pltpu.VMEM((FREQS, channels, 6 * INNER), BF16),
            pltpu.VMEM((length + 8, 3 * WIDTH), F32),
            pltpu.VMEM((FREQS, 6 * INNER, WIDTH), BF16),
            pltpu.VMEM((FREQS, 2 * INNER, WIDTH), F32),
            pltpu.VMEM((length, WIDTH), F32),
            pltpu.VMEM((pieces, length, WIDTH), F32),
            pltpu.VMEM((pieces, length, WIDTH), BF16),
            pltpu.VMEM((length, WIDTH), F32),
            pltpu.VMEM((length, WIDTH), F32),
            pltpu.VMEM((devices, 2, rows_here), F32),
            pltpu.VMEM((devices * copies, 2, rows_here), F32),
            pltpu.VMEM((devices, 1, WIDTH), F32),
            dma,
            dma((pieces, 3)),
            dma,
            dma,
            dma,
            dma,
            dma,
            dma,
            dma,
            dma,
            dma,
        ],
        compiler_params=pltpu.CompilerParams(
            vmem_limit_bytes=LIMIT, collective_id=0, has_side_effects=True
        ),
    )(
        features, destination.reshape(1, rows_here), targets.reshape(1, rows_here),
        domains.reshape(1, rows_here),
        short_filter.transpose(0, 2, 1, 3).reshape(-1, 1, channels), long_filter, skip,
        *table_inputs(),
    )
    return (mixed, sums.reshape(count) / domain_tokens.astype(F32))


def solution(mesh):
    return jax.shard_map(
        body,
        mesh=mesh,
        in_specs=(
            P("ctx", "mp"),
            P("ctx"),
            P("ctx"),
            P("ctx"),
            P(),
            P(None, "mp", None, "ctx"),
            P("mp", "ctx", None),
            P("mp", "ctx"),
        ),
        out_specs=(P("ctx", "mp"), P()),
        check_vma=False,
    )
```

```python
import functools
import math

import jax
import jax.numpy as jnp
import numpy as np
from jax import lax
from jax.experimental import pallas as pl
from jax.experimental.pallas import tpu as pltpu
from jax.sharding import PartitionSpec as P

MODELS = 2


HIGHEST = lax.Precision.HIGHEST


def dft_tables(count, limit, modulus):
    row_index = jnp.arange(count, dtype=jnp.int32)[:, None]
    col_index = jnp.arange(limit, dtype=jnp.int32)[None, :]
    angle = 2.0 * math.pi / modulus * (row_index * col_index % modulus).astype(jnp.float32)
    return (jnp.cos(angle), jnp.sin(angle))


def forward_transform(signal, outer_cos, outer_sin, twist_cos, twist_sin, inner_cos, inner_sin):
    real_a = jnp.einsum("kp,cpq->ckq", outer_cos, signal, precision=HIGHEST)
    imag_a = -jnp.einsum("kp,cpq->ckq", outer_sin, signal, precision=HIGHEST)
    real_b = real_a * twist_cos + imag_a * twist_sin
    imag_b = imag_a * twist_cos - real_a * twist_sin
    real_c = jnp.einsum("ckq,qj->ckj", real_b, inner_cos, precision=HIGHEST) + jnp.einsum(
        "ckq,qj->ckj", imag_b, inner_sin, precision=HIGHEST
    )
    imag_c = jnp.einsum("ckq,qj->ckj", imag_b, inner_cos, precision=HIGHEST) - jnp.einsum(
        "ckq,qj->ckj", real_b, inner_sin, precision=HIGHEST
    )
    return (real_c, imag_c)


def causal_convolution(signal, kernel):
    channels, length = signal.shape
    inner_size = 128
    outer_size = 2 * length // inner_size
    half_outer = outer_size // 2
    outer_cos, outer_sin = dft_tables(outer_size, half_outer, outer_size)
    twist_cos, twist_sin = dft_tables(outer_size, inner_size, 2 * length)
    inner_cos, inner_sin = dft_tables(inner_size, inner_size, inner_size)
    sig_re, sig_im = forward_transform(
        signal.reshape(channels, half_outer, inner_size),
        outer_cos,
        outer_sin,
        twist_cos,
        twist_sin,
        inner_cos,
        inner_sin,
    )
    ker_re, ker_im = forward_transform(
        kernel.reshape(channels, half_outer, inner_size),
        outer_cos,
        outer_sin,
        twist_cos,
        twist_sin,
        inner_cos,
        inner_sin,
    )
    prod_re = sig_re * ker_re - sig_im * ker_im
    prod_im = sig_re * ker_im + sig_im * ker_re
    back_re = jnp.einsum("ckj,qj->ckq", prod_re, inner_cos, precision=HIGHEST) - jnp.einsum(
        "ckj,qj->ckq", prod_im, inner_sin, precision=HIGHEST
    )
    back_im = jnp.einsum("ckj,qj->ckq", prod_im, inner_cos, precision=HIGHEST) + jnp.einsum(
        "ckj,qj->ckq", prod_re, inner_sin, precision=HIGHEST
    )
    turned_re = back_re * twist_cos - back_im * twist_sin
    turned_im = back_im * twist_cos + back_re * twist_sin
    result = jnp.einsum("kp,ckq->cpq", outer_cos, turned_re, precision=HIGHEST) - jnp.einsum(
        "kp,ckq->cpq", outer_sin, turned_im, precision=HIGHEST
    )
    return (result / (2.0 * length)).reshape(channels, length)


def general_body(features, destination, targets, domains, domain_tokens, short_filter, long_filter, skip):
    devices = lax.axis_size("ctx")
    rows_here = features.shape[0]
    length = devices * rows_here
    half_width = features.shape[1] // 3
    channels = half_width // devices
    capacity = 5 * rows_here // (2 * devices)
    owner_dev = destination // rows_here
    offset = destination % rows_here
    order = jnp.arange(rows_here, dtype=jnp.int32)
    ahead = (owner_dev[:, None] == owner_dev[None, :]) & (order[None, :] < order[:, None])
    slot_rank = jnp.sum(ahead.astype(jnp.int32), axis=1)
    buffer = (
        jnp.zeros((devices, capacity, 3 * half_width), features.dtype)
        .at[owner_dev, slot_rank]
        .set(features)
    )
    places = (
        jnp.full((devices, capacity), rows_here, jnp.int32).at[owner_dev, slot_rank].set(offset)
    )
    arrived, arrived_places = (
        lax.all_to_all(buffer, "ctx", split_axis=0, concat_axis=0, tiled=True),
        lax.all_to_all(places, "ctx", split_axis=0, concat_axis=0, tiled=True),
    )
    ordered = jnp.zeros((rows_here + 1, 3 * half_width), features.dtype)
    ordered = ordered.at[arrived_places.reshape(-1)].set(arrived.reshape(-1, 3 * half_width))[
        :rows_here
    ]
    blocks = ordered.reshape(rows_here, 3, devices, channels).transpose(2, 1, 3, 0)
    columns = lax.all_to_all(blocks, "ctx", split_axis=0, concat_axis=3, tiled=True)[0]
    inputs = columns.astype(jnp.float32)
    tap_weights = short_filter[:, 0]
    shorted = jnp.zeros_like(inputs)
    for tap_index in range(tap_weights.shape[0]):
        shifted = jnp.pad(inputs, ((0, 0), (0, 0), (tap_index, 0)))[:, :, :length]
        shorted = shorted + tap_weights[tap_index][:, :, None] * shifted
    signal = shorted[0] * shorted[2]
    long_part = causal_convolution(signal, long_filter[0])
    output_cols = (shorted[1] * (long_part + skip[0][:, None] * signal)).astype(jnp.bfloat16)
    returned = lax.all_to_all(
        output_cols.reshape(channels, devices, rows_here),
        "ctx",
        split_axis=1,
        concat_axis=0,
        tiled=True,
    )
    mixed = returned.reshape(half_width, rows_here).T
    copy_index = lax.axis_index("mp")
    model_index = copy_index // 2
    half_index = copy_index % 2
    values = mixed.astype(jnp.float32)
    part_exp = jnp.sum(jnp.exp(values), axis=1)
    local_target = targets - half_index * half_width
    inside = (local_target >= 0) & (local_target < half_width)
    picked = jnp.take_along_axis(
        values, jnp.clip(local_target, 0, half_width - 1)[:, None], axis=1
    )[:, 0]
    part_target = jnp.where(inside, picked, 0.0)
    is_model = jnp.arange(MODELS, dtype=jnp.int32)[:, None] == model_index
    exp_terms = jnp.where(is_model, part_exp[None, :], 0.0)
    target_terms = jnp.where(is_model, part_target[None, :], 0.0)
    total_exp, total_target = lax.psum((exp_terms, target_terms), "mp")
    losses = jnp.log(total_exp) - total_target
    token_excess = jnp.maximum(losses[0] - losses[1], 0.0)
    domain_count = domain_tokens.shape[0]
    in_domain = domains[None, :] == jnp.arange(domain_count, dtype=jnp.int32)[:, None]
    partial_sums = jnp.sum(jnp.where(in_domain, token_excess[None, :], 0.0), axis=1)
    domain_sums = lax.psum(partial_sums, "ctx")
    return (mixed, domain_sums / domain_tokens.astype(jnp.float32))


INNER = 128
OUTER = 16
FREQS = OUTER // 2 + 1
BF16 = jnp.bfloat16
F32 = jnp.float32


def weighted(terms):
    total = None
    for coef, value in terms:
        if value is None or abs(coef) < 1e-9:
            continue
        if abs(abs(coef) - 1.0) < 1e-9:
            term = value
            if coef < 0:
                total = -term if total is None else total - term
                continue
        else:
            term = coef * value
        total = term if total is None else total + term
    return total


def outer_forward(blocks):
    real, imag = [None] * FREQS, [None] * FREQS
    for k in range(FREQS // 2 + 1):
        angle = [2.0 * math.pi * p * k / OUTER for p in range(8)]
        parts = []
        for first in (0, 1):
            picks = range(first, 8, 2)
            parts.append(weighted([(math.cos(angle[p]), blocks[p]) for p in picks]))
            parts.append(weighted([(-math.sin(angle[p]), blocks[p]) for p in picks]))
        real_even, imag_even, real_odd, imag_odd = parts
        real[k] = weighted([(1.0, real_even), (1.0, real_odd)])
        imag[k] = weighted([(1.0, imag_even), (1.0, imag_odd)])
        if k < 4:
            real[8 - k] = weighted([(1.0, real_even), (-1.0, real_odd)])
            imag[8 - k] = weighted([(-1.0, imag_even), (1.0, imag_odd)])
    return real, imag


def outer_backward(real, imag):
    sums = {}
    for sign in (1.0, -1.0):
        sums[sign] = [
            (
                weighted([(1.0, real[k]), (sign, real[8 - k])]),
                weighted([(1.0, imag[k]), (-sign, imag[8 - k])]) if k else None,
            )
            for k in range(4)
        ]
    blocks = []
    for a in range(8):
        sign = 1.0 if a % 2 == 0 else -1.0
        terms = [(1.0, sums[sign][0][0])]
        for k in range(1, 4):
            angle = 2.0 * math.pi * k * a / OUTER
            terms.append((math.cos(angle), sums[sign][k][0]))
            terms.append((-math.sin(angle), sums[sign][k][1]))
        terms.append((math.cos(math.pi * a / 2), real[4]))
        terms.append((-math.sin(math.pi * a / 2), imag[4]))
        blocks.append(weighted(terms))
    return blocks


def halves(value):
    high = value.astype(BF16)
    return high, (value - high.astype(F32)).astype(BF16)


def stacked_dot(left, right, dims=(((1,), (0,)), ((), ()))):
    return lax.dot_general(left, right, dims, preferred_element_type=F32)


def table_inputs():
    index = np.arange(INNER)
    inner = 2.0 * np.pi * (np.outer(index, index) % INNER) / INNER
    twist = 2.0 * np.pi * np.outer(np.arange(FREQS), index) / (OUTER * INNER)
    inner_tab = np.stack([np.cos(inner), np.sin(inner)]).astype(np.float32)
    row_tab = np.stack([np.cos(twist), np.sin(twist)])[:, :, None, :].astype(np.float32)
    return jnp.asarray(inner_tab), jnp.asarray(row_tab)


def make_tables(inner_ref, row_ref, forward, backward):
    lower, upper = pl.ds(0, INNER), pl.ds(INNER, INNER)

    def store(ref, k, cos, sin, flip):
        cos_parts, sin_parts = halves(cos), halves(sin)
        for place, kind in ((0, 0), (1, 0), (2, 1)):
            c, s = cos_parts[kind], sin_parts[kind]
            first = pl.ds(place * 2 * INNER, INNER)
            second = pl.ds(place * 2 * INNER + INNER, INNER)
            ref[k, lower, first] = c
            ref[k, lower, second] = -s if flip else s
            ref[k, upper, first] = s if flip else -s
            ref[k, upper, second] = c

    def step(k, carry):
        base_cos, base_sin = inner_ref[0], inner_ref[1]
        row_cos, row_sin = row_ref[0, k], row_ref[1, k]
        cos, sin = base_cos * row_cos - base_sin * row_sin, base_sin * row_cos + base_cos * row_sin
        store(forward, k, cos, sin, False)
        col_cos = jnp.broadcast_to(row_cos, (INNER, INNER)).T
        col_sin = jnp.broadcast_to(row_sin, (INNER, INNER)).T
        cos, sin = base_cos * col_cos - base_sin * col_sin, base_sin * col_cos + base_cos * col_sin
        store(backward, k, cos, sin, True)
        return carry

    lax.fori_loop(0, FREQS, step, 0)


def filter_spectrum(filter_ref, forward, work, spectrum_ref):
    channels = filter_ref.shape[1]

    def stage(block, carry):
        rows = pl.ds(pl.multiple_of(block * 16, 16), 16)
        real, imag = outer_forward([filter_ref[0, rows, pl.ds(p * INNER, INNER)] for p in range(8)])
        for k in range(FREQS):
            for place, part in ((0, real[k]), (INNER, imag[k])):
                part = jnp.zeros((16, INNER), F32) if part is None else part
                high, low = halves(part)
                work[k, rows, pl.ds(place, INNER)] = high
                work[k, rows, pl.ds(place + 2 * INNER, INNER)] = low
                work[k, rows, pl.ds(place + 4 * INNER, INNER)] = high
        return carry

    lax.fori_loop(0, channels // 16, stage, 0)

    def transform(k, carry):
        scale = jnp.where((k == 0) | (k == FREQS - 1), 0.5, 1.0) * (2.0 / (OUTER * INNER))
        spectrum_ref[k] = scale * stacked_dot(forward[k], work[k], (((1,), (1,)), ((), ())))
        return carry

    lax.fori_loop(0, FREQS, transform, 0)


WIDTH = 128


def build_picks(places, pick_ref):
    length = pick_ref.shape[0]

    def step(block, carry):
        here = lax.broadcasted_iota(jnp.int32, (128, length), 0) + block * 128
        rows = pl.ds(pl.multiple_of(block * 128, 128), 128)
        pick_ref[rows, :] = jnp.where(here == places, 1.0, 0.0).astype(BF16)
        return carry

    lax.fori_loop(0, length // 128, step, 0)


def order_rows(cols_ref, pick_ref, seq_ref, first, width):
    length = cols_ref.shape[0]

    def step(block, carry):
        rows = pl.multiple_of(block * 256, 256)
        seq_ref[pl.ds(rows + 8, 256), pl.ds(first, width)] = jnp.dot(
            pick_ref[pl.ds(rows, 256), :], cols_ref[:, pl.ds(first, width)],
            preferred_element_type=F32,
        )
        return carry

    lax.fori_loop(0, length // 256, step, 0)


def shorted_rows(seq_ref, taps_ref, start, count, place, part, here):
    window = seq_ref[pl.ds(start, count + 8), pl.ds(place * WIDTH, WIDTH)]
    total = None
    for tap in range(taps_ref.shape[0] // 3):
        weight = taps_ref[tap * 3 + part, :, here]
        term = weight * window[8 - tap : 8 + count - tap]
        total = term if total is None else total + term
    return total


def short_and_outer(seq_ref, taps_ref, work, signal_ref, here):
    def stage(block, carry):
        offset = pl.multiple_of(block * 16, 16)
        signals = []
        for p in range(8):
            rows = pl.ds(p * INNER + offset, 16)
            start = pl.multiple_of(p * INNER + block * 16, 16)
            signal = shorted_rows(seq_ref, taps_ref, start, 16, 0, 0, here) * shorted_rows(
                seq_ref, taps_ref, start, 16, 1, 2, here
            )
            signal_ref[rows, :] = signal
            signals.append(signal)
        real, imag = outer_forward(signals)
        for k in range(FREQS):
            for place, part in ((0, real[k]), (INNER, imag[k])):
                part = jnp.zeros((16, WIDTH), F32) if part is None else part
                high, low = halves(part)
                work[k, pl.ds(place + offset, 16), :] = high
                work[k, pl.ds(place + 2 * INNER + offset, 16), :] = low
                work[k, pl.ds(place + 4 * INNER + offset, 16), :] = high
        return carry

    lax.fori_loop(0, INNER // 16, stage, 0)


def transform_product(spectrum_ref, forward, backward, work, back_ref, here):
    def step(k, carry):
        value = stacked_dot(forward[k], work[k])
        real, imag = value[:INNER], value[INNER:]
        other = spectrum_ref[k, :, here]
        other_real, other_imag = other[:INNER], other[INNER:]
        product = jnp.concatenate(
            [real * other_real - imag * other_imag, real * other_imag + imag * other_real], axis=0
        )
        high, low = halves(product)
        back_ref[k] = stacked_dot(backward[k], jnp.concatenate([high, low, high], axis=0))
        return carry

    lax.fori_loop(0, FREQS, step, 0, unroll=3)


def long_and_direct(back_ref, signal_ref, skip_ref, total_ref, piece, here):
    def step(block, carry):
        offset = pl.multiple_of(block * 16, 16)
        real = [back_ref[k, pl.ds(offset, 16), :] for k in range(FREQS)]
        imag = [
            back_ref[k, pl.ds(INNER + offset, 16), :] if 0 < k < FREQS - 1 else None
            for k in range(FREQS)
        ]
        direct = skip_ref[pl.ds(0, 1), here]
        for p, long_part in enumerate(outer_backward(real, imag)):
            rows = pl.ds(p * INNER + offset, 16)
            total_ref[piece, rows, :] = long_part + direct * signal_ref[rows, :]
        return carry

    lax.fori_loop(0, INNER // 16, step, 0)


LIMIT = 56 * 2**20
MESH = pl.DeviceIdType.MESH
PARTS = (0, 2, 1)


def whole_kernel(
    devices, copies, pieces,
    features, place_ref, target_ref, domain_ref, taps_ref, filter_hbm, skip_ref,
    inner_ref, row_ref,
    mixed_ref, sums_ref,
    filter_ref, cols, places, pick_ref, wanted_ref, spectrum, forward, backward, filter_work,
    seq_ref, work, back_ref, signal_ref, total_ref, out_ref, exp_ref, hit_ref,
    terms_ref, half_out, half_in, gathered, domain_hot, domain_sums,
    in_send, in_recv, place_send, place_recv, out_send, out_recv,
    given_send, given_recv, half_send, half_recv, sum_send, sum_recv, filter_sem,
):
    me = lax.axis_index("ctx")
    copy_index = lax.axis_index("mp")
    rows_here, half_width = mixed_ref.shape
    channels = half_width // devices
    others = devices - 1
    core = lax.rem(copy_index, 2)
    model_index = copy_index // 2
    partner = copy_index + 1 - 2 * core
    span = rows_here * devices // 2
    far = [lax.rem(me + step, devices) for step in range(devices)]
    near = [lax.rem(copy_index + step, copies) for step in range(copies)]

    def rows_of(device):
        return pl.ds(pl.multiple_of(device * rows_here, rows_here), rows_here)

    def feature_cols(device, part, piece):
        start = part * half_width + device * channels + piece * WIDTH
        return pl.ds(pl.multiple_of(start, WIDTH), WIDTH)

    def place_cols(place):
        return pl.ds(place * WIDTH, WIDTH)

    def ctx_start(source, target, send, recv, device):
        pltpu.make_async_remote_copy(
            src_ref=source, dst_ref=target, send_sem=send, recv_sem=recv,
            device_id={"ctx": device}, device_id_type=MESH,
        ).start()

    def wait_for(ref, sem):
        pltpu.make_async_copy(ref, ref, sem).wait()

    def send(piece, kinds):
        for device in far[1:]:
            for place in kinds:
                ctx_start(
                    features.at[:, feature_cols(device, PARTS[place], piece)],
                    cols.at[piece, rows_of(me), place_cols(place)],
                    in_send, in_recv.at[piece, place], device,
                )

    def own(piece, place):
        pltpu.make_async_copy(
            features.at[:, feature_cols(me, PARTS[place], piece)],
            cols.at[piece, rows_of(me), place_cols(place)],
            in_recv.at[piece, place],
        ).start()

    def arrive(piece, kinds):
        for place in kinds:
            wait_for(cols.at[piece, :, place_cols(place)], in_recv.at[piece, place])

    barrier = pltpu.get_barrier_semaphore()
    for device in far[1:]:
        pl.semaphore_signal(barrier, inc=1, device_id={"ctx": device}, device_id_type=MESH)
    for copy in near[1:]:
        pl.semaphore_signal(barrier, inc=1, device_id={"mp": copy}, device_id_type=MESH)
    places[me] = jnp.concatenate([place_ref[...], target_ref[...], domain_ref[...]], axis=0)
    pl.semaphore_wait(barrier, devices + copies - 2)

    send(0, (0, 1))
    for device in far[1:]:
        ctx_start(places.at[me], places.at[me], place_send, place_recv, device)
    for piece in range(1, pieces):
        send(piece, (0, 1))
    for piece in range(pieces):
        send(piece, (2,))
    filter_copy = pltpu.make_async_copy(filter_hbm, filter_ref, filter_sem)
    filter_copy.start()
    for piece in range(pieces):
        for place in range(3):
            own(piece, place)

    make_tables(inner_ref, row_ref, forward, backward)
    filter_copy.wait()
    filter_spectrum(filter_ref, forward, filter_work, spectrum)
    seq_ref[pl.ds(0, 8), :] = jnp.zeros((8, seq_ref.shape[1]), F32)

    wait_for(places.at[pl.ds(0, others)], place_recv)
    build_picks(jnp.concatenate([places[d][0:1] for d in range(devices)], axis=1), pick_ref)
    base = core * half_width + me * channels

    @pl.loop(0, devices // 2)
    def _(step):
        kinds = lax.broadcasted_iota(jnp.int32, (WIDTH, rows_here), 0)
        match = kinds == places[core * (devices // 2) + step][2:3]
        domain_hot[:, rows_of(step)] = jnp.where(match, 1.0, 0.0).astype(BF16)

    @pl.loop(0, devices)
    def _(device):
        loader = places[device][1:2]
        wanted_ref[rows_of(device), :] = jnp.broadcast_to(loader - base, (rows_here, rows_here)).T

    for piece in range(pieces):
        here = pl.ds(piece * WIDTH, WIDTH)
        arrive(piece, (0, 1))
        order_rows(cols.at[piece], pick_ref, seq_ref, 0, 2 * WIDTH)
        short_and_outer(seq_ref, taps_ref, work, signal_ref, here)
        transform_product(spectrum, forward, backward, work, back_ref, here)
        long_and_direct(back_ref, signal_ref, skip_ref, total_ref, piece, here)

    lane = lax.broadcasted_iota(jnp.int32, (rows_here, WIDTH), 1)
    picker_col = lax.broadcasted_iota(jnp.int32, (8, 3 * WIDTH), 1) < 2 * WIDTH
    picker_row = lax.broadcasted_iota(jnp.int32, (8, 3 * WIDTH), 0)
    picker = (picker_col & (picker_row == 0)) | (~picker_col & (picker_row == 1))
    picker = jnp.where(picker, 1.0, 0.0).astype(BF16)

    def gate(piece, owner):
        here = pl.ds(piece * WIDTH, WIDTH)
        start = pl.multiple_of(owner * rows_here, rows_here)
        value = shorted_rows(seq_ref, taps_ref, start, rows_here, 2, 1, here)
        value = (value * total_ref[piece, rows_of(owner), :]).astype(out_ref.dtype)
        out_ref[piece, rows_of(owner), :] = value
        return value.astype(F32)

    def tally(piece, owner, value):
        rows = rows_of(owner)
        power = jnp.exp(value)
        hit = jnp.where(lane + piece * WIDTH == wanted_ref[rows, :], value, 0.0)
        if piece:
            power = power + exp_ref[rows, :]
            hit = hit + hit_ref[rows, :]
        if piece < pieces - 1:
            exp_ref[rows, :] = power
            hit_ref[rows, :] = hit
            return
        high, low = halves(power)
        terms_ref[rows, pl.ds(0, WIDTH)] = high
        terms_ref[rows, pl.ds(WIDTH, WIDTH)] = low
        terms_ref[rows, pl.ds(2 * WIDTH, WIDTH)] = hit.astype(BF16)

    def mixed_part(piece):
        start = pl.multiple_of(me * channels + piece * WIDTH, WIDTH)
        return mixed_ref.at[:, pl.ds(start, WIDTH)]

    def give(piece, device):
        ctx_start(
            out_ref.at[piece, rows_of(device), :], mixed_part(piece), out_send, out_recv, device
        )

    def keep(piece):
        pltpu.make_async_copy(out_ref.at[piece, rows_of(me), :], mixed_part(piece), out_recv).start()

    for piece in range(pieces - 1):
        arrive(piece, (2,))
        order_rows(cols.at[piece], pick_ref, seq_ref, 2 * WIDTH, WIDTH)

        @pl.loop(1, devices)
        def _(step, piece=piece):
            device = lax.rem(me + step, devices)
            gate(piece, device)
            give(piece, device)

        gate(piece, me)
        keep(piece)

        @pl.loop(0, devices)
        def _(device, piece=piece):
            tally(piece, device, out_ref[piece, rows_of(device), :].astype(F32))

    piece = pieces - 1
    arrive(piece, (2,))
    order_rows(cols.at[piece], pick_ref, seq_ref, 2 * WIDTH, WIDTH)

    def half_sums(half):
        @pl.loop(0, devices // 2)
        def _(step):
            owner = half * (devices // 2) + step
            tally(piece, owner, gate(piece, owner))

        rows = pl.ds(pl.multiple_of(half * span, span), span)
        return stacked_dot(picker, terms_ref[rows, :], (((1,), (1,)), ((), ())))[0:2]

    def core_copy(source, target, send, recv):
        return pltpu.make_async_remote_copy(
            src_ref=source, dst_ref=target, send_sem=send, recv_sem=recv,
            device_id={"mp": partner}, device_id_type=MESH,
        )

    half_out[...] = half_sums(1 - core)
    half_copy = core_copy(half_out, half_in, half_send, half_recv)
    half_copy.start()
    half_own = half_sums(core)
    half_copy.wait_recv()
    half_theirs = half_in[...]
    chip = me * MODELS + model_index
    gathered[chip] = half_own + half_theirs
    for step in range(devices):
        for other in range(MODELS):
            if step or other:
                pltpu.make_async_remote_copy(
                    src_ref=gathered.at[chip], dst_ref=gathered.at[chip],
                    send_sem=given_send, recv_sem=given_recv,
                    device_id={"ctx": far[step], "mp": near[2 * other]}, device_id_type=MESH,
                ).start()
    for device in far[1:]:
        give(piece, device)
    keep(piece)

    wait_for(features.at[:, pl.ds(0, 3 * channels * others)], in_send)
    wait_for(places.at[pl.ds(0, others)], place_send)
    half_copy.wait_send()
    wait_for(gathered.at[pl.ds(0, MODELS * devices - 1)], given_recv)
    losses = []
    for model in range(MODELS):
        both = gathered[model]
        for device in range(1, devices):
            both = both + gathered[device * MODELS + model]
        losses.append(jnp.log(both[0:1]) - both[1:2])
    excess = jnp.broadcast_to(jnp.maximum(losses[0] - losses[1], 0.0), (8, span))
    high, low = halves(excess)
    top = lax.broadcasted_iota(jnp.int32, (8, span), 0)
    excess = jnp.where(top == 0, high.astype(F32), jnp.where(top == 1, low.astype(F32), 0.0))
    sums = stacked_dot(excess.astype(BF16), domain_hot[...], (((1,), (1,)), ((), ())))
    domain_sums[core] = sums[0:1] + sums[1:2]
    sum_copy = core_copy(domain_sums.at[core], domain_sums.at[core], sum_send, sum_recv)
    sum_copy.start()
    wait_for(gathered.at[pl.ds(0, MODELS * devices - 1)], given_send)
    sum_copy.wait()
    sums = domain_sums[0] + domain_sums[1]
    sums_ref[...] = sums[:, : sums_ref.shape[1]]
    wait_for(mixed_ref, out_recv)
    wait_for(out_ref.at[:, pl.ds(0, rows_here * others), :], out_send)


def body(features, destination, targets, domains, domain_tokens, short_filter, long_filter, skip):
    devices = lax.axis_size("ctx")
    copies = lax.axis_size("mp")
    rows_here = features.shape[0]
    length = devices * rows_here
    half_width = features.shape[1] // 3
    channels = half_width // devices
    if length != 8 * INNER or rows_here != 128 or channels != 256 or copies != 4 or domain_tokens.shape[0] > WIDTH:
        return general_body(
            features, destination, targets, domains, domain_tokens, short_filter, long_filter, skip
        )
    pieces = channels // WIDTH
    count = domain_tokens.shape[0]
    vmem = pl.BlockSpec(memory_space=pltpu.VMEM)
    hbm = pl.BlockSpec(memory_space=pl.ANY)
    big = (FREQS, 2 * INNER, 6 * INNER)
    dma = pltpu.SemaphoreType.DMA
    mixed, sums = pl.pallas_call(
        functools.partial(whole_kernel, devices, copies, pieces),
        out_shape=[
            pltpu.VMEM((rows_here, half_width), BF16),
            pltpu.VMEM((1, count), F32),
        ],
        in_specs=[hbm, vmem, vmem, vmem, vmem, hbm, vmem, vmem, vmem],
        out_specs=[vmem, vmem],
        scratch_shapes=[
            pltpu.VMEM((1, channels, length), F32),
            pltpu.VMEM((pieces, length, 3 * WIDTH), BF16),
            pltpu.VMEM((devices, 3, rows_here), jnp.int32),
            pltpu.VMEM((length, length), BF16),
            pltpu.VMEM((length, WIDTH), jnp.int32),
            pltpu.VMEM((FREQS, 2 * INNER, channels), F32),
            pltpu.VMEM(big, BF16),
            pltpu.VMEM(big, BF16),
            pltpu.VMEM((FREQS, channels, 6 * INNER), BF16),
            pltpu.VMEM((length + 8, 3 * WIDTH), F32),
            pltpu.VMEM((FREQS, 6 * INNER, WIDTH), BF16),
            pltpu.VMEM((FREQS, 2 * INNER, WIDTH), F32),
            pltpu.VMEM((length, WIDTH), F32),
            pltpu.VMEM((pieces, length, WIDTH), F32),
            pltpu.VMEM((pieces, length, WIDTH), BF16),
            pltpu.VMEM((length, WIDTH), F32),
            pltpu.VMEM((length, WIDTH), F32),
            pltpu.VMEM((length, 3 * WIDTH), BF16),
            pltpu.VMEM((2, length // 2), F32),
            pltpu.VMEM((2, length // 2), F32),
            pltpu.VMEM((MODELS * devices, 2, length // 2), F32),
            pltpu.VMEM((WIDTH, length // 2), BF16),
            pltpu.VMEM((2, 1, WIDTH), F32),
            dma,
            dma((pieces, 3)),
            dma,
            dma,
            dma,
            dma,
            dma,
            dma,
            dma,
            dma,
            dma,
            dma,
            dma,
        ],
        compiler_params=pltpu.CompilerParams(
            vmem_limit_bytes=LIMIT, collective_id=0, has_side_effects=True
        ),
    )(
        features, destination.reshape(1, rows_here), targets.reshape(1, rows_here),
        domains.reshape(1, rows_here),
        short_filter.transpose(0, 2, 1, 3).reshape(-1, 1, channels), long_filter, skip,
        *table_inputs(),
    )
    return (mixed, sums.reshape(count) / domain_tokens.astype(F32))


def solution(mesh):
    return jax.shard_map(
        body,
        mesh=mesh,
        in_specs=(
            P("ctx", "mp"),
            P("ctx"),
            P("ctx"),
            P("ctx"),
            P(),
            P(None, "mp", None, "ctx"),
            P("mp", "ctx", None),
            P("mp", "ctx"),
        ),
        out_specs=(P("ctx", "mp"), P()),
        check_vma=False,
    )
```

```python
import functools
import math

import jax
import jax.numpy as jnp
import numpy as np
from jax import lax
from jax.experimental import pallas as pl
from jax.experimental.pallas import tpu as pltpu
from jax.sharding import PartitionSpec as P

MODELS = 2


HIGHEST = lax.Precision.HIGHEST


def dft_tables(count, limit, modulus):
    row_index = jnp.arange(count, dtype=jnp.int32)[:, None]
    col_index = jnp.arange(limit, dtype=jnp.int32)[None, :]
    angle = 2.0 * math.pi / modulus * (row_index * col_index % modulus).astype(jnp.float32)
    return (jnp.cos(angle), jnp.sin(angle))


def forward_transform(signal, outer_cos, outer_sin, twist_cos, twist_sin, inner_cos, inner_sin):
    real_a = jnp.einsum("kp,cpq->ckq", outer_cos, signal, precision=HIGHEST)
    imag_a = -jnp.einsum("kp,cpq->ckq", outer_sin, signal, precision=HIGHEST)
    real_b = real_a * twist_cos + imag_a * twist_sin
    imag_b = imag_a * twist_cos - real_a * twist_sin
    real_c = jnp.einsum("ckq,qj->ckj", real_b, inner_cos, precision=HIGHEST) + jnp.einsum(
        "ckq,qj->ckj", imag_b, inner_sin, precision=HIGHEST
    )
    imag_c = jnp.einsum("ckq,qj->ckj", imag_b, inner_cos, precision=HIGHEST) - jnp.einsum(
        "ckq,qj->ckj", real_b, inner_sin, precision=HIGHEST
    )
    return (real_c, imag_c)


def causal_convolution(signal, kernel):
    channels, length = signal.shape
    inner_size = 128
    outer_size = 2 * length // inner_size
    half_outer = outer_size // 2
    outer_cos, outer_sin = dft_tables(outer_size, half_outer, outer_size)
    twist_cos, twist_sin = dft_tables(outer_size, inner_size, 2 * length)
    inner_cos, inner_sin = dft_tables(inner_size, inner_size, inner_size)
    sig_re, sig_im = forward_transform(
        signal.reshape(channels, half_outer, inner_size),
        outer_cos,
        outer_sin,
        twist_cos,
        twist_sin,
        inner_cos,
        inner_sin,
    )
    ker_re, ker_im = forward_transform(
        kernel.reshape(channels, half_outer, inner_size),
        outer_cos,
        outer_sin,
        twist_cos,
        twist_sin,
        inner_cos,
        inner_sin,
    )
    prod_re = sig_re * ker_re - sig_im * ker_im
    prod_im = sig_re * ker_im + sig_im * ker_re
    back_re = jnp.einsum("ckj,qj->ckq", prod_re, inner_cos, precision=HIGHEST) - jnp.einsum(
        "ckj,qj->ckq", prod_im, inner_sin, precision=HIGHEST
    )
    back_im = jnp.einsum("ckj,qj->ckq", prod_im, inner_cos, precision=HIGHEST) + jnp.einsum(
        "ckj,qj->ckq", prod_re, inner_sin, precision=HIGHEST
    )
    turned_re = back_re * twist_cos - back_im * twist_sin
    turned_im = back_im * twist_cos + back_re * twist_sin
    result = jnp.einsum("kp,ckq->cpq", outer_cos, turned_re, precision=HIGHEST) - jnp.einsum(
        "kp,ckq->cpq", outer_sin, turned_im, precision=HIGHEST
    )
    return (result / (2.0 * length)).reshape(channels, length)


def general_body(features, destination, targets, domains, domain_tokens, short_filter, long_filter, skip):
    devices = lax.axis_size("ctx")
    rows_here = features.shape[0]
    length = devices * rows_here
    half_width = features.shape[1] // 3
    channels = half_width // devices
    capacity = 5 * rows_here // (2 * devices)
    owner_dev = destination // rows_here
    offset = destination % rows_here
    order = jnp.arange(rows_here, dtype=jnp.int32)
    ahead = (owner_dev[:, None] == owner_dev[None, :]) & (order[None, :] < order[:, None])
    slot_rank = jnp.sum(ahead.astype(jnp.int32), axis=1)
    buffer = (
        jnp.zeros((devices, capacity, 3 * half_width), features.dtype)
        .at[owner_dev, slot_rank]
        .set(features)
    )
    places = (
        jnp.full((devices, capacity), rows_here, jnp.int32).at[owner_dev, slot_rank].set(offset)
    )
    arrived, arrived_places = (
        lax.all_to_all(buffer, "ctx", split_axis=0, concat_axis=0, tiled=True),
        lax.all_to_all(places, "ctx", split_axis=0, concat_axis=0, tiled=True),
    )
    ordered = jnp.zeros((rows_here + 1, 3 * half_width), features.dtype)
    ordered = ordered.at[arrived_places.reshape(-1)].set(arrived.reshape(-1, 3 * half_width))[
        :rows_here
    ]
    blocks = ordered.reshape(rows_here, 3, devices, channels).transpose(2, 1, 3, 0)
    columns = lax.all_to_all(blocks, "ctx", split_axis=0, concat_axis=3, tiled=True)[0]
    inputs = columns.astype(jnp.float32)
    tap_weights = short_filter[:, 0]
    shorted = jnp.zeros_like(inputs)
    for tap_index in range(tap_weights.shape[0]):
        shifted = jnp.pad(inputs, ((0, 0), (0, 0), (tap_index, 0)))[:, :, :length]
        shorted = shorted + tap_weights[tap_index][:, :, None] * shifted
    signal = shorted[0] * shorted[2]
    long_part = causal_convolution(signal, long_filter[0])
    output_cols = (shorted[1] * (long_part + skip[0][:, None] * signal)).astype(jnp.bfloat16)
    returned = lax.all_to_all(
        output_cols.reshape(channels, devices, rows_here),
        "ctx",
        split_axis=1,
        concat_axis=0,
        tiled=True,
    )
    mixed = returned.reshape(half_width, rows_here).T
    copy_index = lax.axis_index("mp")
    model_index = copy_index // 2
    half_index = copy_index % 2
    values = mixed.astype(jnp.float32)
    part_exp = jnp.sum(jnp.exp(values), axis=1)
    local_target = targets - half_index * half_width
    inside = (local_target >= 0) & (local_target < half_width)
    picked = jnp.take_along_axis(
        values, jnp.clip(local_target, 0, half_width - 1)[:, None], axis=1
    )[:, 0]
    part_target = jnp.where(inside, picked, 0.0)
    is_model = jnp.arange(MODELS, dtype=jnp.int32)[:, None] == model_index
    exp_terms = jnp.where(is_model, part_exp[None, :], 0.0)
    target_terms = jnp.where(is_model, part_target[None, :], 0.0)
    total_exp, total_target = lax.psum((exp_terms, target_terms), "mp")
    losses = jnp.log(total_exp) - total_target
    token_excess = jnp.maximum(losses[0] - losses[1], 0.0)
    domain_count = domain_tokens.shape[0]
    in_domain = domains[None, :] == jnp.arange(domain_count, dtype=jnp.int32)[:, None]
    partial_sums = jnp.sum(jnp.where(in_domain, token_excess[None, :], 0.0), axis=1)
    domain_sums = lax.psum(partial_sums, "ctx")
    return (mixed, domain_sums / domain_tokens.astype(jnp.float32))


INNER = 128
OUTER = 16
FREQS = OUTER // 2 + 1
BF16 = jnp.bfloat16
F32 = jnp.float32


def weighted(terms):
    total = None
    for coef, value in terms:
        if value is None or abs(coef) < 1e-9:
            continue
        if abs(abs(coef) - 1.0) < 1e-9:
            term = value
            if coef < 0:
                total = -term if total is None else total - term
                continue
        else:
            term = coef * value
        total = term if total is None else total + term
    return total


def outer_forward(blocks):
    real, imag = [None] * FREQS, [None] * FREQS
    for k in range(FREQS // 2 + 1):
        angle = [2.0 * math.pi * p * k / OUTER for p in range(8)]
        parts = []
        for first in (0, 1):
            picks = range(first, 8, 2)
            parts.append(weighted([(math.cos(angle[p]), blocks[p]) for p in picks]))
            parts.append(weighted([(-math.sin(angle[p]), blocks[p]) for p in picks]))
        real_even, imag_even, real_odd, imag_odd = parts
        real[k] = weighted([(1.0, real_even), (1.0, real_odd)])
        imag[k] = weighted([(1.0, imag_even), (1.0, imag_odd)])
        if k < 4:
            real[8 - k] = weighted([(1.0, real_even), (-1.0, real_odd)])
            imag[8 - k] = weighted([(-1.0, imag_even), (1.0, imag_odd)])
    return real, imag


def outer_backward(real, imag):
    sums = {}
    for sign in (1.0, -1.0):
        sums[sign] = [
            (
                weighted([(1.0, real[k]), (sign, real[8 - k])]),
                weighted([(1.0, imag[k]), (-sign, imag[8 - k])]) if k else None,
            )
            for k in range(4)
        ]
    blocks = []
    for a in range(8):
        sign = 1.0 if a % 2 == 0 else -1.0
        terms = [(1.0, sums[sign][0][0])]
        for k in range(1, 4):
            angle = 2.0 * math.pi * k * a / OUTER
            terms.append((math.cos(angle), sums[sign][k][0]))
            terms.append((-math.sin(angle), sums[sign][k][1]))
        terms.append((math.cos(math.pi * a / 2), real[4]))
        terms.append((-math.sin(math.pi * a / 2), imag[4]))
        blocks.append(weighted(terms))
    return blocks


def halves(value):
    high = value.astype(BF16)
    return high, (value - high.astype(F32)).astype(BF16)


def stacked_dot(left, right, dims=(((1,), (0,)), ((), ()))):
    return lax.dot_general(left, right, dims, preferred_element_type=F32)


def table_inputs():
    index = np.arange(INNER)
    inner = 2.0 * np.pi * (np.outer(index, index) % INNER) / INNER
    twist = 2.0 * np.pi * np.outer(np.arange(FREQS), index) / (OUTER * INNER)
    inner_tab = np.stack([np.cos(inner), np.sin(inner)]).astype(np.float32)
    row_tab = np.stack([np.cos(twist), np.sin(twist)])[:, :, None, :].astype(np.float32)
    return jnp.asarray(inner_tab), jnp.asarray(row_tab)


def make_tables(inner_ref, row_ref, forward, backward):
    lower, upper = pl.ds(0, INNER), pl.ds(INNER, INNER)

    def store(ref, k, cos, sin, flip):
        cos_parts, sin_parts = halves(cos), halves(sin)
        for place, kind in ((0, 0), (1, 0), (2, 1)):
            c, s = cos_parts[kind], sin_parts[kind]
            first = pl.ds(place * 2 * INNER, INNER)
            second = pl.ds(place * 2 * INNER + INNER, INNER)
            ref[k, lower, first] = c
            ref[k, lower, second] = -s if flip else s
            ref[k, upper, first] = s if flip else -s
            ref[k, upper, second] = c

    def step(k, carry):
        base_cos, base_sin = inner_ref[0], inner_ref[1]
        row_cos, row_sin = row_ref[0, k], row_ref[1, k]
        cos, sin = base_cos * row_cos - base_sin * row_sin, base_sin * row_cos + base_cos * row_sin
        store(forward, k, cos, sin, False)
        col_cos = jnp.broadcast_to(row_cos, (INNER, INNER)).T
        col_sin = jnp.broadcast_to(row_sin, (INNER, INNER)).T
        cos, sin = base_cos * col_cos - base_sin * col_sin, base_sin * col_cos + base_cos * col_sin
        store(backward, k, cos, sin, True)
        return carry

    lax.fori_loop(0, FREQS, step, 0)


def filter_spectrum(filter_ref, forward, work, spectrum_ref):
    channels = filter_ref.shape[1]

    def stage(block, carry):
        rows = pl.ds(pl.multiple_of(block * 16, 16), 16)
        real, imag = outer_forward([filter_ref[0, rows, pl.ds(p * INNER, INNER)] for p in range(8)])
        for k in range(FREQS):
            for place, part in ((0, real[k]), (INNER, imag[k])):
                part = jnp.zeros((16, INNER), F32) if part is None else part
                high, low = halves(part)
                work[k, rows, pl.ds(place, INNER)] = high
                work[k, rows, pl.ds(place + 2 * INNER, INNER)] = low
                work[k, rows, pl.ds(place + 4 * INNER, INNER)] = high
        return carry

    lax.fori_loop(0, channels // 16, stage, 0)

    def transform(k, carry):
        scale = jnp.where((k == 0) | (k == FREQS - 1), 0.5, 1.0) * (2.0 / (OUTER * INNER))
        spectrum_ref[k] = scale * stacked_dot(forward[k], work[k], (((1,), (1,)), ((), ())))
        return carry

    lax.fori_loop(0, FREQS, transform, 0)


WIDTH = 128


def build_picks(places, pick_ref):
    length = pick_ref.shape[0]

    def step(block, carry):
        here = lax.broadcasted_iota(jnp.int32, (128, length), 0) + block * 128
        rows = pl.ds(pl.multiple_of(block * 128, 128), 128)
        pick_ref[rows, :] = jnp.where(here == places, 1.0, 0.0).astype(BF16)
        return carry

    lax.fori_loop(0, length // 128, step, 0)


def order_rows(cols_ref, pick_ref, seq_ref, first, width):
    length = cols_ref.shape[0]

    def step(block, carry):
        rows = pl.multiple_of(block * 256, 256)
        seq_ref[pl.ds(rows + 8, 256), pl.ds(first, width)] = jnp.dot(
            pick_ref[pl.ds(rows, 256), :], cols_ref[:, pl.ds(first, width)],
            preferred_element_type=F32,
        )
        return carry

    lax.fori_loop(0, length // 256, step, 0)


def shorted_rows(seq_ref, taps_ref, start, count, place, part, here):
    window = seq_ref[pl.ds(start, count + 8), pl.ds(place * WIDTH, WIDTH)]
    total = None
    for tap in range(taps_ref.shape[0] // 3):
        weight = taps_ref[tap * 3 + part, :, here]
        term = weight * window[8 - tap : 8 + count - tap]
        total = term if total is None else total + term
    return total


def short_and_outer(seq_ref, taps_ref, work, signal_ref, here):
    def stage(block, carry):
        offset = pl.multiple_of(block * 16, 16)
        signals = []
        for p in range(8):
            rows = pl.ds(p * INNER + offset, 16)
            start = pl.multiple_of(p * INNER + block * 16, 16)
            signal = shorted_rows(seq_ref, taps_ref, start, 16, 0, 0, here) * shorted_rows(
                seq_ref, taps_ref, start, 16, 1, 2, here
            )
            signal_ref[rows, :] = signal
            signals.append(signal)
        real, imag = outer_forward(signals)
        for k in range(FREQS):
            for place, part in ((0, real[k]), (INNER, imag[k])):
                part = jnp.zeros((16, WIDTH), F32) if part is None else part
                high, low = halves(part)
                work[k, pl.ds(place + offset, 16), :] = high
                work[k, pl.ds(place + 2 * INNER + offset, 16), :] = low
                work[k, pl.ds(place + 4 * INNER + offset, 16), :] = high
        return carry

    lax.fori_loop(0, INNER // 16, stage, 0)


def transform_product(spectrum_ref, forward, backward, work, back_ref, here):
    def step(k, carry):
        value = stacked_dot(forward[k], work[k])
        real, imag = value[:INNER], value[INNER:]
        other = spectrum_ref[k, :, here]
        other_real, other_imag = other[:INNER], other[INNER:]
        product = jnp.concatenate(
            [real * other_real - imag * other_imag, real * other_imag + imag * other_real], axis=0
        )
        high, low = halves(product)
        back_ref[k] = stacked_dot(backward[k], jnp.concatenate([high, low, high], axis=0))
        return carry

    lax.fori_loop(0, FREQS, step, 0, unroll=3)


def long_and_direct(back_ref, signal_ref, skip_ref, total_ref, piece, here):
    def step(block, carry):
        offset = pl.multiple_of(block * 16, 16)
        real = [back_ref[k, pl.ds(offset, 16), :] for k in range(FREQS)]
        imag = [
            back_ref[k, pl.ds(INNER + offset, 16), :] if 0 < k < FREQS - 1 else None
            for k in range(FREQS)
        ]
        direct = skip_ref[pl.ds(0, 1), here]
        for p, long_part in enumerate(outer_backward(real, imag)):
            rows = pl.ds(p * INNER + offset, 16)
            total_ref[piece, rows, :] = long_part + direct * signal_ref[rows, :]
        return carry

    lax.fori_loop(0, INNER // 16, step, 0)


LIMIT = 56 * 2**20
MESH = pl.DeviceIdType.MESH
PARTS = (0, 2, 1)


def whole_kernel(
    devices, copies, pieces,
    features, place_ref, target_ref, domain_ref, taps_ref, filter_hbm, skip_ref,
    inner_ref, row_ref,
    mixed_ref, sums_ref,
    filter_ref, cols, places, pick_ref, wanted_ref, spectrum, forward, backward, filter_work,
    seq_ref, work, back_ref, signal_ref, total_ref, out_ref, exp_ref, hit_ref,
    terms_ref, half_out, half_in, gathered, domain_hot, domain_sums,
    in_send, in_recv, place_send, place_recv, out_send, out_recv,
    given_send, given_recv, half_send, half_recv, sum_send, sum_recv, filter_sem,
):
    me = lax.axis_index("ctx")
    copy_index = lax.axis_index("mp")
    rows_here, half_width = mixed_ref.shape
    channels = half_width // devices
    others = devices - 1
    core = lax.rem(copy_index, 2)
    model_index = copy_index // 2
    partner = copy_index + 1 - 2 * core
    span = rows_here * devices // 2
    group = devices // 2
    my_group, my_place = me // group, lax.rem(me, group)

    def peer(step):
        turn = step // group
        place = lax.rem(my_place + lax.rem(step, group) + turn, group)
        return lax.rem(my_group + 1 + turn, 2) * group + place

    around = [lax.rem(me + step, devices) for step in range(1, devices)]
    near = [lax.rem(copy_index + step, copies) for step in range(copies)]

    def rows_of(device):
        return pl.ds(pl.multiple_of(device * rows_here, rows_here), rows_here)

    def feature_cols(device, part, piece):
        start = part * half_width + device * channels + piece * WIDTH
        return pl.ds(pl.multiple_of(start, WIDTH), WIDTH)

    def place_cols(place):
        return pl.ds(place * WIDTH, WIDTH)

    def ctx_start(source, target, send, recv, device):
        pltpu.make_async_remote_copy(
            src_ref=source, dst_ref=target, send_sem=send, recv_sem=recv,
            device_id={"ctx": device}, device_id_type=MESH,
        ).start()

    def wait_for(ref, sem):
        pltpu.make_async_copy(ref, ref, sem).wait()

    def send(piece, kinds):
        for device in around:
            for place in kinds:
                ctx_start(
                    features.at[:, feature_cols(device, PARTS[place], piece)],
                    cols.at[piece, rows_of(me), place_cols(place)],
                    in_send, in_recv.at[piece, place], device,
                )

    def own(piece, place):
        pltpu.make_async_copy(
            features.at[:, feature_cols(me, PARTS[place], piece)],
            cols.at[piece, rows_of(me), place_cols(place)],
            in_recv.at[piece, place],
        ).start()

    def arrive(piece, kinds):
        for place in kinds:
            wait_for(cols.at[piece, :, place_cols(place)], in_recv.at[piece, place])

    barrier = pltpu.get_barrier_semaphore()
    for device in around:
        pl.semaphore_signal(barrier, inc=1, device_id={"ctx": device}, device_id_type=MESH)
    for copy in near[1:]:
        pl.semaphore_signal(barrier, inc=1, device_id={"mp": copy}, device_id_type=MESH)
    places[me] = jnp.concatenate([place_ref[...], target_ref[...], domain_ref[...]], axis=0)
    pl.semaphore_wait(barrier, devices + copies - 2)

    send(0, (0, 1))
    for device in around:
        ctx_start(places.at[me], places.at[me], place_send, place_recv, device)
    for piece in range(1, pieces):
        send(piece, (0, 1))
    for piece in range(pieces):
        send(piece, (2,))
    filter_copy = pltpu.make_async_copy(filter_hbm, filter_ref, filter_sem)
    filter_copy.start()
    for piece in range(pieces):
        for place in range(3):
            own(piece, place)

    make_tables(inner_ref, row_ref, forward, backward)
    filter_copy.wait()
    filter_spectrum(filter_ref, forward, filter_work, spectrum)
    seq_ref[pl.ds(0, 8), :] = jnp.zeros((8, seq_ref.shape[1]), F32)

    wait_for(places.at[pl.ds(0, others)], place_recv)
    build_picks(jnp.concatenate([places[d][0:1] for d in range(devices)], axis=1), pick_ref)
    base = core * half_width + me * channels

    @pl.loop(0, devices // 2)
    def _(step):
        kinds = lax.broadcasted_iota(jnp.int32, (WIDTH, rows_here), 0)
        match = kinds == places[core * (devices // 2) + step][2:3]
        domain_hot[:, rows_of(step)] = jnp.where(match, 1.0, 0.0).astype(BF16)

    @pl.loop(0, devices)
    def _(device):
        loader = places[device][1:2]
        wanted_ref[rows_of(device), :] = jnp.broadcast_to(loader - base, (rows_here, rows_here)).T

    for piece in range(pieces):
        here = pl.ds(piece * WIDTH, WIDTH)
        arrive(piece, (0, 1))
        order_rows(cols.at[piece], pick_ref, seq_ref, 0, 2 * WIDTH)
        short_and_outer(seq_ref, taps_ref, work, signal_ref, here)
        transform_product(spectrum, forward, backward, work, back_ref, here)
        long_and_direct(back_ref, signal_ref, skip_ref, total_ref, piece, here)

    lane = lax.broadcasted_iota(jnp.int32, (rows_here, WIDTH), 1)
    picker_col = lax.broadcasted_iota(jnp.int32, (8, 3 * WIDTH), 1) < 2 * WIDTH
    picker_row = lax.broadcasted_iota(jnp.int32, (8, 3 * WIDTH), 0)
    picker = (picker_col & (picker_row == 0)) | (~picker_col & (picker_row == 1))
    picker = jnp.where(picker, 1.0, 0.0).astype(BF16)

    def gate(piece, owner):
        here = pl.ds(piece * WIDTH, WIDTH)
        start = pl.multiple_of(owner * rows_here, rows_here)
        value = shorted_rows(seq_ref, taps_ref, start, rows_here, 2, 1, here)
        value = (value * total_ref[piece, rows_of(owner), :]).astype(out_ref.dtype)
        out_ref[piece, rows_of(owner), :] = value
        return value.astype(F32)

    def tally(piece, owner, value):
        rows = rows_of(owner)
        power = jnp.exp(value)
        hit = jnp.where(lane + piece * WIDTH == wanted_ref[rows, :], value, 0.0)
        if piece:
            power = power + exp_ref[rows, :]
            hit = hit + hit_ref[rows, :]
        if piece < pieces - 1:
            exp_ref[rows, :] = power
            hit_ref[rows, :] = hit
            return
        high, low = halves(power)
        terms_ref[rows, pl.ds(0, WIDTH)] = high
        terms_ref[rows, pl.ds(WIDTH, WIDTH)] = low
        terms_ref[rows, pl.ds(2 * WIDTH, WIDTH)] = hit.astype(BF16)

    def mixed_part(piece):
        start = pl.multiple_of(me * channels + piece * WIDTH, WIDTH)
        return mixed_ref.at[:, pl.ds(start, WIDTH)]

    def give(piece, device):
        ctx_start(
            out_ref.at[piece, rows_of(device), :], mixed_part(piece), out_send, out_recv, device
        )

    def keep(piece):
        pltpu.make_async_copy(out_ref.at[piece, rows_of(me), :], mixed_part(piece), out_recv).start()

    for piece in range(pieces - 1):
        arrive(piece, (2,))
        order_rows(cols.at[piece], pick_ref, seq_ref, 2 * WIDTH, WIDTH)

        @pl.loop(0, others)
        def _(step, piece=piece):
            device = peer(step)
            gate(piece, device)
            give(piece, device)

        gate(piece, me)
        keep(piece)

        @pl.loop(0, devices)
        def _(device, piece=piece):
            tally(piece, device, out_ref[piece, rows_of(device), :].astype(F32))

    piece = pieces - 1
    arrive(piece, (2,))
    order_rows(cols.at[piece], pick_ref, seq_ref, 2 * WIDTH, WIDTH)

    def half_sums(half):
        @pl.loop(0, devices // 2)
        def _(step):
            owner = half * (devices // 2) + step
            tally(piece, owner, gate(piece, owner))

        rows = pl.ds(pl.multiple_of(half * span, span), span)
        return stacked_dot(picker, terms_ref[rows, :], (((1,), (1,)), ((), ())))[0:2]

    def core_copy(source, target, send, recv):
        return pltpu.make_async_remote_copy(
            src_ref=source, dst_ref=target, send_sem=send, recv_sem=recv,
            device_id={"mp": partner}, device_id_type=MESH,
        )

    half_out[...] = half_sums(1 - core)
    half_copy = core_copy(half_out, half_in, half_send, half_recv)
    half_copy.start()
    half_own = half_sums(core)
    half_copy.wait_recv()
    half_theirs = half_in[...]
    chip = me * MODELS + model_index
    gathered[chip] = half_own + half_theirs
    def tell(device, copy):
        pltpu.make_async_remote_copy(
            src_ref=gathered.at[chip], dst_ref=gathered.at[chip],
            send_sem=given_send, recv_sem=given_recv,
            device_id={"ctx": device, "mp": copy}, device_id_type=MESH,
        ).start()

    for device in around:
        for other in range(MODELS):
            tell(device, near[2 * other])
    tell(me, near[2])
    for device in around:
        give(piece, device)
    keep(piece)

    wait_for(features.at[:, pl.ds(0, 3 * channels * others)], in_send)
    wait_for(places.at[pl.ds(0, others)], place_send)
    half_copy.wait_send()
    wait_for(gathered.at[pl.ds(0, MODELS * devices - 1)], given_recv)
    losses = []
    for model in range(MODELS):
        both = gathered[model]
        for device in range(1, devices):
            both = both + gathered[device * MODELS + model]
        losses.append(jnp.log(both[0:1]) - both[1:2])
    excess = jnp.broadcast_to(jnp.maximum(losses[0] - losses[1], 0.0), (8, span))
    high, low = halves(excess)
    top = lax.broadcasted_iota(jnp.int32, (8, span), 0)
    excess = jnp.where(top == 0, high.astype(F32), jnp.where(top == 1, low.astype(F32), 0.0))
    sums = stacked_dot(excess.astype(BF16), domain_hot[...], (((1,), (1,)), ((), ())))
    domain_sums[core] = sums[0:1] + sums[1:2]
    sum_copy = core_copy(domain_sums.at[core], domain_sums.at[core], sum_send, sum_recv)
    sum_copy.start()
    wait_for(gathered.at[pl.ds(0, MODELS * devices - 1)], given_send)
    sum_copy.wait()
    sums = domain_sums[0] + domain_sums[1]
    sums_ref[...] = sums[:, : sums_ref.shape[1]]
    wait_for(mixed_ref, out_recv)
    wait_for(out_ref.at[:, pl.ds(0, rows_here * others), :], out_send)


def last_kernel(mixed_ref, sums_ref, tokens_ref, out_ref, excess_ref, ratio_ref, sems):
    mixed_copy = pltpu.make_async_copy(mixed_ref, out_ref, sems.at[0])
    mixed_copy.start()
    ratio_ref[...] = sums_ref[...] / tokens_ref[...].astype(F32)
    ratio_copy = pltpu.make_async_copy(ratio_ref, excess_ref, sems.at[1])
    ratio_copy.start()
    mixed_copy.wait()
    ratio_copy.wait()


def body(features, destination, targets, domains, domain_tokens, short_filter, long_filter, skip):
    devices = lax.axis_size("ctx")
    copies = lax.axis_size("mp")
    rows_here = features.shape[0]
    length = devices * rows_here
    half_width = features.shape[1] // 3
    channels = half_width // devices
    if length != 8 * INNER or rows_here != 128 or channels != 256 or copies != 4 or domain_tokens.shape[0] > WIDTH:
        return general_body(
            features, destination, targets, domains, domain_tokens, short_filter, long_filter, skip
        )
    pieces = channels // WIDTH
    count = domain_tokens.shape[0]
    vmem = pl.BlockSpec(memory_space=pltpu.VMEM)
    hbm = pl.BlockSpec(memory_space=pl.ANY)
    big = (FREQS, 2 * INNER, 6 * INNER)
    dma = pltpu.SemaphoreType.DMA
    mixed, sums = pl.pallas_call(
        functools.partial(whole_kernel, devices, copies, pieces),
        out_shape=[
            pltpu.VMEM((rows_here, half_width), BF16),
            pltpu.VMEM((1, count), F32),
        ],
        in_specs=[hbm, vmem, vmem, vmem, vmem, hbm, vmem, vmem, vmem],
        out_specs=[vmem, vmem],
        scratch_shapes=[
            pltpu.VMEM((1, channels, length), F32),
            pltpu.VMEM((pieces, length, 3 * WIDTH), BF16),
            pltpu.VMEM((devices, 3, rows_here), jnp.int32),
            pltpu.VMEM((length, length), BF16),
            pltpu.VMEM((length, WIDTH), jnp.int32),
            pltpu.VMEM((FREQS, 2 * INNER, channels), F32),
            pltpu.VMEM(big, BF16),
            pltpu.VMEM(big, BF16),
            pltpu.VMEM((FREQS, channels, 6 * INNER), BF16),
            pltpu.VMEM((length + 8, 3 * WIDTH), F32),
            pltpu.VMEM((FREQS, 6 * INNER, WIDTH), BF16),
            pltpu.VMEM((FREQS, 2 * INNER, WIDTH), F32),
            pltpu.VMEM((length, WIDTH), F32),
            pltpu.VMEM((pieces, length, WIDTH), F32),
            pltpu.VMEM((pieces, length, WIDTH), BF16),
            pltpu.VMEM((length, WIDTH), F32),
            pltpu.VMEM((length, WIDTH), F32),
            pltpu.VMEM((length, 3 * WIDTH), BF16),
            pltpu.VMEM((2, length // 2), F32),
            pltpu.VMEM((2, length // 2), F32),
            pltpu.VMEM((MODELS * devices, 2, length // 2), F32),
            pltpu.VMEM((WIDTH, length // 2), BF16),
            pltpu.VMEM((2, 1, WIDTH), F32),
            dma,
            dma((pieces, 3)),
            dma,
            dma,
            dma,
            dma,
            dma,
            dma,
            dma,
            dma,
            dma,
            dma,
            dma,
        ],
        compiler_params=pltpu.CompilerParams(
            vmem_limit_bytes=LIMIT, collective_id=0, has_side_effects=True
        ),
    )(
        features, destination.reshape(1, rows_here), targets.reshape(1, rows_here),
        domains.reshape(1, rows_here),
        short_filter.transpose(0, 2, 1, 3).reshape(-1, 1, channels), long_filter, skip,
        *table_inputs(),
    )
    mixed, excess = pl.pallas_call(
        last_kernel,
        out_shape=[
            jax.ShapeDtypeStruct((rows_here, half_width), BF16),
            jax.ShapeDtypeStruct((1, count), F32),
        ],
        in_specs=[vmem, vmem, vmem],
        out_specs=[hbm, hbm],
        scratch_shapes=[pltpu.VMEM((1, count), F32), dma((2,))],
        compiler_params=pltpu.CompilerParams(vmem_limit_bytes=2**20),
    )(mixed, sums, domain_tokens.reshape(1, count))
    return (mixed, excess.reshape(count))


def solution(mesh):
    return jax.shard_map(
        body,
        mesh=mesh,
        in_specs=(
            P("ctx", "mp"),
            P("ctx"),
            P("ctx"),
            P("ctx"),
            P(),
            P(None, "mp", None, "ctx"),
            P("mp", "ctx", None),
            P("mp", "ctx"),
        ),
        out_specs=(P("ctx", "mp"), P()),
        check_vma=False,
    )
```

```python
import functools
import math

import jax
import jax.numpy as jnp
import numpy as np
from jax import lax
from jax.experimental import pallas as pl
from jax.experimental.pallas import tpu as pltpu
from jax.sharding import PartitionSpec as P

MODELS = 2


HIGHEST = lax.Precision.HIGHEST


def dft_tables(count, limit, modulus):
    row_index = jnp.arange(count, dtype=jnp.int32)[:, None]
    col_index = jnp.arange(limit, dtype=jnp.int32)[None, :]
    angle = 2.0 * math.pi / modulus * (row_index * col_index % modulus).astype(jnp.float32)
    return (jnp.cos(angle), jnp.sin(angle))


def forward_transform(signal, outer_cos, outer_sin, twist_cos, twist_sin, inner_cos, inner_sin):
    real_a = jnp.einsum("kp,cpq->ckq", outer_cos, signal, precision=HIGHEST)
    imag_a = -jnp.einsum("kp,cpq->ckq", outer_sin, signal, precision=HIGHEST)
    real_b = real_a * twist_cos + imag_a * twist_sin
    imag_b = imag_a * twist_cos - real_a * twist_sin
    real_c = jnp.einsum("ckq,qj->ckj", real_b, inner_cos, precision=HIGHEST) + jnp.einsum(
        "ckq,qj->ckj", imag_b, inner_sin, precision=HIGHEST
    )
    imag_c = jnp.einsum("ckq,qj->ckj", imag_b, inner_cos, precision=HIGHEST) - jnp.einsum(
        "ckq,qj->ckj", real_b, inner_sin, precision=HIGHEST
    )
    return (real_c, imag_c)


def causal_convolution(signal, kernel):
    channels, length = signal.shape
    inner_size = 128
    outer_size = 2 * length // inner_size
    half_outer = outer_size // 2
    outer_cos, outer_sin = dft_tables(outer_size, half_outer, outer_size)
    twist_cos, twist_sin = dft_tables(outer_size, inner_size, 2 * length)
    inner_cos, inner_sin = dft_tables(inner_size, inner_size, inner_size)
    sig_re, sig_im = forward_transform(
        signal.reshape(channels, half_outer, inner_size),
        outer_cos,
        outer_sin,
        twist_cos,
        twist_sin,
        inner_cos,
        inner_sin,
    )
    ker_re, ker_im = forward_transform(
        kernel.reshape(channels, half_outer, inner_size),
        outer_cos,
        outer_sin,
        twist_cos,
        twist_sin,
        inner_cos,
        inner_sin,
    )
    prod_re = sig_re * ker_re - sig_im * ker_im
    prod_im = sig_re * ker_im + sig_im * ker_re
    back_re = jnp.einsum("ckj,qj->ckq", prod_re, inner_cos, precision=HIGHEST) - jnp.einsum(
        "ckj,qj->ckq", prod_im, inner_sin, precision=HIGHEST
    )
    back_im = jnp.einsum("ckj,qj->ckq", prod_im, inner_cos, precision=HIGHEST) + jnp.einsum(
        "ckj,qj->ckq", prod_re, inner_sin, precision=HIGHEST
    )
    turned_re = back_re * twist_cos - back_im * twist_sin
    turned_im = back_im * twist_cos + back_re * twist_sin
    result = jnp.einsum("kp,ckq->cpq", outer_cos, turned_re, precision=HIGHEST) - jnp.einsum(
        "kp,ckq->cpq", outer_sin, turned_im, precision=HIGHEST
    )
    return (result / (2.0 * length)).reshape(channels, length)


def general_body(features, destination, targets, domains, domain_tokens, short_filter, long_filter, skip):
    devices = lax.axis_size("ctx")
    rows_here = features.shape[0]
    length = devices * rows_here
    half_width = features.shape[1] // 3
    channels = half_width // devices
    capacity = 5 * rows_here // (2 * devices)
    owner_dev = destination // rows_here
    offset = destination % rows_here
    order = jnp.arange(rows_here, dtype=jnp.int32)
    ahead = (owner_dev[:, None] == owner_dev[None, :]) & (order[None, :] < order[:, None])
    slot_rank = jnp.sum(ahead.astype(jnp.int32), axis=1)
    buffer = (
        jnp.zeros((devices, capacity, 3 * half_width), features.dtype)
        .at[owner_dev, slot_rank]
        .set(features)
    )
    places = (
        jnp.full((devices, capacity), rows_here, jnp.int32).at[owner_dev, slot_rank].set(offset)
    )
    arrived, arrived_places = (
        lax.all_to_all(buffer, "ctx", split_axis=0, concat_axis=0, tiled=True),
        lax.all_to_all(places, "ctx", split_axis=0, concat_axis=0, tiled=True),
    )
    ordered = jnp.zeros((rows_here + 1, 3 * half_width), features.dtype)
    ordered = ordered.at[arrived_places.reshape(-1)].set(arrived.reshape(-1, 3 * half_width))[
        :rows_here
    ]
    blocks = ordered.reshape(rows_here, 3, devices, channels).transpose(2, 1, 3, 0)
    columns = lax.all_to_all(blocks, "ctx", split_axis=0, concat_axis=3, tiled=True)[0]
    inputs = columns.astype(jnp.float32)
    tap_weights = short_filter[:, 0]
    shorted = jnp.zeros_like(inputs)
    for tap_index in range(tap_weights.shape[0]):
        shifted = jnp.pad(inputs, ((0, 0), (0, 0), (tap_index, 0)))[:, :, :length]
        shorted = shorted + tap_weights[tap_index][:, :, None] * shifted
    signal = shorted[0] * shorted[2]
    long_part = causal_convolution(signal, long_filter[0])
    output_cols = (shorted[1] * (long_part + skip[0][:, None] * signal)).astype(jnp.bfloat16)
    returned = lax.all_to_all(
        output_cols.reshape(channels, devices, rows_here),
        "ctx",
        split_axis=1,
        concat_axis=0,
        tiled=True,
    )
    mixed = returned.reshape(half_width, rows_here).T
    copy_index = lax.axis_index("mp")
    model_index = copy_index // 2
    half_index = copy_index % 2
    values = mixed.astype(jnp.float32)
    part_exp = jnp.sum(jnp.exp(values), axis=1)
    local_target = targets - half_index * half_width
    inside = (local_target >= 0) & (local_target < half_width)
    picked = jnp.take_along_axis(
        values, jnp.clip(local_target, 0, half_width - 1)[:, None], axis=1
    )[:, 0]
    part_target = jnp.where(inside, picked, 0.0)
    is_model = jnp.arange(MODELS, dtype=jnp.int32)[:, None] == model_index
    exp_terms = jnp.where(is_model, part_exp[None, :], 0.0)
    target_terms = jnp.where(is_model, part_target[None, :], 0.0)
    total_exp, total_target = lax.psum((exp_terms, target_terms), "mp")
    losses = jnp.log(total_exp) - total_target
    token_excess = jnp.maximum(losses[0] - losses[1], 0.0)
    domain_count = domain_tokens.shape[0]
    in_domain = domains[None, :] == jnp.arange(domain_count, dtype=jnp.int32)[:, None]
    partial_sums = jnp.sum(jnp.where(in_domain, token_excess[None, :], 0.0), axis=1)
    domain_sums = lax.psum(partial_sums, "ctx")
    return (mixed, domain_sums / domain_tokens.astype(jnp.float32))


INNER = 128
OUTER = 16
FREQS = OUTER // 2 + 1
BF16 = jnp.bfloat16
F32 = jnp.float32


def weighted(terms):
    total = None
    for coef, value in terms:
        if value is None or abs(coef) < 1e-9:
            continue
        if abs(abs(coef) - 1.0) < 1e-9:
            term = value
            if coef < 0:
                total = -term if total is None else total - term
                continue
        else:
            term = coef * value
        total = term if total is None else total + term
    return total


def outer_forward(blocks):
    real, imag = [None] * FREQS, [None] * FREQS
    for k in range(FREQS // 2 + 1):
        angle = [2.0 * math.pi * p * k / OUTER for p in range(8)]
        parts = []
        for first in (0, 1):
            picks = range(first, 8, 2)
            parts.append(weighted([(math.cos(angle[p]), blocks[p]) for p in picks]))
            parts.append(weighted([(-math.sin(angle[p]), blocks[p]) for p in picks]))
        real_even, imag_even, real_odd, imag_odd = parts
        real[k] = weighted([(1.0, real_even), (1.0, real_odd)])
        imag[k] = weighted([(1.0, imag_even), (1.0, imag_odd)])
        if k < 4:
            real[8 - k] = weighted([(1.0, real_even), (-1.0, real_odd)])
            imag[8 - k] = weighted([(-1.0, imag_even), (1.0, imag_odd)])
    return real, imag


def outer_backward(real, imag):
    sums = {}
    for sign in (1.0, -1.0):
        sums[sign] = [
            (
                weighted([(1.0, real[k]), (sign, real[8 - k])]),
                weighted([(1.0, imag[k]), (-sign, imag[8 - k])]) if k else None,
            )
            for k in range(4)
        ]
    blocks = []
    for a in range(8):
        sign = 1.0 if a % 2 == 0 else -1.0
        terms = [(1.0, sums[sign][0][0])]
        for k in range(1, 4):
            angle = 2.0 * math.pi * k * a / OUTER
            terms.append((math.cos(angle), sums[sign][k][0]))
            terms.append((-math.sin(angle), sums[sign][k][1]))
        terms.append((math.cos(math.pi * a / 2), real[4]))
        terms.append((-math.sin(math.pi * a / 2), imag[4]))
        blocks.append(weighted(terms))
    return blocks


def halves(value):
    high = value.astype(BF16)
    return high, (value - high.astype(F32)).astype(BF16)


def stacked_dot(left, right, dims=(((1,), (0,)), ((), ()))):
    return lax.dot_general(left, right, dims, preferred_element_type=F32)


def table_inputs():
    index = np.arange(INNER)
    inner = 2.0 * np.pi * (np.outer(index, index) % INNER) / INNER
    twist = 2.0 * np.pi * np.outer(np.arange(FREQS), index) / (OUTER * INNER)
    inner_tab = np.stack([np.cos(inner), np.sin(inner)]).astype(np.float32)
    row_tab = np.stack([np.cos(twist), np.sin(twist)])[:, :, None, :].astype(np.float32)
    return jnp.asarray(inner_tab), jnp.asarray(row_tab)


def make_tables(inner_ref, row_ref, forward, backward):
    lower, upper = pl.ds(0, INNER), pl.ds(INNER, INNER)

    def store(ref, k, cos, sin, flip):
        cos_parts, sin_parts = halves(cos), halves(sin)
        for place, kind in ((0, 0), (1, 0), (2, 1)):
            c, s = cos_parts[kind], sin_parts[kind]
            first = pl.ds(place * 2 * INNER, INNER)
            second = pl.ds(place * 2 * INNER + INNER, INNER)
            ref[k, lower, first] = c
            ref[k, lower, second] = -s if flip else s
            ref[k, upper, first] = s if flip else -s
            ref[k, upper, second] = c

    def step(k, carry):
        base_cos, base_sin = inner_ref[0], inner_ref[1]
        row_cos, row_sin = row_ref[0, k], row_ref[1, k]
        cos, sin = base_cos * row_cos - base_sin * row_sin, base_sin * row_cos + base_cos * row_sin
        store(forward, k, cos, sin, False)
        col_cos = jnp.broadcast_to(row_cos, (INNER, INNER)).T
        col_sin = jnp.broadcast_to(row_sin, (INNER, INNER)).T
        cos, sin = base_cos * col_cos - base_sin * col_sin, base_sin * col_cos + base_cos * col_sin
        store(backward, k, cos, sin, True)
        return carry

    lax.fori_loop(0, FREQS, step, 0)


def filter_spectrum(filter_ref, forward, work, spectrum_ref):
    channels = filter_ref.shape[1]

    def stage(block, carry):
        rows = pl.ds(pl.multiple_of(block * 16, 16), 16)
        real, imag = outer_forward([filter_ref[0, rows, pl.ds(p * INNER, INNER)] for p in range(8)])
        for k in range(FREQS):
            for place, part in ((0, real[k]), (INNER, imag[k])):
                part = jnp.zeros((16, INNER), F32) if part is None else part
                high, low = halves(part)
                work[k, rows, pl.ds(place, INNER)] = high
                work[k, rows, pl.ds(place + 2 * INNER, INNER)] = low
                work[k, rows, pl.ds(place + 4 * INNER, INNER)] = high
        return carry

    lax.fori_loop(0, channels // 16, stage, 0)

    def transform(k, carry):
        scale = jnp.where((k == 0) | (k == FREQS - 1), 0.5, 1.0) * (2.0 / (OUTER * INNER))
        spectrum_ref[k] = scale * stacked_dot(forward[k], work[k], (((1,), (1,)), ((), ())))
        return carry

    lax.fori_loop(0, FREQS, transform, 0)


WIDTH = 128


def build_picks(places, pick_ref):
    length = pick_ref.shape[0]

    def step(block, carry):
        here = lax.broadcasted_iota(jnp.int32, (128, length), 0) + block * 128
        rows = pl.ds(pl.multiple_of(block * 128, 128), 128)
        pick_ref[rows, :] = jnp.where(here == places, 1.0, 0.0).astype(BF16)
        return carry

    lax.fori_loop(0, length // 128, step, 0)


def order_rows(cols_ref, pick_ref, seq_ref, first, width):
    length = cols_ref.shape[0]

    def step(block, carry):
        rows = pl.multiple_of(block * 256, 256)
        seq_ref[pl.ds(rows + 8, 256), pl.ds(first, width)] = jnp.dot(
            pick_ref[pl.ds(rows, 256), :], cols_ref[:, pl.ds(first, width)],
            preferred_element_type=F32,
        )
        return carry

    lax.fori_loop(0, length // 256, step, 0)


def shorted_rows(seq_ref, taps_ref, start, count, place, part, here):
    window = seq_ref[pl.ds(start, count + 8), pl.ds(place * WIDTH, WIDTH)]
    total = None
    for tap in range(taps_ref.shape[0] // 3):
        weight = taps_ref[tap * 3 + part, :, here]
        term = weight * window[8 - tap : 8 + count - tap]
        total = term if total is None else total + term
    return total


def short_and_outer(seq_ref, taps_ref, work, signal_ref, here):
    def stage(block, carry):
        offset = pl.multiple_of(block * 16, 16)
        signals = []
        for p in range(8):
            rows = pl.ds(p * INNER + offset, 16)
            start = pl.multiple_of(p * INNER + block * 16, 16)
            signal = shorted_rows(seq_ref, taps_ref, start, 16, 0, 0, here) * shorted_rows(
                seq_ref, taps_ref, start, 16, 1, 2, here
            )
            signal_ref[rows, :] = signal
            signals.append(signal)
        real, imag = outer_forward(signals)
        for k in range(FREQS):
            for place, part in ((0, real[k]), (INNER, imag[k])):
                part = jnp.zeros((16, WIDTH), F32) if part is None else part
                high, low = halves(part)
                work[k, pl.ds(place + offset, 16), :] = high
                work[k, pl.ds(place + 2 * INNER + offset, 16), :] = low
                work[k, pl.ds(place + 4 * INNER + offset, 16), :] = high
        return carry

    lax.fori_loop(0, INNER // 16, stage, 0)


def transform_product(spectrum_ref, forward, backward, work, back_ref, here):
    def step(k, carry):
        value = stacked_dot(forward[k], work[k])
        real, imag = value[:INNER], value[INNER:]
        other = spectrum_ref[k, :, here]
        other_real, other_imag = other[:INNER], other[INNER:]
        product = jnp.concatenate(
            [real * other_real - imag * other_imag, real * other_imag + imag * other_real], axis=0
        )
        high, low = halves(product)
        back_ref[k] = stacked_dot(backward[k], jnp.concatenate([high, low, high], axis=0))
        return carry

    lax.fori_loop(0, FREQS, step, 0, unroll=3)


def long_and_direct(back_ref, signal_ref, skip_ref, total_ref, piece, here):
    def step(block, carry):
        offset = pl.multiple_of(block * 16, 16)
        real = [back_ref[k, pl.ds(offset, 16), :] for k in range(FREQS)]
        imag = [
            back_ref[k, pl.ds(INNER + offset, 16), :] if 0 < k < FREQS - 1 else None
            for k in range(FREQS)
        ]
        direct = skip_ref[pl.ds(0, 1), here]
        for p, long_part in enumerate(outer_backward(real, imag)):
            rows = pl.ds(p * INNER + offset, 16)
            total_ref[piece, rows, :] = long_part + direct * signal_ref[rows, :]
        return carry

    lax.fori_loop(0, INNER // 16, step, 0)


LIMIT = 56 * 2**20
MESH = pl.DeviceIdType.MESH
PARTS = (0, 2, 1)


def whole_kernel(
    devices, copies, pieces,
    features, place_ref, target_ref, domain_ref, taps_ref, filter_hbm, skip_ref,
    inner_ref, row_ref,
    mixed_ref, sums_ref,
    filter_ref, cols, places, pick_ref, wanted_ref, spectrum, forward, backward, filter_work,
    seq_ref, work, back_ref, signal_ref, total_ref, out_ref, exp_ref, hit_ref,
    terms_ref, half_out, half_in, gathered, domain_hot, domain_sums,
    in_send, in_recv, place_send, place_recv, out_send, out_recv,
    given_send, given_recv, half_send, half_recv, sum_send, sum_recv, filter_sem, ready,
):
    me = lax.axis_index("ctx")
    copy_index = lax.axis_index("mp")
    rows_here, half_width = mixed_ref.shape
    channels = half_width // devices
    others = devices - 1
    core = lax.rem(copy_index, 2)
    model_index = copy_index // 2
    partner = copy_index + 1 - 2 * core
    span = rows_here * devices // 2
    group = devices // 2
    my_group, my_place = me // group, lax.rem(me, group)

    def peer(step):
        turn = step // group
        place = lax.rem(my_place + lax.rem(step, group) + turn, group)
        return lax.rem(my_group + 1 + turn, 2) * group + place

    around = [lax.rem(me + step, devices) for step in range(1, devices)]
    near = [lax.rem(copy_index + step, copies) for step in range(copies)]

    def rows_of(device):
        return pl.ds(pl.multiple_of(device * rows_here, rows_here), rows_here)

    def feature_cols(device, part, piece):
        start = part * half_width + device * channels + piece * WIDTH
        return pl.ds(pl.multiple_of(start, WIDTH), WIDTH)

    def place_cols(place):
        return pl.ds(place * WIDTH, WIDTH)

    def ctx_start(source, target, send, recv, device):
        pltpu.make_async_remote_copy(
            src_ref=source, dst_ref=target, send_sem=send, recv_sem=recv,
            device_id={"ctx": device}, device_id_type=MESH,
        ).start()

    def wait_for(ref, sem):
        pltpu.make_async_copy(ref, ref, sem).wait()

    def send(piece, kinds, targets):
        for device in targets:
            for place in kinds:
                ctx_start(
                    features.at[:, feature_cols(device, PARTS[place], piece)],
                    cols.at[piece, rows_of(me), place_cols(place)],
                    in_send, in_recv.at[piece, place], device,
                )

    def own(piece, place):
        pltpu.make_async_copy(
            features.at[:, feature_cols(me, PARTS[place], piece)],
            cols.at[piece, rows_of(me), place_cols(place)],
            in_recv.at[piece, place],
        ).start()

    def arrive(piece, kinds):
        for place in kinds:
            wait_for(cols.at[piece, :, place_cols(place)], in_recv.at[piece, place])

    def outer(index):
        return index + group * (index // 2)

    def inner(index):
        return index + 2

    def send_places(targets):
        for device in targets:
            ctx_start(places.at[me], places.at[me], place_send, place_recv, device)

    def signal(semaphore, device):
        pl.semaphore_signal(semaphore, inc=1, device_id={"ctx": device}, device_id_type=MESH)

    is_inner = (me >= 2) & (me < 2 + group)
    barrier = pltpu.get_barrier_semaphore()
    for copy in near[1:]:
        pl.semaphore_signal(barrier, inc=1, device_id={"mp": copy}, device_id_type=MESH)
    places[me] = jnp.concatenate([place_ref[...], target_ref[...], domain_ref[...]], axis=0)

    @pl.when(is_inner)
    def _():
        place = me - 2
        inside = [inner(lax.rem(place + step, group)) for step in range(1, group)]
        outside = [outer(lax.rem(place + step, group)) for step in range(group)]
        for device in inside:
            signal(barrier, device)
        pl.semaphore_wait(barrier, copies - 1 + group - 1)
        for device in outside:
            signal(barrier, device)
        send(0, (0, 1), inside)
        send_places(inside)
        pl.semaphore_wait(ready, group)
        signal(ready, jnp.where(me < group, me - 2, me + 2))
        send(0, (0, 1), outside)
        send_places(outside)
        send(1, (0, 1), around)
        for piece in range(pieces):
            send(piece, (2,), around)

    @pl.when(jnp.logical_not(is_inner))
    def _():
        place = jnp.where(me < 2, me, me - group)
        inside = [inner(lax.rem(place + step, group)) for step in range(group)]
        outside = [outer(lax.rem(place + step, group)) for step in range(1, group)]
        pl.semaphore_wait(barrier, copies - 1 + group)
        for device in inside:
            signal(ready, device)
        send(0, (0, 1), inside)
        send_places(inside)
        pl.semaphore_wait(ready, 1)
        send(0, (0, 1), outside)
        send_places(outside)
        send(1, (0, 1), around)
        for piece in range(pieces):
            send(piece, (2,), around)

    filter_copy = pltpu.make_async_copy(filter_hbm, filter_ref, filter_sem)
    filter_copy.start()
    for piece in range(pieces):
        for place in range(3):
            own(piece, place)

    make_tables(inner_ref, row_ref, forward, backward)
    filter_copy.wait()
    filter_spectrum(filter_ref, forward, filter_work, spectrum)
    seq_ref[pl.ds(0, 8), :] = jnp.zeros((8, seq_ref.shape[1]), F32)

    wait_for(places.at[pl.ds(0, others)], place_recv)
    build_picks(jnp.concatenate([places[d][0:1] for d in range(devices)], axis=1), pick_ref)
    base = core * half_width + me * channels

    @pl.loop(0, devices // 2)
    def _(step):
        kinds = lax.broadcasted_iota(jnp.int32, (WIDTH, rows_here), 0)
        match = kinds == places[core * (devices // 2) + step][2:3]
        domain_hot[:, rows_of(step)] = jnp.where(match, 1.0, 0.0).astype(BF16)

    @pl.loop(0, devices)
    def _(device):
        loader = places[device][1:2]
        wanted_ref[rows_of(device), :] = jnp.broadcast_to(loader - base, (rows_here, rows_here)).T

    for piece in range(pieces):
        here = pl.ds(piece * WIDTH, WIDTH)
        arrive(piece, (0, 1))
        order_rows(cols.at[piece], pick_ref, seq_ref, 0, 2 * WIDTH)
        short_and_outer(seq_ref, taps_ref, work, signal_ref, here)
        transform_product(spectrum, forward, backward, work, back_ref, here)
        long_and_direct(back_ref, signal_ref, skip_ref, total_ref, piece, here)

    lane = lax.broadcasted_iota(jnp.int32, (rows_here, WIDTH), 1)
    picker_col = lax.broadcasted_iota(jnp.int32, (8, 3 * WIDTH), 1) < 2 * WIDTH
    picker_row = lax.broadcasted_iota(jnp.int32, (8, 3 * WIDTH), 0)
    picker = (picker_col & (picker_row == 0)) | (~picker_col & (picker_row == 1))
    picker = jnp.where(picker, 1.0, 0.0).astype(BF16)

    def gate(piece, owner):
        here = pl.ds(piece * WIDTH, WIDTH)
        start = pl.multiple_of(owner * rows_here, rows_here)
        value = shorted_rows(seq_ref, taps_ref, start, rows_here, 2, 1, here)
        value = (value * total_ref[piece, rows_of(owner), :]).astype(out_ref.dtype)
        out_ref[piece, rows_of(owner), :] = value
        return value.astype(F32)

    def tally(piece, owner, value):
        rows = rows_of(owner)
        power = jnp.exp(value)
        hit = jnp.where(lane + piece * WIDTH == wanted_ref[rows, :], value, 0.0)
        if piece:
            power = power + exp_ref[rows, :]
            hit = hit + hit_ref[rows, :]
        if piece < pieces - 1:
            exp_ref[rows, :] = power
            hit_ref[rows, :] = hit
            return
        high, low = halves(power)
        terms_ref[rows, pl.ds(0, WIDTH)] = high
        terms_ref[rows, pl.ds(WIDTH, WIDTH)] = low
        terms_ref[rows, pl.ds(2 * WIDTH, WIDTH)] = hit.astype(BF16)

    def mixed_part(piece):
        start = pl.multiple_of(me * channels + piece * WIDTH, WIDTH)
        return mixed_ref.at[:, pl.ds(start, WIDTH)]

    def give(piece, device):
        ctx_start(
            out_ref.at[piece, rows_of(device), :], mixed_part(piece), out_send, out_recv, device
        )

    def keep(piece):
        pltpu.make_async_copy(out_ref.at[piece, rows_of(me), :], mixed_part(piece), out_recv).start()

    for piece in range(pieces - 1):
        arrive(piece, (2,))
        order_rows(cols.at[piece], pick_ref, seq_ref, 2 * WIDTH, WIDTH)

        @pl.loop(0, others)
        def _(step, piece=piece):
            device = peer(step)
            gate(piece, device)
            give(piece, device)

        gate(piece, me)
        keep(piece)

        @pl.loop(0, devices)
        def _(device, piece=piece):
            tally(piece, device, out_ref[piece, rows_of(device), :].astype(F32))

    piece = pieces - 1
    arrive(piece, (2,))
    order_rows(cols.at[piece], pick_ref, seq_ref, 2 * WIDTH, WIDTH)

    def half_sums(half):
        @pl.loop(0, devices // 2)
        def _(step):
            owner = half * (devices // 2) + step
            tally(piece, owner, gate(piece, owner))

        rows = pl.ds(pl.multiple_of(half * span, span), span)
        return stacked_dot(picker, terms_ref[rows, :], (((1,), (1,)), ((), ())))[0:2]

    def core_copy(source, target, send, recv):
        return pltpu.make_async_remote_copy(
            src_ref=source, dst_ref=target, send_sem=send, recv_sem=recv,
            device_id={"mp": partner}, device_id_type=MESH,
        )

    half_out[...] = half_sums(1 - core)
    half_copy = core_copy(half_out, half_in, half_send, half_recv)
    half_copy.start()
    half_own = half_sums(core)
    half_copy.wait_recv()
    half_theirs = half_in[...]
    chip = me * MODELS + model_index
    gathered[chip] = half_own + half_theirs
    def tell(device, copy):
        pltpu.make_async_remote_copy(
            src_ref=gathered.at[chip], dst_ref=gathered.at[chip],
            send_sem=given_send, recv_sem=given_recv,
            device_id={"ctx": device, "mp": copy}, device_id_type=MESH,
        ).start()

    for device in around:
        for other in range(MODELS):
            tell(device, near[2 * other])
    tell(me, near[2])
    for device in around:
        give(piece, device)
    keep(piece)

    wait_for(features.at[:, pl.ds(0, 3 * channels * others)], in_send)
    wait_for(places.at[pl.ds(0, others)], place_send)
    half_copy.wait_send()
    wait_for(gathered.at[pl.ds(0, MODELS * devices - 1)], given_recv)
    losses = []
    for model in range(MODELS):
        both = gathered[model]
        for device in range(1, devices):
            both = both + gathered[device * MODELS + model]
        losses.append(jnp.log(both[0:1]) - both[1:2])
    excess = jnp.broadcast_to(jnp.maximum(losses[0] - losses[1], 0.0), (8, span))
    high, low = halves(excess)
    top = lax.broadcasted_iota(jnp.int32, (8, span), 0)
    excess = jnp.where(top == 0, high.astype(F32), jnp.where(top == 1, low.astype(F32), 0.0))
    sums = stacked_dot(excess.astype(BF16), domain_hot[...], (((1,), (1,)), ((), ())))
    domain_sums[core] = sums[0:1] + sums[1:2]
    sum_copy = core_copy(domain_sums.at[core], domain_sums.at[core], sum_send, sum_recv)
    sum_copy.start()
    wait_for(gathered.at[pl.ds(0, MODELS * devices - 1)], given_send)
    sum_copy.wait()
    sums = domain_sums[0] + domain_sums[1]
    sums_ref[...] = sums[:, : sums_ref.shape[1]]
    wait_for(mixed_ref, out_recv)
    wait_for(out_ref.at[:, pl.ds(0, rows_here * others), :], out_send)


def last_kernel(mixed_ref, sums_ref, tokens_ref, out_ref, excess_ref, ratio_ref, sems):
    mixed_copy = pltpu.make_async_copy(mixed_ref, out_ref, sems.at[0])
    mixed_copy.start()
    ratio_ref[...] = sums_ref[...] / tokens_ref[...].astype(F32)
    ratio_copy = pltpu.make_async_copy(ratio_ref, excess_ref, sems.at[1])
    ratio_copy.start()
    mixed_copy.wait()
    ratio_copy.wait()


def body(features, destination, targets, domains, domain_tokens, short_filter, long_filter, skip):
    devices = lax.axis_size("ctx")
    copies = lax.axis_size("mp")
    rows_here = features.shape[0]
    length = devices * rows_here
    half_width = features.shape[1] // 3
    channels = half_width // devices
    if length != 8 * INNER or rows_here != 128 or channels != 256 or copies != 4 or domain_tokens.shape[0] > WIDTH:
        return general_body(
            features, destination, targets, domains, domain_tokens, short_filter, long_filter, skip
        )
    pieces = channels // WIDTH
    count = domain_tokens.shape[0]
    vmem = pl.BlockSpec(memory_space=pltpu.VMEM)
    hbm = pl.BlockSpec(memory_space=pl.ANY)
    big = (FREQS, 2 * INNER, 6 * INNER)
    dma = pltpu.SemaphoreType.DMA
    mixed, sums = pl.pallas_call(
        functools.partial(whole_kernel, devices, copies, pieces),
        out_shape=[
            pltpu.VMEM((rows_here, half_width), BF16),
            pltpu.VMEM((1, count), F32),
        ],
        in_specs=[hbm, vmem, vmem, vmem, vmem, hbm, vmem, vmem, vmem],
        out_specs=[vmem, vmem],
        scratch_shapes=[
            pltpu.VMEM((1, channels, length), F32),
            pltpu.VMEM((pieces, length, 3 * WIDTH), BF16),
            pltpu.VMEM((devices, 3, rows_here), jnp.int32),
            pltpu.VMEM((length, length), BF16),
            pltpu.VMEM((length, WIDTH), jnp.int32),
            pltpu.VMEM((FREQS, 2 * INNER, channels), F32),
            pltpu.VMEM(big, BF16),
            pltpu.VMEM(big, BF16),
            pltpu.VMEM((FREQS, channels, 6 * INNER), BF16),
            pltpu.VMEM((length + 8, 3 * WIDTH), F32),
            pltpu.VMEM((FREQS, 6 * INNER, WIDTH), BF16),
            pltpu.VMEM((FREQS, 2 * INNER, WIDTH), F32),
            pltpu.VMEM((length, WIDTH), F32),
            pltpu.VMEM((pieces, length, WIDTH), F32),
            pltpu.VMEM((pieces, length, WIDTH), BF16),
            pltpu.VMEM((length, WIDTH), F32),
            pltpu.VMEM((length, WIDTH), F32),
            pltpu.VMEM((length, 3 * WIDTH), BF16),
            pltpu.VMEM((2, length // 2), F32),
            pltpu.VMEM((2, length // 2), F32),
            pltpu.VMEM((MODELS * devices, 2, length // 2), F32),
            pltpu.VMEM((WIDTH, length // 2), BF16),
            pltpu.VMEM((2, 1, WIDTH), F32),
            dma,
            dma((pieces, 3)),
            dma,
            dma,
            dma,
            dma,
            dma,
            dma,
            dma,
            dma,
            dma,
            dma,
            dma,
            pltpu.SemaphoreType.REGULAR,
        ],
        compiler_params=pltpu.CompilerParams(
            vmem_limit_bytes=LIMIT, collective_id=0, has_side_effects=True
        ),
    )(
        features, destination.reshape(1, rows_here), targets.reshape(1, rows_here),
        domains.reshape(1, rows_here),
        short_filter.transpose(0, 2, 1, 3).reshape(-1, 1, channels), long_filter, skip,
        *table_inputs(),
    )
    mixed, excess = pl.pallas_call(
        last_kernel,
        out_shape=[
            jax.ShapeDtypeStruct((rows_here, half_width), BF16),
            jax.ShapeDtypeStruct((1, count), F32),
        ],
        in_specs=[vmem, vmem, vmem],
        out_specs=[hbm, hbm],
        scratch_shapes=[pltpu.VMEM((1, count), F32), dma((2,))],
        compiler_params=pltpu.CompilerParams(vmem_limit_bytes=2**20),
    )(mixed, sums, domain_tokens.reshape(1, count))
    return (mixed, excess.reshape(count))


def solution(mesh):
    return jax.shard_map(
        body,
        mesh=mesh,
        in_specs=(
            P("ctx", "mp"),
            P("ctx"),
            P("ctx"),
            P("ctx"),
            P(),
            P(None, "mp", None, "ctx"),
            P("mp", "ctx", None),
            P("mp", "ctx"),
        ),
        out_specs=(P("ctx", "mp"), P()),
        check_vma=False,
    )
```

```python
import functools
import math

import jax
import jax.numpy as jnp
import numpy as np
from jax import lax
from jax.experimental import pallas as pl
from jax.experimental.pallas import tpu as pltpu
from jax.sharding import PartitionSpec as P

MODELS = 2


HIGHEST = lax.Precision.HIGHEST


def dft_tables(count, limit, modulus):
    row_index = jnp.arange(count, dtype=jnp.int32)[:, None]
    col_index = jnp.arange(limit, dtype=jnp.int32)[None, :]
    angle = 2.0 * math.pi / modulus * (row_index * col_index % modulus).astype(jnp.float32)
    return (jnp.cos(angle), jnp.sin(angle))


def forward_transform(signal, outer_cos, outer_sin, twist_cos, twist_sin, inner_cos, inner_sin):
    real_a = jnp.einsum("kp,cpq->ckq", outer_cos, signal, precision=HIGHEST)
    imag_a = -jnp.einsum("kp,cpq->ckq", outer_sin, signal, precision=HIGHEST)
    real_b = real_a * twist_cos + imag_a * twist_sin
    imag_b = imag_a * twist_cos - real_a * twist_sin
    real_c = jnp.einsum("ckq,qj->ckj", real_b, inner_cos, precision=HIGHEST) + jnp.einsum(
        "ckq,qj->ckj", imag_b, inner_sin, precision=HIGHEST
    )
    imag_c = jnp.einsum("ckq,qj->ckj", imag_b, inner_cos, precision=HIGHEST) - jnp.einsum(
        "ckq,qj->ckj", real_b, inner_sin, precision=HIGHEST
    )
    return (real_c, imag_c)


def causal_convolution(signal, kernel):
    channels, length = signal.shape
    inner_size = 128
    outer_size = 2 * length // inner_size
    half_outer = outer_size // 2
    outer_cos, outer_sin = dft_tables(outer_size, half_outer, outer_size)
    twist_cos, twist_sin = dft_tables(outer_size, inner_size, 2 * length)
    inner_cos, inner_sin = dft_tables(inner_size, inner_size, inner_size)
    sig_re, sig_im = forward_transform(
        signal.reshape(channels, half_outer, inner_size),
        outer_cos,
        outer_sin,
        twist_cos,
        twist_sin,
        inner_cos,
        inner_sin,
    )
    ker_re, ker_im = forward_transform(
        kernel.reshape(channels, half_outer, inner_size),
        outer_cos,
        outer_sin,
        twist_cos,
        twist_sin,
        inner_cos,
        inner_sin,
    )
    prod_re = sig_re * ker_re - sig_im * ker_im
    prod_im = sig_re * ker_im + sig_im * ker_re
    back_re = jnp.einsum("ckj,qj->ckq", prod_re, inner_cos, precision=HIGHEST) - jnp.einsum(
        "ckj,qj->ckq", prod_im, inner_sin, precision=HIGHEST
    )
    back_im = jnp.einsum("ckj,qj->ckq", prod_im, inner_cos, precision=HIGHEST) + jnp.einsum(
        "ckj,qj->ckq", prod_re, inner_sin, precision=HIGHEST
    )
    turned_re = back_re * twist_cos - back_im * twist_sin
    turned_im = back_im * twist_cos + back_re * twist_sin
    result = jnp.einsum("kp,ckq->cpq", outer_cos, turned_re, precision=HIGHEST) - jnp.einsum(
        "kp,ckq->cpq", outer_sin, turned_im, precision=HIGHEST
    )
    return (result / (2.0 * length)).reshape(channels, length)


def general_body(features, destination, targets, domains, domain_tokens, short_filter, long_filter, skip):
    devices = lax.axis_size("ctx")
    rows_here = features.shape[0]
    length = devices * rows_here
    half_width = features.shape[1] // 3
    channels = half_width // devices
    capacity = 5 * rows_here // (2 * devices)
    owner_dev = destination // rows_here
    offset = destination % rows_here
    order = jnp.arange(rows_here, dtype=jnp.int32)
    ahead = (owner_dev[:, None] == owner_dev[None, :]) & (order[None, :] < order[:, None])
    slot_rank = jnp.sum(ahead.astype(jnp.int32), axis=1)
    buffer = (
        jnp.zeros((devices, capacity, 3 * half_width), features.dtype)
        .at[owner_dev, slot_rank]
        .set(features)
    )
    places = (
        jnp.full((devices, capacity), rows_here, jnp.int32).at[owner_dev, slot_rank].set(offset)
    )
    arrived, arrived_places = (
        lax.all_to_all(buffer, "ctx", split_axis=0, concat_axis=0, tiled=True),
        lax.all_to_all(places, "ctx", split_axis=0, concat_axis=0, tiled=True),
    )
    ordered = jnp.zeros((rows_here + 1, 3 * half_width), features.dtype)
    ordered = ordered.at[arrived_places.reshape(-1)].set(arrived.reshape(-1, 3 * half_width))[
        :rows_here
    ]
    blocks = ordered.reshape(rows_here, 3, devices, channels).transpose(2, 1, 3, 0)
    columns = lax.all_to_all(blocks, "ctx", split_axis=0, concat_axis=3, tiled=True)[0]
    inputs = columns.astype(jnp.float32)
    tap_weights = short_filter[:, 0]
    shorted = jnp.zeros_like(inputs)
    for tap_index in range(tap_weights.shape[0]):
        shifted = jnp.pad(inputs, ((0, 0), (0, 0), (tap_index, 0)))[:, :, :length]
        shorted = shorted + tap_weights[tap_index][:, :, None] * shifted
    signal = shorted[0] * shorted[2]
    long_part = causal_convolution(signal, long_filter[0])
    output_cols = (shorted[1] * (long_part + skip[0][:, None] * signal)).astype(jnp.bfloat16)
    returned = lax.all_to_all(
        output_cols.reshape(channels, devices, rows_here),
        "ctx",
        split_axis=1,
        concat_axis=0,
        tiled=True,
    )
    mixed = returned.reshape(half_width, rows_here).T
    copy_index = lax.axis_index("mp")
    model_index = copy_index // 2
    half_index = copy_index % 2
    values = mixed.astype(jnp.float32)
    part_exp = jnp.sum(jnp.exp(values), axis=1)
    local_target = targets - half_index * half_width
    inside = (local_target >= 0) & (local_target < half_width)
    picked = jnp.take_along_axis(
        values, jnp.clip(local_target, 0, half_width - 1)[:, None], axis=1
    )[:, 0]
    part_target = jnp.where(inside, picked, 0.0)
    is_model = jnp.arange(MODELS, dtype=jnp.int32)[:, None] == model_index
    exp_terms = jnp.where(is_model, part_exp[None, :], 0.0)
    target_terms = jnp.where(is_model, part_target[None, :], 0.0)
    total_exp, total_target = lax.psum((exp_terms, target_terms), "mp")
    losses = jnp.log(total_exp) - total_target
    token_excess = jnp.maximum(losses[0] - losses[1], 0.0)
    domain_count = domain_tokens.shape[0]
    in_domain = domains[None, :] == jnp.arange(domain_count, dtype=jnp.int32)[:, None]
    partial_sums = jnp.sum(jnp.where(in_domain, token_excess[None, :], 0.0), axis=1)
    domain_sums = lax.psum(partial_sums, "ctx")
    return (mixed, domain_sums / domain_tokens.astype(jnp.float32))


INNER = 128
OUTER = 16
FREQS = OUTER // 2 + 1
BF16 = jnp.bfloat16
F32 = jnp.float32


def weighted(terms):
    total = None
    for coef, value in terms:
        if value is None or abs(coef) < 1e-9:
            continue
        if abs(abs(coef) - 1.0) < 1e-9:
            term = value
            if coef < 0:
                total = -term if total is None else total - term
                continue
        else:
            term = coef * value
        total = term if total is None else total + term
    return total


def outer_forward(blocks):
    real, imag = [None] * FREQS, [None] * FREQS
    for k in range(FREQS // 2 + 1):
        angle = [2.0 * math.pi * p * k / OUTER for p in range(8)]
        parts = []
        for first in (0, 1):
            picks = range(first, 8, 2)
            parts.append(weighted([(math.cos(angle[p]), blocks[p]) for p in picks]))
            parts.append(weighted([(-math.sin(angle[p]), blocks[p]) for p in picks]))
        real_even, imag_even, real_odd, imag_odd = parts
        real[k] = weighted([(1.0, real_even), (1.0, real_odd)])
        imag[k] = weighted([(1.0, imag_even), (1.0, imag_odd)])
        if k < 4:
            real[8 - k] = weighted([(1.0, real_even), (-1.0, real_odd)])
            imag[8 - k] = weighted([(-1.0, imag_even), (1.0, imag_odd)])
    return real, imag


def outer_backward(real, imag):
    sums = {}
    for sign in (1.0, -1.0):
        sums[sign] = [
            (
                weighted([(1.0, real[k]), (sign, real[8 - k])]),
                weighted([(1.0, imag[k]), (-sign, imag[8 - k])]) if k else None,
            )
            for k in range(4)
        ]
    blocks = []
    for a in range(8):
        sign = 1.0 if a % 2 == 0 else -1.0
        terms = [(1.0, sums[sign][0][0])]
        for k in range(1, 4):
            angle = 2.0 * math.pi * k * a / OUTER
            terms.append((math.cos(angle), sums[sign][k][0]))
            terms.append((-math.sin(angle), sums[sign][k][1]))
        terms.append((math.cos(math.pi * a / 2), real[4]))
        terms.append((-math.sin(math.pi * a / 2), imag[4]))
        blocks.append(weighted(terms))
    return blocks


def halves(value):
    high = value.astype(BF16)
    return high, (value - high.astype(F32)).astype(BF16)


def stacked_dot(left, right, dims=(((1,), (0,)), ((), ()))):
    return lax.dot_general(left, right, dims, preferred_element_type=F32)


def table_inputs():
    index = np.arange(INNER)
    inner = 2.0 * np.pi * (np.outer(index, index) % INNER) / INNER
    twist = 2.0 * np.pi * np.outer(np.arange(FREQS), index) / (OUTER * INNER)
    inner_tab = np.stack([np.cos(inner), np.sin(inner)]).astype(np.float32)
    row_tab = np.stack([np.cos(twist), np.sin(twist)])[:, :, None, :].astype(np.float32)
    return jnp.asarray(inner_tab), jnp.asarray(row_tab)


def make_tables(inner_ref, row_ref, forward, backward):
    lower, upper = pl.ds(0, INNER), pl.ds(INNER, INNER)

    def store(ref, k, cos, sin, flip):
        cos_parts, sin_parts = halves(cos), halves(sin)
        for place, kind in ((0, 0), (1, 0), (2, 1)):
            c, s = cos_parts[kind], sin_parts[kind]
            first = pl.ds(place * 2 * INNER, INNER)
            second = pl.ds(place * 2 * INNER + INNER, INNER)
            ref[k, lower, first] = c
            ref[k, lower, second] = -s if flip else s
            ref[k, upper, first] = s if flip else -s
            ref[k, upper, second] = c

    def step(k, carry):
        base_cos, base_sin = inner_ref[0], inner_ref[1]
        row_cos, row_sin = row_ref[0, k], row_ref[1, k]
        cos, sin = base_cos * row_cos - base_sin * row_sin, base_sin * row_cos + base_cos * row_sin
        store(forward, k, cos, sin, False)
        col_cos = jnp.broadcast_to(row_cos, (INNER, INNER)).T
        col_sin = jnp.broadcast_to(row_sin, (INNER, INNER)).T
        cos, sin = base_cos * col_cos - base_sin * col_sin, base_sin * col_cos + base_cos * col_sin
        store(backward, k, cos, sin, True)
        return carry

    lax.fori_loop(0, FREQS, step, 0)


def filter_spectrum(filter_ref, forward, work, spectrum_ref):
    channels = filter_ref.shape[1]

    def stage(block, carry):
        rows = pl.ds(pl.multiple_of(block * 16, 16), 16)
        real, imag = outer_forward([filter_ref[0, rows, pl.ds(p * INNER, INNER)] for p in range(8)])
        for k in range(FREQS):
            for place, part in ((0, real[k]), (INNER, imag[k])):
                part = jnp.zeros((16, INNER), F32) if part is None else part
                high, low = halves(part)
                work[k, rows, pl.ds(place, INNER)] = high
                work[k, rows, pl.ds(place + 2 * INNER, INNER)] = low
                work[k, rows, pl.ds(place + 4 * INNER, INNER)] = high
        return carry

    lax.fori_loop(0, channels // 16, stage, 0)

    def transform(k, carry):
        scale = jnp.where((k == 0) | (k == FREQS - 1), 0.5, 1.0) * (2.0 / (OUTER * INNER))
        spectrum_ref[k] = scale * stacked_dot(forward[k], work[k], (((1,), (1,)), ((), ())))
        return carry

    lax.fori_loop(0, FREQS, transform, 0)


WIDTH = 128


def build_picks(places, pick_ref):
    length = pick_ref.shape[0]

    def step(block, carry):
        here = lax.broadcasted_iota(jnp.int32, (128, length), 0) + block * 128
        rows = pl.ds(pl.multiple_of(block * 128, 128), 128)
        pick_ref[rows, :] = jnp.where(here == places, 1.0, 0.0).astype(BF16)
        return carry

    lax.fori_loop(0, length // 128, step, 0)


def order_rows(cols_ref, pick_ref, seq_ref, first, width):
    length = cols_ref.shape[0]

    def step(block, carry):
        rows = pl.multiple_of(block * 256, 256)
        seq_ref[pl.ds(rows + 8, 256), pl.ds(first, width)] = jnp.dot(
            pick_ref[pl.ds(rows, 256), :], cols_ref[:, pl.ds(first, width)],
            preferred_element_type=F32,
        )
        return carry

    lax.fori_loop(0, length // 256, step, 0, unroll=True)


def shorted_rows(seq_ref, taps_ref, start, count, place, part, here):
    window = seq_ref[pl.ds(start, count + 8), pl.ds(place * WIDTH, WIDTH)]
    total = None
    for tap in range(taps_ref.shape[0] // 3):
        weight = taps_ref[tap * 3 + part, :, here]
        term = weight * window[8 - tap : 8 + count - tap]
        total = term if total is None else total + term
    return total


def short_and_outer(seq_ref, taps_ref, work, signal_ref, here):
    def stage(block, carry):
        offset = pl.multiple_of(block * 16, 16)
        signals = []
        for p in range(8):
            rows = pl.ds(p * INNER + offset, 16)
            start = pl.multiple_of(p * INNER + block * 16, 16)
            signal = shorted_rows(seq_ref, taps_ref, start, 16, 0, 0, here) * shorted_rows(
                seq_ref, taps_ref, start, 16, 1, 2, here
            )
            signal_ref[rows, :] = signal
            signals.append(signal)
        real, imag = outer_forward(signals)
        for k in range(FREQS):
            for place, part in ((0, real[k]), (INNER, imag[k])):
                part = jnp.zeros((16, WIDTH), F32) if part is None else part
                high, low = halves(part)
                work[k, pl.ds(place + offset, 16), :] = high
                work[k, pl.ds(place + 2 * INNER + offset, 16), :] = low
                work[k, pl.ds(place + 4 * INNER + offset, 16), :] = high
        return carry

    lax.fori_loop(0, INNER // 16, stage, 0)


def transform_product(spectrum_ref, forward, backward, work, back_ref, here):
    def step(k, carry):
        value = stacked_dot(forward[k], work[k])
        real, imag = value[:INNER], value[INNER:]
        other = spectrum_ref[k, :, here]
        other_real, other_imag = other[:INNER], other[INNER:]
        product = jnp.concatenate(
            [real * other_real - imag * other_imag, real * other_imag + imag * other_real], axis=0
        )
        high, low = halves(product)
        back_ref[k] = stacked_dot(backward[k], jnp.concatenate([high, low, high], axis=0))
        return carry

    lax.fori_loop(0, FREQS, step, 0, unroll=3)


def long_and_direct(back_ref, signal_ref, skip_ref, total_ref, piece, here):
    def step(block, carry):
        offset = pl.multiple_of(block * 16, 16)
        real = [back_ref[k, pl.ds(offset, 16), :] for k in range(FREQS)]
        imag = [
            back_ref[k, pl.ds(INNER + offset, 16), :] if 0 < k < FREQS - 1 else None
            for k in range(FREQS)
        ]
        direct = skip_ref[pl.ds(0, 1), here]
        for p, long_part in enumerate(outer_backward(real, imag)):
            rows = pl.ds(p * INNER + offset, 16)
            total_ref[piece, rows, :] = long_part + direct * signal_ref[rows, :]
        return carry

    lax.fori_loop(0, INNER // 16, step, 0)


LIMIT = 56 * 2**20
MESH = pl.DeviceIdType.MESH
PARTS = (0, 2, 1)


def whole_kernel(
    devices, copies, pieces,
    features, place_ref, target_ref, domain_ref, taps_ref, filter_hbm, skip_ref,
    inner_ref, row_ref,
    mixed_ref, sums_ref,
    filter_ref, cols, places, pick_ref, wanted_ref, spectrum, forward, backward, filter_work,
    seq_ref, work, back_ref, signal_ref, total_ref, out_ref, exp_ref, hit_ref,
    terms_ref, half_out, half_in, gathered, domain_hot, domain_sums,
    in_send, in_recv, place_send, place_recv, out_send, out_recv,
    given_send, given_recv, half_send, half_recv, sum_send, sum_recv, filter_sem, ready,
):
    me = lax.axis_index("ctx")
    copy_index = lax.axis_index("mp")
    rows_here, half_width = mixed_ref.shape
    channels = half_width // devices
    others = devices - 1
    core = lax.rem(copy_index, 2)
    model_index = copy_index // 2
    partner = copy_index + 1 - 2 * core
    span = rows_here * devices // 2
    group = devices // 2
    around = [lax.rem(me + step, devices) for step in range(1, devices)]
    near = [lax.rem(copy_index + step, copies) for step in range(copies)]

    def rows_of(device):
        return pl.ds(pl.multiple_of(device * rows_here, rows_here), rows_here)

    def feature_cols(device, part, piece):
        start = part * half_width + device * channels + piece * WIDTH
        return pl.ds(pl.multiple_of(start, WIDTH), WIDTH)

    def place_cols(place):
        return pl.ds(place * WIDTH, WIDTH)

    def ctx_start(source, target, send, recv, device):
        pltpu.make_async_remote_copy(
            src_ref=source, dst_ref=target, send_sem=send, recv_sem=recv,
            device_id={"ctx": device}, device_id_type=MESH,
        ).start()

    def wait_for(ref, sem):
        pltpu.make_async_copy(ref, ref, sem).wait()

    def send(piece, kinds, targets):
        for device in targets:
            for place in kinds:
                ctx_start(
                    features.at[:, feature_cols(device, PARTS[place], piece)],
                    cols.at[piece, rows_of(me), place_cols(place)],
                    in_send, in_recv.at[piece, place], device,
                )

    def own(piece, place):
        pltpu.make_async_copy(
            features.at[:, feature_cols(me, PARTS[place], piece)],
            cols.at[piece, rows_of(me), place_cols(place)],
            in_recv.at[piece, place],
        ).start()

    def arrive(piece, kinds):
        for place in kinds:
            wait_for(cols.at[piece, :, place_cols(place)], in_recv.at[piece, place])

    def outer(index):
        return index + group * (index // 2)

    def inner(index):
        return index + 2

    def send_places(targets):
        for device in targets:
            ctx_start(places.at[me], places.at[me], place_send, place_recv, device)

    def signal(semaphore, device):
        pl.semaphore_signal(semaphore, inc=1, device_id={"ctx": device}, device_id_type=MESH)

    is_inner = (me >= 2) & (me < 2 + group)
    barrier = pltpu.get_barrier_semaphore()
    for copy in near[1:]:
        pl.semaphore_signal(barrier, inc=1, device_id={"mp": copy}, device_id_type=MESH)
    places[me] = jnp.concatenate([place_ref[...], target_ref[...], domain_ref[...]], axis=0)

    @pl.when(is_inner)
    def _():
        place = me - 2
        inside = [inner(lax.rem(place + step, group)) for step in range(1, group)]
        outside = [outer(lax.rem(place + step, group)) for step in range(group)]
        for device in inside:
            signal(barrier, device)
        pl.semaphore_wait(barrier, copies - 1 + group - 1)
        for device in outside:
            signal(barrier, device)
        send(0, (0, 1), inside)
        send_places(inside)
        pl.semaphore_wait(ready, group)
        signal(ready, jnp.where(me < group, me - 2, me + 2))
        send(0, (0, 1), outside)
        send_places(outside)
        send(1, (0, 1), around)
        for piece in range(pieces):
            send(piece, (2,), around)

    @pl.when(jnp.logical_not(is_inner))
    def _():
        place = jnp.where(me < 2, me, me - group)
        inside = [inner(lax.rem(place + step, group)) for step in range(group)]
        outside = [outer(lax.rem(place + step, group)) for step in range(1, group)]
        pl.semaphore_wait(barrier, copies - 1 + group)
        for device in inside:
            signal(ready, device)
        send(0, (0, 1), inside)
        send_places(inside)
        pl.semaphore_wait(ready, 1)
        send(0, (0, 1), outside)
        send_places(outside)
        send(1, (0, 1), around)
        for piece in range(pieces):
            send(piece, (2,), around)

    filter_copy = pltpu.make_async_copy(filter_hbm, filter_ref, filter_sem)
    filter_copy.start()
    for piece in range(pieces):
        for place in range(3):
            own(piece, place)

    make_tables(inner_ref, row_ref, forward, backward)
    filter_copy.wait()
    filter_spectrum(filter_ref, forward, filter_work, spectrum)
    seq_ref[pl.ds(0, 8), :] = jnp.zeros((8, seq_ref.shape[1]), F32)

    wait_for(places.at[pl.ds(0, others)], place_recv)
    build_picks(jnp.concatenate([places[d][0:1] for d in range(devices)], axis=1), pick_ref)
    base = core * half_width + me * channels

    @pl.loop(0, devices // 2)
    def _(step):
        kinds = lax.broadcasted_iota(jnp.int32, (WIDTH, rows_here), 0)
        match = kinds == places[core * (devices // 2) + step][2:3]
        domain_hot[:, rows_of(step)] = jnp.where(match, 1.0, 0.0).astype(BF16)

    @pl.loop(0, devices)
    def _(device):
        loader = places[device][1:2]
        wanted_ref[rows_of(device), :] = jnp.broadcast_to(loader - base, (rows_here, rows_here)).T

    for piece in range(pieces):
        here = pl.ds(piece * WIDTH, WIDTH)
        arrive(piece, (0, 1))
        order_rows(cols.at[piece], pick_ref, seq_ref, 0, 2 * WIDTH)
        short_and_outer(seq_ref, taps_ref, work, signal_ref, here)
        transform_product(spectrum, forward, backward, work, back_ref, here)
        long_and_direct(back_ref, signal_ref, skip_ref, total_ref, piece, here)

    lane = lax.broadcasted_iota(jnp.int32, (rows_here, WIDTH), 1)
    picker_col = lax.broadcasted_iota(jnp.int32, (8, 3 * WIDTH), 1) < 2 * WIDTH
    picker_row = lax.broadcasted_iota(jnp.int32, (8, 3 * WIDTH), 0)
    picker = (picker_col & (picker_row == 0)) | (~picker_col & (picker_row == 1))
    picker = jnp.where(picker, 1.0, 0.0).astype(BF16)

    def gate(piece, owner):
        here = pl.ds(piece * WIDTH, WIDTH)
        start = pl.multiple_of(owner * rows_here, rows_here)
        value = shorted_rows(seq_ref, taps_ref, start, rows_here, 2, 1, here)
        value = (value * total_ref[piece, rows_of(owner), :]).astype(out_ref.dtype)
        out_ref[piece, rows_of(owner), :] = value
        return value.astype(F32)

    def tally(piece, owner, value):
        rows = rows_of(owner)
        power = jnp.exp(value)
        hit = jnp.where(lane + piece * WIDTH == wanted_ref[rows, :], value, 0.0)
        if piece:
            power = power + exp_ref[rows, :]
            hit = hit + hit_ref[rows, :]
        if piece < pieces - 1:
            exp_ref[rows, :] = power
            hit_ref[rows, :] = hit
            return
        high, low = halves(power)
        terms_ref[rows, pl.ds(0, WIDTH)] = high
        terms_ref[rows, pl.ds(WIDTH, WIDTH)] = low
        terms_ref[rows, pl.ds(2 * WIDTH, WIDTH)] = hit.astype(BF16)

    def mixed_part(piece):
        start = pl.multiple_of(me * channels + piece * WIDTH, WIDTH)
        return mixed_ref.at[:, pl.ds(start, WIDTH)]

    def give(piece, device):
        ctx_start(
            out_ref.at[piece, rows_of(device), :], mixed_part(piece), out_send, out_recv, device
        )

    def keep(piece):
        pltpu.make_async_copy(out_ref.at[piece, rows_of(me), :], mixed_part(piece), out_recv).start()

    for piece in range(pieces - 1):
        arrive(piece, (2,))
        order_rows(cols.at[piece], pick_ref, seq_ref, 2 * WIDTH, WIDTH)

        @pl.loop(0, others)
        def _(step, piece=piece):
            device = lax.rem(me + 1 + step, devices)
            gate(piece, device)
            give(piece, device)

        gate(piece, me)
        keep(piece)

        @pl.loop(0, devices)
        def _(device, piece=piece):
            tally(piece, device, out_ref[piece, rows_of(device), :].astype(F32))

    piece = pieces - 1
    arrive(piece, (2,))
    order_rows(cols.at[piece], pick_ref, seq_ref, 2 * WIDTH, WIDTH)

    def half_sums(half):
        @pl.loop(0, devices // 2)
        def _(step):
            owner = half * (devices // 2) + step
            tally(piece, owner, gate(piece, owner))

        rows = pl.ds(pl.multiple_of(half * span, span), span)
        return stacked_dot(picker, terms_ref[rows, :], (((1,), (1,)), ((), ())))[0:2]

    def core_copy(source, target, send, recv):
        return pltpu.make_async_remote_copy(
            src_ref=source, dst_ref=target, send_sem=send, recv_sem=recv,
            device_id={"mp": partner}, device_id_type=MESH,
        )

    half_out[...] = half_sums(1 - core)
    half_copy = core_copy(half_out, half_in, half_send, half_recv)
    half_copy.start()
    half_own = half_sums(core)
    half_copy.wait_recv()
    half_theirs = half_in[...]
    chip = me * MODELS + model_index
    gathered[chip] = half_own + half_theirs
    def tell(device, copy):
        pltpu.make_async_remote_copy(
            src_ref=gathered.at[chip], dst_ref=gathered.at[chip],
            send_sem=given_send, recv_sem=given_recv,
            device_id={"ctx": device, "mp": copy}, device_id_type=MESH,
        ).start()

    for device in around:
        for other in range(MODELS):
            tell(device, near[2 * other])
    tell(me, near[2])
    for device in around:
        give(piece, device)
    keep(piece)

    wait_for(features.at[:, pl.ds(0, 3 * channels * others)], in_send)
    wait_for(places.at[pl.ds(0, others)], place_send)
    half_copy.wait_send()
    wait_for(gathered.at[pl.ds(0, MODELS * devices - 1)], given_recv)
    losses = []
    for model in range(MODELS):
        both = gathered[model]
        for device in range(1, devices):
            both = both + gathered[device * MODELS + model]
        losses.append(jnp.log(both[0:1]) - both[1:2])
    excess = jnp.broadcast_to(jnp.maximum(losses[0] - losses[1], 0.0), (8, span))
    high, low = halves(excess)
    top = lax.broadcasted_iota(jnp.int32, (8, span), 0)
    excess = jnp.where(top == 0, high.astype(F32), jnp.where(top == 1, low.astype(F32), 0.0))
    sums = stacked_dot(excess.astype(BF16), domain_hot[...], (((1,), (1,)), ((), ())))
    domain_sums[core] = sums[0:1] + sums[1:2]
    sum_copy = core_copy(domain_sums.at[core], domain_sums.at[core], sum_send, sum_recv)
    sum_copy.start()
    wait_for(gathered.at[pl.ds(0, MODELS * devices - 1)], given_send)
    sum_copy.wait()
    sums = domain_sums[0] + domain_sums[1]
    sums_ref[...] = sums[:, : sums_ref.shape[1]]
    wait_for(mixed_ref, out_recv)
    wait_for(out_ref.at[:, pl.ds(0, rows_here * others), :], out_send)


def last_kernel(mixed_ref, sums_ref, tokens_ref, out_ref, excess_ref, ratio_ref, sems):
    mixed_copy = pltpu.make_async_copy(mixed_ref, out_ref, sems.at[0])
    mixed_copy.start()
    ratio_ref[...] = sums_ref[...] / tokens_ref[...].astype(F32)
    ratio_copy = pltpu.make_async_copy(ratio_ref, excess_ref, sems.at[1])
    ratio_copy.start()
    mixed_copy.wait()
    ratio_copy.wait()


def body(features, destination, targets, domains, domain_tokens, short_filter, long_filter, skip):
    devices = lax.axis_size("ctx")
    copies = lax.axis_size("mp")
    rows_here = features.shape[0]
    length = devices * rows_here
    half_width = features.shape[1] // 3
    channels = half_width // devices
    if length != 8 * INNER or rows_here != 128 or channels != 256 or copies != 4 or domain_tokens.shape[0] > WIDTH:
        return general_body(
            features, destination, targets, domains, domain_tokens, short_filter, long_filter, skip
        )
    pieces = channels // WIDTH
    count = domain_tokens.shape[0]
    vmem = pl.BlockSpec(memory_space=pltpu.VMEM)
    hbm = pl.BlockSpec(memory_space=pl.ANY)
    big = (FREQS, 2 * INNER, 6 * INNER)
    dma = pltpu.SemaphoreType.DMA
    mixed, sums = pl.pallas_call(
        functools.partial(whole_kernel, devices, copies, pieces),
        out_shape=[
            pltpu.VMEM((rows_here, half_width), BF16),
            pltpu.VMEM((1, count), F32),
        ],
        in_specs=[hbm, vmem, vmem, vmem, vmem, hbm, vmem, vmem, vmem],
        out_specs=[vmem, vmem],
        scratch_shapes=[
            pltpu.VMEM((1, channels, length), F32),
            pltpu.VMEM((pieces, length, 3 * WIDTH), BF16),
            pltpu.VMEM((devices, 3, rows_here), jnp.int32),
            pltpu.VMEM((length, length), BF16),
            pltpu.VMEM((length, WIDTH), jnp.int32),
            pltpu.VMEM((FREQS, 2 * INNER, channels), F32),
            pltpu.VMEM(big, BF16),
            pltpu.VMEM(big, BF16),
            pltpu.VMEM((FREQS, channels, 6 * INNER), BF16),
            pltpu.VMEM((length + 8, 3 * WIDTH), F32),
            pltpu.VMEM((FREQS, 6 * INNER, WIDTH), BF16),
            pltpu.VMEM((FREQS, 2 * INNER, WIDTH), F32),
            pltpu.VMEM((length, WIDTH), F32),
            pltpu.VMEM((pieces, length, WIDTH), F32),
            pltpu.VMEM((pieces, length, WIDTH), BF16),
            pltpu.VMEM((length, WIDTH), F32),
            pltpu.VMEM((length, WIDTH), F32),
            pltpu.VMEM((length, 3 * WIDTH), BF16),
            pltpu.VMEM((2, length // 2), F32),
            pltpu.VMEM((2, length // 2), F32),
            pltpu.VMEM((MODELS * devices, 2, length // 2), F32),
            pltpu.VMEM((WIDTH, length // 2), BF16),
            pltpu.VMEM((2, 1, WIDTH), F32),
            dma,
            dma((pieces, 3)),
            dma,
            dma,
            dma,
            dma,
            dma,
            dma,
            dma,
            dma,
            dma,
            dma,
            dma,
            pltpu.SemaphoreType.REGULAR,
        ],
        compiler_params=pltpu.CompilerParams(
            vmem_limit_bytes=LIMIT, collective_id=0, has_side_effects=True
        ),
    )(
        features, destination.reshape(1, rows_here), targets.reshape(1, rows_here),
        domains.reshape(1, rows_here),
        short_filter.transpose(0, 2, 1, 3).reshape(-1, 1, channels), long_filter, skip,
        *table_inputs(),
    )
    mixed, excess = pl.pallas_call(
        last_kernel,
        out_shape=[
            jax.ShapeDtypeStruct((rows_here, half_width), BF16),
            jax.ShapeDtypeStruct((1, count), F32),
        ],
        in_specs=[vmem, vmem, vmem],
        out_specs=[hbm, hbm],
        scratch_shapes=[pltpu.VMEM((1, count), F32), dma((2,))],
        compiler_params=pltpu.CompilerParams(vmem_limit_bytes=2**20),
    )(mixed, sums, domain_tokens.reshape(1, count))
    return (mixed, excess.reshape(count))


def solution(mesh):
    return jax.shard_map(
        body,
        mesh=mesh,
        in_specs=(
            P("ctx", "mp"),
            P("ctx"),
            P("ctx"),
            P("ctx"),
            P(),
            P(None, "mp", None, "ctx"),
            P("mp", "ctx", None),
            P("mp", "ctx"),
        ),
        out_specs=(P("ctx", "mp"), P()),
        check_vma=False,
    )
```

```python
import functools
import math

import jax
import jax.numpy as jnp
import numpy as np
from jax import lax
from jax.experimental import pallas as pl
from jax.experimental.pallas import tpu as pltpu
from jax.sharding import PartitionSpec as P

MODELS = 2


HIGHEST = lax.Precision.HIGHEST


def dft_tables(count, limit, modulus):
    row_index = jnp.arange(count, dtype=jnp.int32)[:, None]
    col_index = jnp.arange(limit, dtype=jnp.int32)[None, :]
    angle = 2.0 * math.pi / modulus * (row_index * col_index % modulus).astype(jnp.float32)
    return (jnp.cos(angle), jnp.sin(angle))


def forward_transform(signal, outer_cos, outer_sin, twist_cos, twist_sin, inner_cos, inner_sin):
    real_a = jnp.einsum("kp,cpq->ckq", outer_cos, signal, precision=HIGHEST)
    imag_a = -jnp.einsum("kp,cpq->ckq", outer_sin, signal, precision=HIGHEST)
    real_b = real_a * twist_cos + imag_a * twist_sin
    imag_b = imag_a * twist_cos - real_a * twist_sin
    real_c = jnp.einsum("ckq,qj->ckj", real_b, inner_cos, precision=HIGHEST) + jnp.einsum(
        "ckq,qj->ckj", imag_b, inner_sin, precision=HIGHEST
    )
    imag_c = jnp.einsum("ckq,qj->ckj", imag_b, inner_cos, precision=HIGHEST) - jnp.einsum(
        "ckq,qj->ckj", real_b, inner_sin, precision=HIGHEST
    )
    return (real_c, imag_c)


def causal_convolution(signal, kernel):
    channels, length = signal.shape
    inner_size = 128
    outer_size = 2 * length // inner_size
    half_outer = outer_size // 2
    outer_cos, outer_sin = dft_tables(outer_size, half_outer, outer_size)
    twist_cos, twist_sin = dft_tables(outer_size, inner_size, 2 * length)
    inner_cos, inner_sin = dft_tables(inner_size, inner_size, inner_size)
    sig_re, sig_im = forward_transform(
        signal.reshape(channels, half_outer, inner_size),
        outer_cos,
        outer_sin,
        twist_cos,
        twist_sin,
        inner_cos,
        inner_sin,
    )
    ker_re, ker_im = forward_transform(
        kernel.reshape(channels, half_outer, inner_size),
        outer_cos,
        outer_sin,
        twist_cos,
        twist_sin,
        inner_cos,
        inner_sin,
    )
    prod_re = sig_re * ker_re - sig_im * ker_im
    prod_im = sig_re * ker_im + sig_im * ker_re
    back_re = jnp.einsum("ckj,qj->ckq", prod_re, inner_cos, precision=HIGHEST) - jnp.einsum(
        "ckj,qj->ckq", prod_im, inner_sin, precision=HIGHEST
    )
    back_im = jnp.einsum("ckj,qj->ckq", prod_im, inner_cos, precision=HIGHEST) + jnp.einsum(
        "ckj,qj->ckq", prod_re, inner_sin, precision=HIGHEST
    )
    turned_re = back_re * twist_cos - back_im * twist_sin
    turned_im = back_im * twist_cos + back_re * twist_sin
    result = jnp.einsum("kp,ckq->cpq", outer_cos, turned_re, precision=HIGHEST) - jnp.einsum(
        "kp,ckq->cpq", outer_sin, turned_im, precision=HIGHEST
    )
    return (result / (2.0 * length)).reshape(channels, length)


def general_body(features, destination, targets, domains, domain_tokens, short_filter, long_filter, skip):
    devices = lax.axis_size("ctx")
    rows_here = features.shape[0]
    length = devices * rows_here
    half_width = features.shape[1] // 3
    channels = half_width // devices
    capacity = 5 * rows_here // (2 * devices)
    owner_dev = destination // rows_here
    offset = destination % rows_here
    order = jnp.arange(rows_here, dtype=jnp.int32)
    ahead = (owner_dev[:, None] == owner_dev[None, :]) & (order[None, :] < order[:, None])
    slot_rank = jnp.sum(ahead.astype(jnp.int32), axis=1)
    buffer = (
        jnp.zeros((devices, capacity, 3 * half_width), features.dtype)
        .at[owner_dev, slot_rank]
        .set(features)
    )
    places = (
        jnp.full((devices, capacity), rows_here, jnp.int32).at[owner_dev, slot_rank].set(offset)
    )
    arrived, arrived_places = (
        lax.all_to_all(buffer, "ctx", split_axis=0, concat_axis=0, tiled=True),
        lax.all_to_all(places, "ctx", split_axis=0, concat_axis=0, tiled=True),
    )
    ordered = jnp.zeros((rows_here + 1, 3 * half_width), features.dtype)
    ordered = ordered.at[arrived_places.reshape(-1)].set(arrived.reshape(-1, 3 * half_width))[
        :rows_here
    ]
    blocks = ordered.reshape(rows_here, 3, devices, channels).transpose(2, 1, 3, 0)
    columns = lax.all_to_all(blocks, "ctx", split_axis=0, concat_axis=3, tiled=True)[0]
    inputs = columns.astype(jnp.float32)
    tap_weights = short_filter[:, 0]
    shorted = jnp.zeros_like(inputs)
    for tap_index in range(tap_weights.shape[0]):
        shifted = jnp.pad(inputs, ((0, 0), (0, 0), (tap_index, 0)))[:, :, :length]
        shorted = shorted + tap_weights[tap_index][:, :, None] * shifted
    signal = shorted[0] * shorted[2]
    long_part = causal_convolution(signal, long_filter[0])
    output_cols = (shorted[1] * (long_part + skip[0][:, None] * signal)).astype(jnp.bfloat16)
    returned = lax.all_to_all(
        output_cols.reshape(channels, devices, rows_here),
        "ctx",
        split_axis=1,
        concat_axis=0,
        tiled=True,
    )
    mixed = returned.reshape(half_width, rows_here).T
    copy_index = lax.axis_index("mp")
    model_index = copy_index // 2
    half_index = copy_index % 2
    values = mixed.astype(jnp.float32)
    part_exp = jnp.sum(jnp.exp(values), axis=1)
    local_target = targets - half_index * half_width
    inside = (local_target >= 0) & (local_target < half_width)
    picked = jnp.take_along_axis(
        values, jnp.clip(local_target, 0, half_width - 1)[:, None], axis=1
    )[:, 0]
    part_target = jnp.where(inside, picked, 0.0)
    is_model = jnp.arange(MODELS, dtype=jnp.int32)[:, None] == model_index
    exp_terms = jnp.where(is_model, part_exp[None, :], 0.0)
    target_terms = jnp.where(is_model, part_target[None, :], 0.0)
    total_exp, total_target = lax.psum((exp_terms, target_terms), "mp")
    losses = jnp.log(total_exp) - total_target
    token_excess = jnp.maximum(losses[0] - losses[1], 0.0)
    domain_count = domain_tokens.shape[0]
    in_domain = domains[None, :] == jnp.arange(domain_count, dtype=jnp.int32)[:, None]
    partial_sums = jnp.sum(jnp.where(in_domain, token_excess[None, :], 0.0), axis=1)
    domain_sums = lax.psum(partial_sums, "ctx")
    return (mixed, domain_sums / domain_tokens.astype(jnp.float32))


INNER = 128
OUTER = 16
FREQS = OUTER // 2 + 1
BF16 = jnp.bfloat16
F32 = jnp.float32


def weighted(terms):
    total = None
    for coef, value in terms:
        if value is None or abs(coef) < 1e-9:
            continue
        if abs(abs(coef) - 1.0) < 1e-9:
            term = value
            if coef < 0:
                total = -term if total is None else total - term
                continue
        else:
            term = coef * value
        total = term if total is None else total + term
    return total


def outer_forward(blocks):
    real, imag = [None] * FREQS, [None] * FREQS
    for k in range(FREQS // 2 + 1):
        angle = [2.0 * math.pi * p * k / OUTER for p in range(8)]
        parts = []
        for first in (0, 1):
            picks = range(first, 8, 2)
            parts.append(weighted([(math.cos(angle[p]), blocks[p]) for p in picks]))
            parts.append(weighted([(-math.sin(angle[p]), blocks[p]) for p in picks]))
        real_even, imag_even, real_odd, imag_odd = parts
        real[k] = weighted([(1.0, real_even), (1.0, real_odd)])
        imag[k] = weighted([(1.0, imag_even), (1.0, imag_odd)])
        if k < 4:
            real[8 - k] = weighted([(1.0, real_even), (-1.0, real_odd)])
            imag[8 - k] = weighted([(-1.0, imag_even), (1.0, imag_odd)])
    return real, imag


def outer_backward(real, imag):
    sums = {}
    for sign in (1.0, -1.0):
        sums[sign] = [
            (
                weighted([(1.0, real[k]), (sign, real[8 - k])]),
                weighted([(1.0, imag[k]), (-sign, imag[8 - k])]) if k else None,
            )
            for k in range(4)
        ]
    blocks = []
    for a in range(8):
        sign = 1.0 if a % 2 == 0 else -1.0
        terms = [(1.0, sums[sign][0][0])]
        for k in range(1, 4):
            angle = 2.0 * math.pi * k * a / OUTER
            terms.append((math.cos(angle), sums[sign][k][0]))
            terms.append((-math.sin(angle), sums[sign][k][1]))
        terms.append((math.cos(math.pi * a / 2), real[4]))
        terms.append((-math.sin(math.pi * a / 2), imag[4]))
        blocks.append(weighted(terms))
    return blocks


def halves(value):
    high = value.astype(BF16)
    return high, (value - high.astype(F32)).astype(BF16)


def stacked_dot(left, right, dims=(((1,), (0,)), ((), ()))):
    return lax.dot_general(left, right, dims, preferred_element_type=F32)


def table_inputs():
    index = np.arange(INNER)
    inner = 2.0 * np.pi * (np.outer(index, index) % INNER) / INNER
    twist = 2.0 * np.pi * np.outer(np.arange(FREQS), index) / (OUTER * INNER)
    inner_tab = np.stack([np.cos(inner), np.sin(inner)]).astype(np.float32)
    row_tab = np.stack([np.cos(twist), np.sin(twist)])[:, :, None, :].astype(np.float32)
    return jnp.asarray(inner_tab), jnp.asarray(row_tab)


def make_tables(inner_ref, row_ref, forward, backward):
    lower, upper = pl.ds(0, INNER), pl.ds(INNER, INNER)

    def store(ref, k, cos, sin, flip):
        cos_parts, sin_parts = halves(cos), halves(sin)
        for place, kind in ((0, 0), (1, 0), (2, 1)):
            c, s = cos_parts[kind], sin_parts[kind]
            first = pl.ds(place * 2 * INNER, INNER)
            second = pl.ds(place * 2 * INNER + INNER, INNER)
            ref[k, lower, first] = c
            ref[k, lower, second] = -s if flip else s
            ref[k, upper, first] = s if flip else -s
            ref[k, upper, second] = c

    def step(k, carry):
        base_cos, base_sin = inner_ref[0], inner_ref[1]
        row_cos, row_sin = row_ref[0, k], row_ref[1, k]
        cos, sin = base_cos * row_cos - base_sin * row_sin, base_sin * row_cos + base_cos * row_sin
        store(forward, k, cos, sin, False)
        col_cos = jnp.broadcast_to(row_cos, (INNER, INNER)).T
        col_sin = jnp.broadcast_to(row_sin, (INNER, INNER)).T
        cos, sin = base_cos * col_cos - base_sin * col_sin, base_sin * col_cos + base_cos * col_sin
        store(backward, k, cos, sin, True)
        return carry

    lax.fori_loop(0, FREQS, step, 0)


def filter_spectrum(filter_ref, forward, work, spectrum_ref):
    channels = filter_ref.shape[1]

    def stage(block, carry):
        rows = pl.ds(pl.multiple_of(block * 16, 16), 16)
        real, imag = outer_forward([filter_ref[0, rows, pl.ds(p * INNER, INNER)] for p in range(8)])
        for k in range(FREQS):
            for place, part in ((0, real[k]), (INNER, imag[k])):
                part = jnp.zeros((16, INNER), F32) if part is None else part
                high, low = halves(part)
                work[k, rows, pl.ds(place, INNER)] = high
                work[k, rows, pl.ds(place + 2 * INNER, INNER)] = low
                work[k, rows, pl.ds(place + 4 * INNER, INNER)] = high
        return carry

    lax.fori_loop(0, channels // 16, stage, 0)

    def transform(k, carry):
        scale = jnp.where((k == 0) | (k == FREQS - 1), 0.5, 1.0) * (2.0 / (OUTER * INNER))
        spectrum_ref[k] = scale * stacked_dot(forward[k], work[k], (((1,), (1,)), ((), ())))
        return carry

    lax.fori_loop(0, FREQS, transform, 0)


WIDTH = 128


def build_picks(places, pick_ref):
    length = pick_ref.shape[0]

    def step(block, carry):
        here = lax.broadcasted_iota(jnp.int32, (128, length), 0) + block * 128
        rows = pl.ds(pl.multiple_of(block * 128, 128), 128)
        pick_ref[rows, :] = jnp.where(here == places, 1.0, 0.0).astype(BF16)
        return carry

    lax.fori_loop(0, length // 128, step, 0)


def order_rows(cols_ref, pick_ref, seq_ref, first, width):
    length = cols_ref.shape[0]

    def step(block, carry):
        rows = pl.multiple_of(block * 256, 256)
        seq_ref[pl.ds(rows + 8, 256), pl.ds(first, width)] = jnp.dot(
            pick_ref[pl.ds(rows, 256), :], cols_ref[:, pl.ds(first, width)],
            preferred_element_type=F32,
        )
        return carry

    lax.fori_loop(0, length // 256, step, 0, unroll=True)


def shorted_rows(seq_ref, taps_ref, start, count, place, part, here):
    window = seq_ref[pl.ds(start, count + 8), pl.ds(place * WIDTH, WIDTH)]
    total = None
    for tap in range(taps_ref.shape[0] // 3):
        weight = taps_ref[tap * 3 + part, :, here]
        term = weight * window[8 - tap : 8 + count - tap]
        total = term if total is None else total + term
    return total


def short_and_outer(seq_ref, taps_ref, work, signal_ref, here):
    def stage(block, carry):
        offset = pl.multiple_of(block * 16, 16)
        signals = []
        for p in range(8):
            rows = pl.ds(p * INNER + offset, 16)
            start = pl.multiple_of(p * INNER + block * 16, 16)
            signal = shorted_rows(seq_ref, taps_ref, start, 16, 0, 0, here) * shorted_rows(
                seq_ref, taps_ref, start, 16, 1, 2, here
            )
            signal_ref[rows, :] = signal
            signals.append(signal)
        real, imag = outer_forward(signals)
        for k in range(FREQS):
            for place, part in ((0, real[k]), (INNER, imag[k])):
                part = jnp.zeros((16, WIDTH), F32) if part is None else part
                high, low = halves(part)
                work[k, pl.ds(place + offset, 16), :] = high
                work[k, pl.ds(place + 2 * INNER + offset, 16), :] = low
                work[k, pl.ds(place + 4 * INNER + offset, 16), :] = high
        return carry

    lax.fori_loop(0, INNER // 16, stage, 0)


def transform_product(spectrum_ref, forward, backward, work, back_ref, here):
    def step(k, carry):
        value = stacked_dot(forward[k], work[k])
        real, imag = value[:INNER], value[INNER:]
        other = spectrum_ref[k, :, here]
        other_real, other_imag = other[:INNER], other[INNER:]
        product = jnp.concatenate(
            [real * other_real - imag * other_imag, real * other_imag + imag * other_real], axis=0
        )
        high, low = halves(product)
        back_ref[k] = stacked_dot(backward[k], jnp.concatenate([high, low, high], axis=0))
        return carry

    lax.fori_loop(0, FREQS, step, 0, unroll=3)


def long_and_direct(back_ref, signal_ref, skip_ref, total_ref, piece, here):
    def step(block, carry):
        offset = pl.multiple_of(block * 16, 16)
        real = [back_ref[k, pl.ds(offset, 16), :] for k in range(FREQS)]
        imag = [
            back_ref[k, pl.ds(INNER + offset, 16), :] if 0 < k < FREQS - 1 else None
            for k in range(FREQS)
        ]
        direct = skip_ref[pl.ds(0, 1), here]
        for p, long_part in enumerate(outer_backward(real, imag)):
            rows = pl.ds(p * INNER + offset, 16)
            total_ref[piece, rows, :] = long_part + direct * signal_ref[rows, :]
        return carry

    lax.fori_loop(0, INNER // 16, step, 0)


LIMIT = 56 * 2**20
MESH = pl.DeviceIdType.MESH
PARTS = (0, 2, 1)


def whole_kernel(
    devices, copies, pieces,
    features, place_ref, target_ref, domain_ref, taps_ref, filter_hbm, skip_ref,
    inner_ref, row_ref,
    mixed_ref, sums_ref,
    filter_ref, cols, places, pick_ref, wanted_ref, spectrum, forward, backward, filter_work,
    seq_ref, work, back_ref, signal_ref, total_ref, out_ref, exp_ref, hit_ref,
    terms_ref, half_out, half_in, gathered, domain_sums,
    in_send, in_recv, place_send, place_recv, out_send, out_recv,
    given_send, given_recv, half_send, half_recv, sum_send, sum_recv, filter_sem, ready,
):
    me = lax.axis_index("ctx")
    copy_index = lax.axis_index("mp")
    rows_here, half_width = mixed_ref.shape
    channels = half_width // devices
    others = devices - 1
    core = lax.rem(copy_index, 2)
    model_index = copy_index // 2
    partner = copy_index + 1 - 2 * core
    span = rows_here * devices // 2
    group = devices // 2
    around = [lax.rem(me + step, devices) for step in range(1, devices)]
    near = [lax.rem(copy_index + step, copies) for step in range(copies)]

    def rows_of(device):
        return pl.ds(pl.multiple_of(device * rows_here, rows_here), rows_here)

    def feature_cols(device, part, piece):
        start = part * half_width + device * channels + piece * WIDTH
        return pl.ds(pl.multiple_of(start, WIDTH), WIDTH)

    def place_cols(place):
        return pl.ds(place * WIDTH, WIDTH)

    def ctx_start(source, target, send, recv, device):
        pltpu.make_async_remote_copy(
            src_ref=source, dst_ref=target, send_sem=send, recv_sem=recv,
            device_id={"ctx": device}, device_id_type=MESH,
        ).start()

    def wait_for(ref, sem):
        pltpu.make_async_copy(ref, ref, sem).wait()

    def send(piece, kinds, targets):
        for device in targets:
            for place in kinds:
                ctx_start(
                    features.at[:, feature_cols(device, PARTS[place], piece)],
                    cols.at[piece, rows_of(me), place_cols(place)],
                    in_send, in_recv.at[piece, place], device,
                )

    def own(piece, place):
        pltpu.make_async_copy(
            features.at[:, feature_cols(me, PARTS[place], piece)],
            cols.at[piece, rows_of(me), place_cols(place)],
            in_recv.at[piece, place],
        ).start()

    def arrive(piece, kinds):
        for place in kinds:
            wait_for(cols.at[piece, :, place_cols(place)], in_recv.at[piece, place])

    def outer(index):
        return index + group * (index // 2)

    def inner(index):
        return index + 2

    def send_places(targets):
        for device in targets:
            ctx_start(places.at[me], places.at[me], place_send, place_recv, device)

    def signal(semaphore, device):
        pl.semaphore_signal(semaphore, inc=1, device_id={"ctx": device}, device_id_type=MESH)

    is_inner = (me >= 2) & (me < 2 + group)
    barrier = pltpu.get_barrier_semaphore()
    for copy in near[1:]:
        pl.semaphore_signal(barrier, inc=1, device_id={"mp": copy}, device_id_type=MESH)
    places[me] = jnp.concatenate([place_ref[...], target_ref[...], domain_ref[...]], axis=0)

    @pl.when(is_inner)
    def _():
        place = me - 2
        inside = [inner(lax.rem(place + step, group)) for step in range(1, group)]
        outside = [outer(lax.rem(place + step, group)) for step in range(group)]
        for device in inside:
            signal(barrier, device)
        pl.semaphore_wait(barrier, copies - 1 + group - 1)
        for device in outside:
            signal(barrier, device)
        send(0, (0, 1), inside)
        send_places(inside)
        pl.semaphore_wait(ready, group)
        signal(ready, jnp.where(me < group, me - 2, me + 2))
        send(0, (0, 1), outside)
        send_places(outside)
        send(1, (0, 1), around)
        for piece in range(pieces):
            send(piece, (2,), around)

    @pl.when(jnp.logical_not(is_inner))
    def _():
        place = jnp.where(me < 2, me, me - group)
        inside = [inner(lax.rem(place + step, group)) for step in range(group)]
        outside = [outer(lax.rem(place + step, group)) for step in range(1, group)]
        pl.semaphore_wait(barrier, copies - 1 + group)
        for device in inside:
            signal(ready, device)
        send(0, (0, 1), inside)
        send_places(inside)
        pl.semaphore_wait(ready, 1)
        send(0, (0, 1), outside)
        send_places(outside)
        send(1, (0, 1), around)
        for piece in range(pieces):
            send(piece, (2,), around)

    filter_copy = pltpu.make_async_copy(filter_hbm, filter_ref, filter_sem)
    filter_copy.start()
    for piece in range(pieces):
        for place in range(3):
            own(piece, place)

    make_tables(inner_ref, row_ref, forward, backward)
    filter_copy.wait()
    filter_spectrum(filter_ref, forward, filter_work, spectrum)
    seq_ref[pl.ds(0, 8), :] = jnp.zeros((8, seq_ref.shape[1]), F32)

    wait_for(places.at[pl.ds(0, others)], place_recv)
    build_picks(jnp.concatenate([places[d][0:1] for d in range(devices)], axis=1), pick_ref)
    base = core * half_width + me * channels

    @pl.loop(0, devices)
    def _(device):
        loader = places[device][1:2]
        wanted_ref[rows_of(device), :] = jnp.broadcast_to(loader - base, (rows_here, rows_here)).T

    for piece in range(pieces):
        here = pl.ds(piece * WIDTH, WIDTH)
        arrive(piece, (0, 1))
        order_rows(cols.at[piece], pick_ref, seq_ref, 0, 2 * WIDTH)
        short_and_outer(seq_ref, taps_ref, work, signal_ref, here)
        transform_product(spectrum, forward, backward, work, back_ref, here)
        long_and_direct(back_ref, signal_ref, skip_ref, total_ref, piece, here)

    lane = lax.broadcasted_iota(jnp.int32, (rows_here, WIDTH), 1)

    def gate(piece, owner):
        here = pl.ds(piece * WIDTH, WIDTH)
        start = pl.multiple_of(owner * rows_here, rows_here)
        value = shorted_rows(seq_ref, taps_ref, start, rows_here, 2, 1, here)
        value = (value * total_ref[piece, rows_of(owner), :]).astype(out_ref.dtype)
        out_ref[piece, rows_of(owner), :] = value
        return value.astype(F32)

    def tally(piece, owner, value):
        rows = rows_of(owner)
        power = jnp.exp(value)
        hit = jnp.where(lane + piece * WIDTH == wanted_ref[rows, :], value, 0.0)
        if piece:
            power = power + exp_ref[rows, :]
            hit = hit + hit_ref[rows, :]
        if piece < pieces - 1:
            exp_ref[rows, :] = power
            hit_ref[rows, :] = hit
            return
        terms_ref[:, rows] = jnp.concatenate(
            [jnp.sum(part.T, axis=0, keepdims=True) for part in (power, hit)], axis=0
        )

    def mixed_part(piece):
        start = pl.multiple_of(me * channels + piece * WIDTH, WIDTH)
        return mixed_ref.at[:, pl.ds(start, WIDTH)]

    def give(piece, device):
        ctx_start(
            out_ref.at[piece, rows_of(device), :], mixed_part(piece), out_send, out_recv, device
        )

    def keep(piece):
        pltpu.make_async_copy(out_ref.at[piece, rows_of(me), :], mixed_part(piece), out_recv).start()

    for piece in range(pieces - 1):
        arrive(piece, (2,))
        order_rows(cols.at[piece], pick_ref, seq_ref, 2 * WIDTH, WIDTH)

        @pl.loop(0, others)
        def _(step, piece=piece):
            device = lax.rem(me + 1 + step, devices)
            gate(piece, device)
            give(piece, device)

        gate(piece, me)
        keep(piece)

        @pl.loop(0, devices)
        def _(device, piece=piece):
            tally(piece, device, out_ref[piece, rows_of(device), :].astype(F32))

    piece = pieces - 1
    arrive(piece, (2,))
    order_rows(cols.at[piece], pick_ref, seq_ref, 2 * WIDTH, WIDTH)

    def half_sums(half):
        @pl.loop(0, devices // 2)
        def _(step):
            owner = half * (devices // 2) + step
            tally(piece, owner, gate(piece, owner))

        rows = pl.ds(pl.multiple_of(half * span, span), span)
        return terms_ref[:, rows]

    def core_copy(source, target, send, recv):
        return pltpu.make_async_remote_copy(
            src_ref=source, dst_ref=target, send_sem=send, recv_sem=recv,
            device_id={"mp": partner}, device_id_type=MESH,
        )

    half_out[...] = half_sums(1 - core)
    half_copy = core_copy(half_out, half_in, half_send, half_recv)
    half_copy.start()
    half_own = half_sums(core)
    half_copy.wait_recv()
    half_theirs = half_in[...]
    chip = me * MODELS + model_index
    gathered[chip] = half_own + half_theirs
    def tell(device, copy):
        pltpu.make_async_remote_copy(
            src_ref=gathered.at[chip], dst_ref=gathered.at[chip],
            send_sem=given_send, recv_sem=given_recv,
            device_id={"ctx": device, "mp": copy}, device_id_type=MESH,
        ).start()

    for device in around:
        for other in range(MODELS):
            tell(device, near[2 * other])
    tell(me, near[2])
    for device in around:
        give(piece, device)
    keep(piece)

    wait_for(features.at[:, pl.ds(0, 3 * channels * others)], in_send)
    wait_for(places.at[pl.ds(0, others)], place_send)
    half_copy.wait_send()
    wait_for(gathered.at[pl.ds(0, MODELS * devices - 1)], given_recv)
    losses = []
    for model in range(MODELS):
        both = gathered[model]
        for device in range(1, devices):
            both = both + gathered[device * MODELS + model]
        losses.append(jnp.log(both[0:1]) - both[1:2])
    excess = jnp.maximum(losses[0] - losses[1], 0.0)
    kinds = lax.broadcasted_iota(jnp.int32, (WIDTH, rows_here), 0)
    by_kind = jnp.zeros((WIDTH, rows_here), F32)
    for step in range(devices // 2):
        match = kinds == places[core * (devices // 2) + step][2:3]
        part = excess[:, step * rows_here : (step + 1) * rows_here]
        by_kind = by_kind + jnp.where(match, part, 0.0)
    domain_sums[core] = jnp.sum(by_kind.T, axis=0, keepdims=True)
    sum_copy = core_copy(domain_sums.at[core], domain_sums.at[core], sum_send, sum_recv)
    sum_copy.start()
    wait_for(gathered.at[pl.ds(0, MODELS * devices - 1)], given_send)
    sum_copy.wait()
    sums = domain_sums[0] + domain_sums[1]
    sums_ref[...] = sums[:, : sums_ref.shape[1]]
    wait_for(mixed_ref, out_recv)
    wait_for(out_ref.at[:, pl.ds(0, rows_here * others), :], out_send)


def last_kernel(mixed_ref, sums_ref, tokens_ref, out_ref, excess_ref, ratio_ref, sems):
    mixed_copy = pltpu.make_async_copy(mixed_ref, out_ref, sems.at[0])
    mixed_copy.start()
    ratio_ref[...] = sums_ref[...] / tokens_ref[...].astype(F32)
    ratio_copy = pltpu.make_async_copy(ratio_ref, excess_ref, sems.at[1])
    ratio_copy.start()
    mixed_copy.wait()
    ratio_copy.wait()


def body(features, destination, targets, domains, domain_tokens, short_filter, long_filter, skip):
    devices = lax.axis_size("ctx")
    copies = lax.axis_size("mp")
    rows_here = features.shape[0]
    length = devices * rows_here
    half_width = features.shape[1] // 3
    channels = half_width // devices
    if length != 8 * INNER or rows_here != 128 or channels != 256 or copies != 4 or domain_tokens.shape[0] > WIDTH:
        return general_body(
            features, destination, targets, domains, domain_tokens, short_filter, long_filter, skip
        )
    pieces = channels // WIDTH
    count = domain_tokens.shape[0]
    vmem = pl.BlockSpec(memory_space=pltpu.VMEM)
    hbm = pl.BlockSpec(memory_space=pl.ANY)
    big = (FREQS, 2 * INNER, 6 * INNER)
    dma = pltpu.SemaphoreType.DMA
    mixed, sums = pl.pallas_call(
        functools.partial(whole_kernel, devices, copies, pieces),
        out_shape=[
            pltpu.VMEM((rows_here, half_width), BF16),
            pltpu.VMEM((1, count), F32),
        ],
        in_specs=[hbm, vmem, vmem, vmem, vmem, hbm, vmem, vmem, vmem],
        out_specs=[vmem, vmem],
        scratch_shapes=[
            pltpu.VMEM((1, channels, length), F32),
            pltpu.VMEM((pieces, length, 3 * WIDTH), BF16),
            pltpu.VMEM((devices, 3, rows_here), jnp.int32),
            pltpu.VMEM((length, length), BF16),
            pltpu.VMEM((length, WIDTH), jnp.int32),
            pltpu.VMEM((FREQS, 2 * INNER, channels), F32),
            pltpu.VMEM(big, BF16),
            pltpu.VMEM(big, BF16),
            pltpu.VMEM((FREQS, channels, 6 * INNER), BF16),
            pltpu.VMEM((length + 8, 3 * WIDTH), F32),
            pltpu.VMEM((FREQS, 6 * INNER, WIDTH), BF16),
            pltpu.VMEM((FREQS, 2 * INNER, WIDTH), F32),
            pltpu.VMEM((length, WIDTH), F32),
            pltpu.VMEM((pieces, length, WIDTH), F32),
            pltpu.VMEM((pieces, length, WIDTH), BF16),
            pltpu.VMEM((length, WIDTH), F32),
            pltpu.VMEM((length, WIDTH), F32),
            pltpu.VMEM((2, length), F32),
            pltpu.VMEM((2, length // 2), F32),
            pltpu.VMEM((2, length // 2), F32),
            pltpu.VMEM((MODELS * devices, 2, length // 2), F32),
            pltpu.VMEM((2, 1, WIDTH), F32),
            dma,
            dma((pieces, 3)),
            dma,
            dma,
            dma,
            dma,
            dma,
            dma,
            dma,
            dma,
            dma,
            dma,
            dma,
            pltpu.SemaphoreType.REGULAR,
        ],
        compiler_params=pltpu.CompilerParams(
            vmem_limit_bytes=LIMIT, collective_id=0, has_side_effects=True
        ),
    )(
        features, destination.reshape(1, rows_here), targets.reshape(1, rows_here),
        domains.reshape(1, rows_here),
        short_filter.transpose(0, 2, 1, 3).reshape(-1, 1, channels), long_filter, skip,
        *table_inputs(),
    )
    mixed, excess = pl.pallas_call(
        last_kernel,
        out_shape=[
            jax.ShapeDtypeStruct((rows_here, half_width), BF16),
            jax.ShapeDtypeStruct((1, count), F32),
        ],
        in_specs=[vmem, vmem, vmem],
        out_specs=[hbm, hbm],
        scratch_shapes=[pltpu.VMEM((1, count), F32), dma((2,))],
        compiler_params=pltpu.CompilerParams(vmem_limit_bytes=2**20),
    )(mixed, sums, domain_tokens.reshape(1, count))
    return (mixed, excess.reshape(count))


def solution(mesh):
    return jax.shard_map(
        body,
        mesh=mesh,
        in_specs=(
            P("ctx", "mp"),
            P("ctx"),
            P("ctx"),
            P("ctx"),
            P(),
            P(None, "mp", None, "ctx"),
            P("mp", "ctx", None),
            P("mp", "ctx"),
        ),
        out_specs=(P("ctx", "mp"), P()),
        check_vma=False,
    )
```

```python
import functools
import math

import jax
import jax.numpy as jnp
import numpy as np
from jax import lax
from jax.experimental import pallas as pl
from jax.experimental.pallas import tpu as pltpu
from jax.sharding import PartitionSpec as P

MODELS = 2


HIGHEST = lax.Precision.HIGHEST


def dft_tables(count, limit, modulus):
    row_index = jnp.arange(count, dtype=jnp.int32)[:, None]
    col_index = jnp.arange(limit, dtype=jnp.int32)[None, :]
    angle = 2.0 * math.pi / modulus * (row_index * col_index % modulus).astype(jnp.float32)
    return (jnp.cos(angle), jnp.sin(angle))


def forward_transform(signal, outer_cos, outer_sin, twist_cos, twist_sin, inner_cos, inner_sin):
    real_a = jnp.einsum("kp,cpq->ckq", outer_cos, signal, precision=HIGHEST)
    imag_a = -jnp.einsum("kp,cpq->ckq", outer_sin, signal, precision=HIGHEST)
    real_b = real_a * twist_cos + imag_a * twist_sin
    imag_b = imag_a * twist_cos - real_a * twist_sin
    real_c = jnp.einsum("ckq,qj->ckj", real_b, inner_cos, precision=HIGHEST) + jnp.einsum(
        "ckq,qj->ckj", imag_b, inner_sin, precision=HIGHEST
    )
    imag_c = jnp.einsum("ckq,qj->ckj", imag_b, inner_cos, precision=HIGHEST) - jnp.einsum(
        "ckq,qj->ckj", real_b, inner_sin, precision=HIGHEST
    )
    return (real_c, imag_c)


def causal_convolution(signal, kernel):
    channels, length = signal.shape
    inner_size = 128
    outer_size = 2 * length // inner_size
    half_outer = outer_size // 2
    outer_cos, outer_sin = dft_tables(outer_size, half_outer, outer_size)
    twist_cos, twist_sin = dft_tables(outer_size, inner_size, 2 * length)
    inner_cos, inner_sin = dft_tables(inner_size, inner_size, inner_size)
    sig_re, sig_im = forward_transform(
        signal.reshape(channels, half_outer, inner_size),
        outer_cos,
        outer_sin,
        twist_cos,
        twist_sin,
        inner_cos,
        inner_sin,
    )
    ker_re, ker_im = forward_transform(
        kernel.reshape(channels, half_outer, inner_size),
        outer_cos,
        outer_sin,
        twist_cos,
        twist_sin,
        inner_cos,
        inner_sin,
    )
    prod_re = sig_re * ker_re - sig_im * ker_im
    prod_im = sig_re * ker_im + sig_im * ker_re
    back_re = jnp.einsum("ckj,qj->ckq", prod_re, inner_cos, precision=HIGHEST) - jnp.einsum(
        "ckj,qj->ckq", prod_im, inner_sin, precision=HIGHEST
    )
    back_im = jnp.einsum("ckj,qj->ckq", prod_im, inner_cos, precision=HIGHEST) + jnp.einsum(
        "ckj,qj->ckq", prod_re, inner_sin, precision=HIGHEST
    )
    turned_re = back_re * twist_cos - back_im * twist_sin
    turned_im = back_im * twist_cos + back_re * twist_sin
    result = jnp.einsum("kp,ckq->cpq", outer_cos, turned_re, precision=HIGHEST) - jnp.einsum(
        "kp,ckq->cpq", outer_sin, turned_im, precision=HIGHEST
    )
    return (result / (2.0 * length)).reshape(channels, length)


def general_body(features, destination, targets, domains, domain_tokens, short_filter, long_filter, skip):
    devices = lax.axis_size("ctx")
    rows_here = features.shape[0]
    length = devices * rows_here
    half_width = features.shape[1] // 3
    channels = half_width // devices
    capacity = 5 * rows_here // (2 * devices)
    owner_dev = destination // rows_here
    offset = destination % rows_here
    order = jnp.arange(rows_here, dtype=jnp.int32)
    ahead = (owner_dev[:, None] == owner_dev[None, :]) & (order[None, :] < order[:, None])
    slot_rank = jnp.sum(ahead.astype(jnp.int32), axis=1)
    buffer = (
        jnp.zeros((devices, capacity, 3 * half_width), features.dtype)
        .at[owner_dev, slot_rank]
        .set(features)
    )
    places = (
        jnp.full((devices, capacity), rows_here, jnp.int32).at[owner_dev, slot_rank].set(offset)
    )
    arrived, arrived_places = (
        lax.all_to_all(buffer, "ctx", split_axis=0, concat_axis=0, tiled=True),
        lax.all_to_all(places, "ctx", split_axis=0, concat_axis=0, tiled=True),
    )
    ordered = jnp.zeros((rows_here + 1, 3 * half_width), features.dtype)
    ordered = ordered.at[arrived_places.reshape(-1)].set(arrived.reshape(-1, 3 * half_width))[
        :rows_here
    ]
    blocks = ordered.reshape(rows_here, 3, devices, channels).transpose(2, 1, 3, 0)
    columns = lax.all_to_all(blocks, "ctx", split_axis=0, concat_axis=3, tiled=True)[0]
    inputs = columns.astype(jnp.float32)
    tap_weights = short_filter[:, 0]
    shorted = jnp.zeros_like(inputs)
    for tap_index in range(tap_weights.shape[0]):
        shifted = jnp.pad(inputs, ((0, 0), (0, 0), (tap_index, 0)))[:, :, :length]
        shorted = shorted + tap_weights[tap_index][:, :, None] * shifted
    signal = shorted[0] * shorted[2]
    long_part = causal_convolution(signal, long_filter[0])
    output_cols = (shorted[1] * (long_part + skip[0][:, None] * signal)).astype(jnp.bfloat16)
    returned = lax.all_to_all(
        output_cols.reshape(channels, devices, rows_here),
        "ctx",
        split_axis=1,
        concat_axis=0,
        tiled=True,
    )
    mixed = returned.reshape(half_width, rows_here).T
    copy_index = lax.axis_index("mp")
    model_index = copy_index // 2
    half_index = copy_index % 2
    values = mixed.astype(jnp.float32)
    part_exp = jnp.sum(jnp.exp(values), axis=1)
    local_target = targets - half_index * half_width
    inside = (local_target >= 0) & (local_target < half_width)
    picked = jnp.take_along_axis(
        values, jnp.clip(local_target, 0, half_width - 1)[:, None], axis=1
    )[:, 0]
    part_target = jnp.where(inside, picked, 0.0)
    is_model = jnp.arange(MODELS, dtype=jnp.int32)[:, None] == model_index
    exp_terms = jnp.where(is_model, part_exp[None, :], 0.0)
    target_terms = jnp.where(is_model, part_target[None, :], 0.0)
    total_exp, total_target = lax.psum((exp_terms, target_terms), "mp")
    losses = jnp.log(total_exp) - total_target
    token_excess = jnp.maximum(losses[0] - losses[1], 0.0)
    domain_count = domain_tokens.shape[0]
    in_domain = domains[None, :] == jnp.arange(domain_count, dtype=jnp.int32)[:, None]
    partial_sums = jnp.sum(jnp.where(in_domain, token_excess[None, :], 0.0), axis=1)
    domain_sums = lax.psum(partial_sums, "ctx")
    return (mixed, domain_sums / domain_tokens.astype(jnp.float32))


INNER = 128
OUTER = 16
FREQS = OUTER // 2 + 1
BF16 = jnp.bfloat16
F32 = jnp.float32


def weighted(terms):
    total = None
    for coef, value in terms:
        if value is None or abs(coef) < 1e-9:
            continue
        if abs(abs(coef) - 1.0) < 1e-9:
            term = value
            if coef < 0:
                total = -term if total is None else total - term
                continue
        else:
            term = coef * value
        total = term if total is None else total + term
    return total


def outer_forward(blocks):
    real, imag = [None] * FREQS, [None] * FREQS
    for k in range(FREQS // 2 + 1):
        angle = [2.0 * math.pi * p * k / OUTER for p in range(8)]
        parts = []
        for first in (0, 1):
            picks = range(first, 8, 2)
            parts.append(weighted([(math.cos(angle[p]), blocks[p]) for p in picks]))
            parts.append(weighted([(-math.sin(angle[p]), blocks[p]) for p in picks]))
        real_even, imag_even, real_odd, imag_odd = parts
        real[k] = weighted([(1.0, real_even), (1.0, real_odd)])
        imag[k] = weighted([(1.0, imag_even), (1.0, imag_odd)])
        if k < 4:
            real[8 - k] = weighted([(1.0, real_even), (-1.0, real_odd)])
            imag[8 - k] = weighted([(-1.0, imag_even), (1.0, imag_odd)])
    return real, imag


def outer_backward(real, imag):
    sums = {}
    for sign in (1.0, -1.0):
        sums[sign] = [
            (
                weighted([(1.0, real[k]), (sign, real[8 - k])]),
                weighted([(1.0, imag[k]), (-sign, imag[8 - k])]) if k else None,
            )
            for k in range(4)
        ]
    blocks = []
    for a in range(8):
        sign = 1.0 if a % 2 == 0 else -1.0
        terms = [(1.0, sums[sign][0][0])]
        for k in range(1, 4):
            angle = 2.0 * math.pi * k * a / OUTER
            terms.append((math.cos(angle), sums[sign][k][0]))
            terms.append((-math.sin(angle), sums[sign][k][1]))
        terms.append((math.cos(math.pi * a / 2), real[4]))
        terms.append((-math.sin(math.pi * a / 2), imag[4]))
        blocks.append(weighted(terms))
    return blocks


def halves(value):
    high = value.astype(BF16)
    return high, (value - high.astype(F32)).astype(BF16)


def stacked_dot(left, right, dims=(((1,), (0,)), ((), ()))):
    return lax.dot_general(left, right, dims, preferred_element_type=F32)


def table_inputs():
    index = np.arange(INNER)
    inner = 2.0 * np.pi * (np.outer(index, index) % INNER) / INNER
    twist = 2.0 * np.pi * np.outer(np.arange(FREQS), index) / (OUTER * INNER)
    inner_tab = np.stack([np.cos(inner), np.sin(inner)]).astype(np.float32)
    row_tab = np.stack([np.cos(twist), np.sin(twist)])[:, :, None, :].astype(np.float32)
    return jnp.asarray(inner_tab), jnp.asarray(row_tab)


def make_tables(inner_ref, row_ref, forward, backward):
    lower, upper = pl.ds(0, INNER), pl.ds(INNER, INNER)

    def store(ref, k, cos, sin, flip):
        cos_parts, sin_parts = halves(cos), halves(sin)
        for place, kind in ((0, 0), (1, 0), (2, 1)):
            c, s = cos_parts[kind], sin_parts[kind]
            first = pl.ds(place * 2 * INNER, INNER)
            second = pl.ds(place * 2 * INNER + INNER, INNER)
            ref[k, lower, first] = c
            ref[k, lower, second] = -s if flip else s
            ref[k, upper, first] = s if flip else -s
            ref[k, upper, second] = c

    def step(k, carry):
        base_cos, base_sin = inner_ref[0], inner_ref[1]
        row_cos, row_sin = row_ref[0, k], row_ref[1, k]
        cos, sin = base_cos * row_cos - base_sin * row_sin, base_sin * row_cos + base_cos * row_sin
        store(forward, k, cos, sin, False)
        col_cos = jnp.broadcast_to(row_cos, (INNER, INNER)).T
        col_sin = jnp.broadcast_to(row_sin, (INNER, INNER)).T
        cos, sin = base_cos * col_cos - base_sin * col_sin, base_sin * col_cos + base_cos * col_sin
        store(backward, k, cos, sin, True)
        return carry

    lax.fori_loop(0, FREQS, step, 0)


def filter_spectrum(filter_ref, forward, work, spectrum_ref):
    channels = filter_ref.shape[1]

    def stage(block, carry):
        rows = pl.ds(pl.multiple_of(block * 16, 16), 16)
        real, imag = outer_forward([filter_ref[0, rows, pl.ds(p * INNER, INNER)] for p in range(8)])
        for k in range(FREQS):
            for place, part in ((0, real[k]), (INNER, imag[k])):
                part = jnp.zeros((16, INNER), F32) if part is None else part
                high, low = halves(part)
                work[k, rows, pl.ds(place, INNER)] = high
                work[k, rows, pl.ds(place + 2 * INNER, INNER)] = low
                work[k, rows, pl.ds(place + 4 * INNER, INNER)] = high
        return carry

    lax.fori_loop(0, channels // 16, stage, 0)

    def transform(k, carry):
        scale = jnp.where((k == 0) | (k == FREQS - 1), 0.5, 1.0) * (2.0 / (OUTER * INNER))
        spectrum_ref[k] = scale * stacked_dot(forward[k], work[k], (((1,), (1,)), ((), ())))
        return carry

    lax.fori_loop(0, FREQS, transform, 0)


WIDTH = 128


def build_picks(places, pick_ref):
    length = pick_ref.shape[0]

    def step(block, carry):
        here = lax.broadcasted_iota(jnp.int32, (128, length), 0) + block * 128
        rows = pl.ds(pl.multiple_of(block * 128, 128), 128)
        pick_ref[rows, :] = jnp.where(here == places, 1.0, 0.0).astype(BF16)
        return carry

    lax.fori_loop(0, length // 128, step, 0)


def order_rows(cols_ref, pick_ref, seq_ref, first, width):
    length = cols_ref.shape[0]

    def step(block, carry):
        rows = pl.multiple_of(block * 256, 256)
        seq_ref[pl.ds(rows + 8, 256), pl.ds(first, width)] = jnp.dot(
            pick_ref[pl.ds(rows, 256), :], cols_ref[:, pl.ds(first, width)],
            preferred_element_type=F32,
        )
        return carry

    lax.fori_loop(0, length // 256, step, 0, unroll=True)


def shorted_rows(seq_ref, taps_ref, start, count, place, part, here):
    window = seq_ref[pl.ds(start, count + 8), pl.ds(place * WIDTH, WIDTH)]
    total = None
    for tap in range(taps_ref.shape[0] // 3):
        weight = taps_ref[tap * 3 + part, :, here]
        term = weight * window[8 - tap : 8 + count - tap]
        total = term if total is None else total + term
    return total


def short_and_outer(seq_ref, taps_ref, work, signal_ref, here):
    def stage(block, carry):
        offset = pl.multiple_of(block * 16, 16)
        signals = []
        for p in range(8):
            rows = pl.ds(p * INNER + offset, 16)
            start = pl.multiple_of(p * INNER + block * 16, 16)
            signal = shorted_rows(seq_ref, taps_ref, start, 16, 0, 0, here) * shorted_rows(
                seq_ref, taps_ref, start, 16, 1, 2, here
            )
            signal_ref[rows, :] = signal
            signals.append(signal)
        real, imag = outer_forward(signals)
        for k in range(FREQS):
            for place, part in ((0, real[k]), (INNER, imag[k])):
                part = jnp.zeros((16, WIDTH), F32) if part is None else part
                high, low = halves(part)
                work[k, pl.ds(place + offset, 16), :] = high
                work[k, pl.ds(place + 2 * INNER + offset, 16), :] = low
                work[k, pl.ds(place + 4 * INNER + offset, 16), :] = high
        return carry

    lax.fori_loop(0, INNER // 16, stage, 0)


def transform_product(spectrum_ref, forward, backward, work, back_ref, here):
    def step(k, carry):
        value = stacked_dot(forward[k], work[k])
        real, imag = value[:INNER], value[INNER:]
        other = spectrum_ref[k, :, here]
        other_real, other_imag = other[:INNER], other[INNER:]
        product = jnp.concatenate(
            [real * other_real - imag * other_imag, real * other_imag + imag * other_real], axis=0
        )
        high, low = halves(product)
        back_ref[k] = stacked_dot(backward[k], jnp.concatenate([high, low, high], axis=0))
        return carry

    lax.fori_loop(0, FREQS, step, 0, unroll=3)


def long_and_direct(back_ref, signal_ref, skip_ref, total_ref, piece, here):
    def step(block, carry):
        offset = pl.multiple_of(block * 16, 16)
        real = [back_ref[k, pl.ds(offset, 16), :] for k in range(FREQS)]
        imag = [
            back_ref[k, pl.ds(INNER + offset, 16), :] if 0 < k < FREQS - 1 else None
            for k in range(FREQS)
        ]
        direct = skip_ref[pl.ds(0, 1), here]
        for p, long_part in enumerate(outer_backward(real, imag)):
            rows = pl.ds(p * INNER + offset, 16)
            total_ref[piece, rows, :] = long_part + direct * signal_ref[rows, :]
        return carry

    lax.fori_loop(0, INNER // 16, step, 0)


LIMIT = 56 * 2**20
MESH = pl.DeviceIdType.MESH
PARTS = (0, 2, 1)


def whole_kernel(
    devices, copies, pieces,
    features, place_ref, target_ref, domain_ref, taps_ref, filter_hbm, skip_ref,
    inner_ref, row_ref,
    mixed_ref, sums_ref,
    filter_ref, cols, places, pick_ref, wanted_ref, spectrum, forward, backward, filter_work,
    seq_ref, work, back_ref, signal_ref, total_ref, out_ref, exp_ref, hit_ref,
    terms_ref, half_out, half_in, gathered, domain_sums,
    in_send, in_recv, place_send, place_recv, out_send, out_recv,
    given_send, given_recv, half_send, half_recv, sum_send, sum_recv, filter_sem, ready,
):
    me = lax.axis_index("ctx")
    copy_index = lax.axis_index("mp")
    rows_here, half_width = mixed_ref.shape
    channels = half_width // devices
    others = devices - 1
    core = lax.rem(copy_index, 2)
    model_index = copy_index // 2
    partner = copy_index + 1 - 2 * core
    span = rows_here * devices // 2
    group = devices // 2
    around = [lax.rem(me + step, devices) for step in range(1, devices)]
    near = [lax.rem(copy_index + step, copies) for step in range(copies)]

    def rows_of(device):
        return pl.ds(pl.multiple_of(device * rows_here, rows_here), rows_here)

    def feature_cols(device, part, piece):
        start = part * half_width + device * channels + piece * WIDTH
        return pl.ds(pl.multiple_of(start, WIDTH), WIDTH)

    def place_cols(place):
        return pl.ds(place * WIDTH, WIDTH)

    def ctx_start(source, target, send, recv, device):
        pltpu.make_async_remote_copy(
            src_ref=source, dst_ref=target, send_sem=send, recv_sem=recv,
            device_id={"ctx": device}, device_id_type=MESH,
        ).start()

    def wait_for(ref, sem):
        pltpu.make_async_copy(ref, ref, sem).wait()

    def send(piece, kinds, targets):
        for device in targets:
            for place in kinds:
                ctx_start(
                    features.at[:, feature_cols(device, PARTS[place], piece)],
                    cols.at[piece, rows_of(me), place_cols(place)],
                    in_send, in_recv.at[piece, place], device,
                )

    def own(piece, place):
        pltpu.make_async_copy(
            features.at[:, feature_cols(me, PARTS[place], piece)],
            cols.at[piece, rows_of(me), place_cols(place)],
            in_recv.at[piece, place],
        ).start()

    def arrive(piece, kinds):
        for place in kinds:
            wait_for(cols.at[piece, :, place_cols(place)], in_recv.at[piece, place])

    def outer(index):
        return index + group * (index // 2)

    def inner(index):
        return index + 2

    def send_places(targets):
        for device in targets:
            ctx_start(places.at[me], places.at[me], place_send, place_recv, device)

    def signal(semaphore, device):
        pl.semaphore_signal(semaphore, inc=1, device_id={"ctx": device}, device_id_type=MESH)

    is_inner = (me >= 2) & (me < 2 + group)
    barrier = pltpu.get_barrier_semaphore()
    for copy in near[1:]:
        pl.semaphore_signal(barrier, inc=1, device_id={"mp": copy}, device_id_type=MESH)
    places[me] = jnp.concatenate([place_ref[...], target_ref[...], domain_ref[...]], axis=0)

    @pl.when(is_inner)
    def _():
        place = me - 2
        inside = [inner(lax.rem(place + step, group)) for step in range(1, group)]
        outside = [outer(lax.rem(place + step, group)) for step in range(group)]
        for device in inside:
            signal(barrier, device)
        pl.semaphore_wait(barrier, copies - 1 + group - 1)
        for device in outside:
            signal(barrier, device)
        send(0, (0, 1), inside)
        send_places(inside)
        pl.semaphore_wait(ready, group)
        signal(ready, jnp.where(me < group, me - 2, me + 2))
        send(0, (0, 1), outside)
        send_places(outside)
        send(1, (0, 1), around)
        for piece in range(pieces):
            send(piece, (2,), around)

    @pl.when(jnp.logical_not(is_inner))
    def _():
        place = jnp.where(me < 2, me, me - group)
        inside = [inner(lax.rem(place + step, group)) for step in range(group)]
        outside = [outer(lax.rem(place + step, group)) for step in range(1, group)]
        pl.semaphore_wait(barrier, copies - 1 + group)
        for device in inside:
            signal(ready, device)
        send(0, (0, 1), inside)
        send_places(inside)
        pl.semaphore_wait(ready, 1)
        send(0, (0, 1), outside)
        send_places(outside)
        send(1, (0, 1), around)
        for piece in range(pieces):
            send(piece, (2,), around)

    filter_copy = pltpu.make_async_copy(filter_hbm, filter_ref, filter_sem)
    filter_copy.start()
    for piece in range(pieces):
        for place in range(3):
            own(piece, place)

    make_tables(inner_ref, row_ref, forward, backward)
    filter_copy.wait()
    filter_spectrum(filter_ref, forward, filter_work, spectrum)
    seq_ref[pl.ds(0, 8), :] = jnp.zeros((8, seq_ref.shape[1]), F32)

    wait_for(places.at[pl.ds(0, others)], place_recv)
    build_picks(jnp.concatenate([places[d][0:1] for d in range(devices)], axis=1), pick_ref)
    base = core * half_width + me * channels

    @pl.loop(0, devices)
    def _(device):
        loader = places[device][1:2]
        wanted_ref[rows_of(device), :] = jnp.broadcast_to(loader - base, (rows_here, rows_here)).T

    for piece in range(pieces):
        here = pl.ds(piece * WIDTH, WIDTH)
        arrive(piece, (0, 1))
        order_rows(cols.at[piece], pick_ref, seq_ref, 0, 2 * WIDTH)
        short_and_outer(seq_ref, taps_ref, work, signal_ref, here)
        transform_product(spectrum, forward, backward, work, back_ref, here)
        long_and_direct(back_ref, signal_ref, skip_ref, total_ref, piece, here)

    lane = lax.broadcasted_iota(jnp.int32, (rows_here, WIDTH), 1)

    def gate(piece, owner):
        here = pl.ds(piece * WIDTH, WIDTH)
        start = pl.multiple_of(owner * rows_here, rows_here)
        value = shorted_rows(seq_ref, taps_ref, start, rows_here, 2, 1, here)
        value = (value * total_ref[piece, rows_of(owner), :]).astype(out_ref.dtype)
        out_ref[piece, rows_of(owner), :] = value
        return value.astype(F32)

    def tally(piece, owner, value):
        rows = rows_of(owner)
        power = jnp.exp(value)
        hit = jnp.where(lane + piece * WIDTH == wanted_ref[rows, :], value, 0.0)
        if piece:
            power = power + exp_ref[rows, :]
            hit = hit + hit_ref[rows, :]
        if piece < pieces - 1:
            exp_ref[rows, :] = power
            hit_ref[rows, :] = hit
            return
        terms_ref[:, rows] = jnp.concatenate(
            [jnp.sum(part.T, axis=0, keepdims=True) for part in (power, hit)], axis=0
        )

    def mixed_part(piece):
        start = pl.multiple_of(me * channels + piece * WIDTH, WIDTH)
        return mixed_ref.at[:, pl.ds(start, WIDTH)]

    def give(piece, device):
        ctx_start(
            out_ref.at[piece, rows_of(device), :], mixed_part(piece), out_send, out_recv, device
        )

    def keep(piece):
        pltpu.make_async_copy(out_ref.at[piece, rows_of(me), :], mixed_part(piece), out_recv).start()

    for piece in range(pieces - 1):
        arrive(piece, (2,))
        order_rows(cols.at[piece], pick_ref, seq_ref, 2 * WIDTH, WIDTH)

        @pl.loop(0, devices)
        def _(owner, piece=piece):
            gate(piece, owner)

        for device in around:
            give(piece, device)
        keep(piece)

        @pl.loop(0, devices)
        def _(device, piece=piece):
            tally(piece, device, out_ref[piece, rows_of(device), :].astype(F32))

    piece = pieces - 1
    arrive(piece, (2,))
    order_rows(cols.at[piece], pick_ref, seq_ref, 2 * WIDTH, WIDTH)

    def half_sums(half):
        @pl.loop(0, devices // 2)
        def _(step):
            owner = half * (devices // 2) + step
            tally(piece, owner, gate(piece, owner))

        rows = pl.ds(pl.multiple_of(half * span, span), span)
        return terms_ref[:, rows]

    def core_copy(source, target, send, recv):
        return pltpu.make_async_remote_copy(
            src_ref=source, dst_ref=target, send_sem=send, recv_sem=recv,
            device_id={"mp": partner}, device_id_type=MESH,
        )

    half_out[...] = half_sums(1 - core)
    half_copy = core_copy(half_out, half_in, half_send, half_recv)
    half_copy.start()
    half_own = half_sums(core)
    half_copy.wait_recv()
    half_theirs = half_in[...]
    chip = me * MODELS + model_index
    gathered[chip] = half_own + half_theirs
    def tell(device, copy):
        pltpu.make_async_remote_copy(
            src_ref=gathered.at[chip], dst_ref=gathered.at[chip],
            send_sem=given_send, recv_sem=given_recv,
            device_id={"ctx": device, "mp": copy}, device_id_type=MESH,
        ).start()

    for device in around:
        for other in range(MODELS):
            tell(device, near[2 * other])
    tell(me, near[2])
    for device in around:
        give(piece, device)
    keep(piece)

    wait_for(features.at[:, pl.ds(0, 3 * channels * others)], in_send)
    wait_for(places.at[pl.ds(0, others)], place_send)
    half_copy.wait_send()
    wait_for(gathered.at[pl.ds(0, MODELS * devices - 1)], given_recv)
    losses = []
    for model in range(MODELS):
        both = gathered[model]
        for device in range(1, devices):
            both = both + gathered[device * MODELS + model]
        losses.append(jnp.log(both[0:1]) - both[1:2])
    excess = jnp.maximum(losses[0] - losses[1], 0.0)
    kinds = lax.broadcasted_iota(jnp.int32, (WIDTH, rows_here), 0)
    by_kind = jnp.zeros((WIDTH, rows_here), F32)
    for step in range(devices // 2):
        match = kinds == places[core * (devices // 2) + step][2:3]
        part = excess[:, step * rows_here : (step + 1) * rows_here]
        by_kind = by_kind + jnp.where(match, part, 0.0)
    domain_sums[core] = jnp.sum(by_kind.T, axis=0, keepdims=True)
    sum_copy = core_copy(domain_sums.at[core], domain_sums.at[core], sum_send, sum_recv)
    sum_copy.start()
    wait_for(gathered.at[pl.ds(0, MODELS * devices - 1)], given_send)
    sum_copy.wait()
    sums = domain_sums[0] + domain_sums[1]
    sums_ref[...] = sums[:, : sums_ref.shape[1]]
    wait_for(mixed_ref, out_recv)
    wait_for(out_ref.at[:, pl.ds(0, rows_here * others), :], out_send)


def last_kernel(mixed_ref, sums_ref, tokens_ref, out_ref, excess_ref, ratio_ref, sems):
    mixed_copy = pltpu.make_async_copy(mixed_ref, out_ref, sems.at[0])
    mixed_copy.start()
    ratio_ref[...] = sums_ref[...] / tokens_ref[...].astype(F32)
    ratio_copy = pltpu.make_async_copy(ratio_ref, excess_ref, sems.at[1])
    ratio_copy.start()
    mixed_copy.wait()
    ratio_copy.wait()


def body(features, destination, targets, domains, domain_tokens, short_filter, long_filter, skip):
    devices = lax.axis_size("ctx")
    copies = lax.axis_size("mp")
    rows_here = features.shape[0]
    length = devices * rows_here
    half_width = features.shape[1] // 3
    channels = half_width // devices
    if length != 8 * INNER or rows_here != 128 or channels != 256 or copies != 4 or domain_tokens.shape[0] > WIDTH:
        return general_body(
            features, destination, targets, domains, domain_tokens, short_filter, long_filter, skip
        )
    pieces = channels // WIDTH
    count = domain_tokens.shape[0]
    vmem = pl.BlockSpec(memory_space=pltpu.VMEM)
    hbm = pl.BlockSpec(memory_space=pl.ANY)
    big = (FREQS, 2 * INNER, 6 * INNER)
    dma = pltpu.SemaphoreType.DMA
    mixed, sums = pl.pallas_call(
        functools.partial(whole_kernel, devices, copies, pieces),
        out_shape=[
            pltpu.VMEM((rows_here, half_width), BF16),
            pltpu.VMEM((1, count), F32),
        ],
        in_specs=[hbm, vmem, vmem, vmem, vmem, hbm, vmem, vmem, vmem],
        out_specs=[vmem, vmem],
        scratch_shapes=[
            pltpu.VMEM((1, channels, length), F32),
            pltpu.VMEM((pieces, length, 3 * WIDTH), BF16),
            pltpu.VMEM((devices, 3, rows_here), jnp.int32),
            pltpu.VMEM((length, length), BF16),
            pltpu.VMEM((length, WIDTH), jnp.int32),
            pltpu.VMEM((FREQS, 2 * INNER, channels), F32),
            pltpu.VMEM(big, BF16),
            pltpu.VMEM(big, BF16),
            pltpu.VMEM((FREQS, channels, 6 * INNER), BF16),
            pltpu.VMEM((length + 8, 3 * WIDTH), F32),
            pltpu.VMEM((FREQS, 6 * INNER, WIDTH), BF16),
            pltpu.VMEM((FREQS, 2 * INNER, WIDTH), F32),
            pltpu.VMEM((length, WIDTH), F32),
            pltpu.VMEM((pieces, length, WIDTH), F32),
            pltpu.VMEM((pieces, length, WIDTH), BF16),
            pltpu.VMEM((length, WIDTH), F32),
            pltpu.VMEM((length, WIDTH), F32),
            pltpu.VMEM((2, length), F32),
            pltpu.VMEM((2, length // 2), F32),
            pltpu.VMEM((2, length // 2), F32),
            pltpu.VMEM((MODELS * devices, 2, length // 2), F32),
            pltpu.VMEM((2, 1, WIDTH), F32),
            dma,
            dma((pieces, 3)),
            dma,
            dma,
            dma,
            dma,
            dma,
            dma,
            dma,
            dma,
            dma,
            dma,
            dma,
            pltpu.SemaphoreType.REGULAR,
        ],
        compiler_params=pltpu.CompilerParams(
            vmem_limit_bytes=LIMIT, collective_id=0, has_side_effects=True
        ),
    )(
        features, destination.reshape(1, rows_here), targets.reshape(1, rows_here),
        domains.reshape(1, rows_here),
        short_filter.transpose(0, 2, 1, 3).reshape(-1, 1, channels), long_filter, skip,
        *table_inputs(),
    )
    mixed, excess = pl.pallas_call(
        last_kernel,
        out_shape=[
            jax.ShapeDtypeStruct((rows_here, half_width), BF16),
            jax.ShapeDtypeStruct((1, count), F32),
        ],
        in_specs=[vmem, vmem, vmem],
        out_specs=[hbm, hbm],
        scratch_shapes=[pltpu.VMEM((1, count), F32), dma((2,))],
        compiler_params=pltpu.CompilerParams(vmem_limit_bytes=2**20),
    )(mixed, sums, domain_tokens.reshape(1, count))
    return (mixed, excess.reshape(count))


def solution(mesh):
    return jax.shard_map(
        body,
        mesh=mesh,
        in_specs=(
            P("ctx", "mp"),
            P("ctx"),
            P("ctx"),
            P("ctx"),
            P(),
            P(None, "mp", None, "ctx"),
            P("mp", "ctx", None),
            P("mp", "ctx"),
        ),
        out_specs=(P("ctx", "mp"), P()),
        check_vma=False,
    )
```
